32 devices in a mesh: gx: 2 (over core), gy: 4 (over y, x), gz: 4 (over z).
Axes of the slice: x: 2, y: 2, z: 4, core: 2. Of those that a mesh axis runs over, the one named last changes fastest.
Arguments:
- particles: float32 [128, 8, 128], P(('gx', 'gy', 'gz')), as said below
- local_pairs: int32 [128, 2], P(('gx', 'gy', 'gz')), may hold values from 0 to 3, as said below
- cross_pairs: int32 [64, 2], P(('gx', 'gy', 'gz')), may hold values from 0 to 3
- drag_cell: int32 [128, 128], P(('gx', 'gy', 'gz')), may hold values from 0 to 65535
- drag_share: float32 [128, 128], P(('gx', 'gy', 'gz')), may hold values from 0 to 1
- fluid: float32 [3, 16, 256, 512], P(None, 'gx', 'gy', 'gz'), may hold values from -6 to 6
Outputs:
- particle_force: float32 [128, 3, 128], P(('gx', 'gy', 'gz'))
- fluid_next: float32 [3, 16, 256, 512], P(None, 'gx', 'gy', 'gz')
The draws below stay inside these ranges and needn't reach their ends.
Inputs may be any that keep to these rules, and one draw needn't show every extreme that they name: `particles`: positions lie in 0 to 4 along each direction, radii in 0.3 to 0.6, elastic moduli in 0.5 to 2. `local_pairs`: each row names two different local blocks of its device; a pair may be listed more than once. `cross_pairs`: row entries: a local block of the listing device, then a local block of the device above it along the bed height; lists of devices at the top of gx have no partner and contribute nothing. `drag_cell`: index height * 64 * 128 + first lateral * 128 + second lateral within the owning device's cells.
All inputs are finite; a program needn't handle non-finite values.
Results may differ from the reference program's by a relative error of at most 0.00002.
Values sent between devices are 32-bit elements; how exact they have to be, the bound alone decides.
No kernel may reach another device: no remote copies, remote signals or barrier semaphores. Data moves between devices by JAX's collectives and lax.ppermute only.
A program may use at most 256 MiB of HBM per device.

```python
import math
import jax
import jax.numpy as jnp
from jax import lax

NB = 4
CX = 8
CY = 64
CZ = 128
LP_DEV = 4
CP_DEV = 2
NBLK = 128
LP_ALL = 128
CP_ALL = 64
GRID_H = 16
GRID_A = 256
GRID_B = 512
N_GX = 2
N_GY = 4
N_GZ = 4


def draw_particles(key, part):
    keys = jax.random.split(key, 4)
    places = jax.random.uniform(keys[0], (NBLK, 3, 128), jnp.float32, 0.0, 4.0)
    speeds = jax.random.normal(keys[1], (NBLK, 3, 128), jnp.float32)
    radii = jax.random.uniform(keys[2], (NBLK, 1, 128), jnp.float32, 0.3, 0.6)
    moduli = jnp.exp(jax.random.uniform(keys[3], (NBLK, 1, 128), jnp.float32, math.log(0.5), math.log(2.0)))
    return jnp.concatenate([places, speeds, radii, moduli], axis=1)


def draw_local_pairs(key, part):
    keys = jax.random.split(jax.random.fold_in(key, 7), 2)
    first = jax.random.randint(keys[0], (LP_ALL,), 0, NB, jnp.int32)
    step_off = jax.random.randint(keys[1], (LP_ALL,), 1, NB, jnp.int32)
    second = (first + step_off) % NB
    return jnp.stack([first, second], axis=1)


def place_ends(values, rng, smallest, high):
    spot = [jax.random.randint(jax.random.fold_in(rng, axis), (), 0, length) for axis, length in enumerate(values.shape)]
    longest = values.shape.index(max(values.shape))
    neighbour = spot[:longest] + [(spot[longest] + 1) % values.shape[longest]] + spot[longest + 1:]
    return values.at[tuple(spot)].set(smallest).at[tuple(neighbour)].set(high)


def shard_levels(rng, dims, shards, smallest, top_value):
    def one(position, shards_of):
        steps = jax.random.uniform(jax.random.fold_in(jax.random.fold_in(rng, 6), position), (shards_of,), jnp.float32, smallest / len(shards), top_value / len(shards))
        return jnp.repeat(jnp.exp(steps), dims[position] // shards_of).reshape((-1,) + (1,) * (len(dims) - position - 1))

    factor_of = one(*shards[0])
    for cut in shards[1:]:
        factor_of = factor_of * one(*cut)
    return factor_of


def bell_draw(key, extent, spread, bound, cuts=(), held_as=jnp.bfloat16):
    values = spread * jax.random.normal(key, extent, jnp.float32)
    if cuts:
        values = values * shard_levels(key, extent, cuts, -0.22, 0.18)
    return jnp.clip(values, -bound, bound).astype(held_as)


def setup_inputs(seed: int = 0) -> dict:
    streams_of = jax.random.split(jax.random.key(seed), 7)
    return {
        "particles": draw_particles(jax.random.fold_in(streams_of[6], 71), 0),
        "local_pairs": draw_local_pairs(jax.random.fold_in(streams_of[6], 71), 0),
        "cross_pairs": place_ends(jax.random.randint(streams_of[2], (CP_ALL, 2), 0, NB), jax.random.fold_in(streams_of[2], 1), 0, NB - 1).astype(jnp.int32),
        "drag_cell": place_ends(jax.random.randint(streams_of[3], (NBLK, 128), 0, CX * CY * CZ), jax.random.fold_in(streams_of[3], 1), 0, (CX * CY * CZ) - 1).astype(jnp.int32),
        "drag_share": jnp.clip(1.0 * jax.random.uniform(streams_of[4], (NBLK, 128), jnp.float32) ** shard_levels(streams_of[4], (NBLK, 128), ((0, 32),), -0.2, 0.2), 0.0, 1.0),
        "fluid": bell_draw(streams_of[5], (3, GRID_H, GRID_A, GRID_B), 1.0, 6.0, ((1, 2), (2, 4), (3, 4)), jnp.float32),
    }


soft_core = 0.01
damp_normal = 0.3
damp_tangent = 0.2
drag_coef = 1.5
diffuse = 0.1
source_gain = 0.5

def pair_force(left, right):
    offset = left[0:3][:, :, None] - right[0:3][:, None, :]
    distance = jnp.sqrt(lax.optimization_barrier(jnp.sum(offset * offset, axis=0)) + soft_core)
    normal = offset / distance
    radius_left = left[6][:, None]
    radius_right = right[6][None, :]
    modulus_left = left[7][:, None]
    modulus_right = right[7][None, :]
    intersection = jnp.maximum(radius_left + radius_right - distance, 0.0)
    radius_eff = radius_left * radius_right / (radius_left + radius_right)
    modulus_eff = modulus_left * modulus_right / (modulus_left + modulus_right)
    stiffness = 2.0 * modulus_eff * jnp.sqrt(radius_eff * intersection)
    relative = left[3:6][:, :, None] - right[3:6][:, None, :]
    normal_speed = lax.optimization_barrier(jnp.sum(relative * normal, axis=0))
    tangent = relative - normal_speed * normal
    pairwise = stiffness * (intersection * (2.0 / 3.0) - damp_normal * normal_speed) * normal - damp_tangent * stiffness * tangent
    return (lax.optimization_barrier(jnp.sum(pairwise, axis=2)), -lax.optimization_barrier(jnp.sum(pairwise, axis=1)))

def grouped(operands):
    count = operands[0].shape[0]
    group_size = math.gcd(8, count)
    shaped = tuple((item.reshape((count // group_size, group_size) + item.shape[1:]) for item in operands))
    result = lax.map(lambda group: jax.vmap(pair_force)(*group), shaped)
    return tuple((item.reshape((count,) + item.shape[2:]) for item in result))

def block_forces(own, above, local_list, cross_list):
    self_force = grouped((own, own))[0]
    first = local_list[:, 0]
    second = local_list[:, 1]
    near_force, near_react = grouped((own[first], own[second]))
    force = self_force.at[first].add(near_force).at[second].add(near_react)
    mine = cross_list[:, 0]
    theirs = cross_list[:, 1]
    cross_force, cross_react = grouped((own[mine], above[theirs]))
    force = force.at[mine].add(cross_force)
    reaction = jnp.zeros_like(force).at[theirs].add(cross_react)
    return (force, reaction)

def reference(particles, local_pairs, cross_pairs, drag_cell, drag_share, fluid):
    stride = N_GY * N_GZ
    devices = N_GX * stride
    blocks = particles.reshape(devices, NB, 8, 128)
    above_all = jnp.concatenate([blocks[stride:], jnp.zeros_like(blocks[:stride])], axis=0)
    lists_local = local_pairs.reshape(devices, LP_DEV, 2)
    lists_cross = cross_pairs.reshape(devices, CP_DEV, 2)
    force, reaction = lax.map(lambda item: block_forces(item[0], item[1], item[2], item[3]), (blocks, above_all, lists_local, lists_cross))
    received = jnp.concatenate([jnp.zeros_like(reaction[:stride]), reaction[:-stride]], axis=0)
    contact = (force + received).reshape(NBLK, 3, 128)
    owner = (jnp.arange(NBLK, dtype=jnp.int32) // NB)[:, None]
    owner_h = owner // stride
    owner_a = owner // N_GZ % N_GY
    owner_b = owner % N_GZ
    cell_h = owner_h * CX + drag_cell // (CY * CZ)
    cell_a = owner_a * CY + drag_cell // CZ % CY
    cell_b = owner_b * CZ + drag_cell % CZ
    raised = jnp.pad(fluid, ((0, 0), (0, 1), (0, 0), (0, 0)))
    lower = raised[:, cell_h, cell_a, cell_b]
    upper = raised[:, cell_h + 1, cell_a, cell_b]
    interp = (1.0 - drag_share) * lower + drag_share * upper
    drag = drag_coef * particles[:, 6, :][:, None, :] * (jnp.transpose(interp, (1, 0, 2)) - particles[:, 3:6, :])
    terms = -jnp.transpose(drag, (1, 0, 2))
    source = jnp.zeros((3, GRID_H + 1, GRID_A, GRID_B), jnp.float32)
    source = source.at[:, cell_h, cell_a, cell_b].add((1.0 - drag_share) * terms)
    source = source.at[:, cell_h + 1, cell_a, cell_b].add(drag_share * terms)
    source = source[:, :GRID_H]
    padded = jnp.pad(fluid, ((0, 0), (1, 1), (1, 1), (1, 1)))
    beside = padded[:, 2:, 1:-1, 1:-1] + padded[:, :-2, 1:-1, 1:-1]
    beside = beside + padded[:, 1:-1, 2:, 1:-1] + padded[:, 1:-1, :-2, 1:-1]
    beside = beside + padded[:, 1:-1, 1:-1, 2:] + padded[:, 1:-1, 1:-1, :-2]
    fluid_next = fluid + diffuse * (beside - 6.0 * fluid) + source_gain * source
    return (contact + drag, fluid_next)
```

```python
import functools

import jax
import jax.numpy as jnp
from jax import lax
from jax.experimental import pallas as pl
from jax.experimental.pallas import tpu as pltpu
from jax.sharding import PartitionSpec as P

soft_core = 0.01
damp_normal = 0.3
damp_tangent = 0.2
drag_coef = 1.5
diffuse = 0.1
source_gain = 0.5

F32 = jnp.float32
BF16 = jnp.bfloat16
PARTS = 3


def split_parts(value):
    parts = []
    for _ in range(PARTS):
        part = value.astype(BF16)
        parts.append(part)
        value = value - part.astype(F32)
    return parts


def places(cell, across, along):
    layer = across * along
    if layer & (layer - 1) or along & (along - 1):
        return cell // layer, cell // along % across, cell % along
    shift = along.bit_length() - 1
    high = layer.bit_length() - 1
    return (
        lax.shift_right_logical(cell, high),
        lax.shift_right_logical(cell, shift) & (across - 1),
        cell & (along - 1),
    )


def spread_block(block, store):
    rows = jnp.concatenate([block, block[7:8] * jnp.sqrt(block[6:7]), jnp.zeros((7, 128), F32)], axis=0)
    columns = jnp.transpose(rows)
    for i in range(9):
        store[i] = jnp.broadcast_to(columns[:, i : i + 1], (128, 128))


def pair_sum(left, spread):
    rows = [left[i : i + 1] for i in range(8)]
    scale = (2.0 * damp_tangent) * rows[7] * jnp.sqrt(rows[6])
    wide = [jnp.broadcast_to(row, (8, 128)) for row in rows + [scale]]
    total = [jnp.zeros((8, 128), F32) for _ in range(3)]
    for tile in range(16):
        there = [spread[i, tile * 8 : tile * 8 + 8, :] for i in range(9)]
        ex, ey, ez, wx, wy, wz = [wide[i] - there[i] for i in range(6)]
        inverse = lax.rsqrt((ex * ex + ey * ey) + (ez * ez + soft_core))
        dist = ((ex * ex + ey * ey) + (ez * ez + soft_core)) * inverse
        reach = wide[6] + there[6]
        delta = jnp.maximum(reach - dist, 0.0)
        mass = wide[7] + there[7]
        under = jnp.maximum(delta * reach * (mass * mass), 1e-30)
        tangent = (wide[8] * there[8]) * (delta * lax.rsqrt(under))
        speed = ((wx * ex + wy * ey) + wz * ez) * inverse
        along = (
            tangent
            * (
                (2.0 / 3.0 / damp_tangent) * delta
                - ((damp_normal - damp_tangent) / damp_tangent) * speed
            )
            * inverse
        )
        total[0] += along * ex - tangent * wx
        total[1] += along * ey - tangent * wy
        total[2] += along * ez - tangent * wz
    return [jnp.sum(item, axis=0, keepdims=True) for item in total]


def pack_kernel(blocks, pairs, pair_ref, flag_ref, part_ref, cell_ref, share_ref, fluid_ref, *outs):
    depth, across, along = fluid_ref.shape[1:]
    even = [flag_ref[0, axis] == 0 for axis in range(3)]
    height_outs, across_outs, along_outs = outs
    for n, out in enumerate(height_outs):
        upward = even[0] if n == 0 else jnp.logical_not(even[0])
        layer = jnp.where(upward, depth - 1, 0)
        for c in range(3):
            out[c * across : (c + 1) * across, :] = fluid_ref[c, layer]
        base = 3 * across
        for b in range(blocks):
            out[base + 8 * b : base + 8 * b + 8, :] = part_ref[b]
        base += 8 * blocks
        out[base : base + blocks, :] = cell_ref[...].astype(F32)
        out[base + blocks : base + 2 * blocks, :] = share_ref[...]
        base += 2 * blocks
        for k in range(pairs):
            for side in range(2):
                row = base + 2 * k + side
                out[row : row + 1, :] = jnp.full((1, 128), pair_ref[k, side], jnp.int32).astype(F32)
        used = base + 2 * pairs
        if used < out.shape[0]:
            out[used:, :] = jnp.zeros((out.shape[0] - used, 128), F32)
    for n, out in enumerate(across_outs):
        upward = even[1] if n == 0 else jnp.logical_not(even[1])
        for k in range(3 * depth):
            c, h = divmod(k, depth)
            last = fluid_ref[c, h, across - 1 : across, :]
            first = fluid_ref[c, h, 0:1, :]
            out[k : k + 1, :] = jnp.where(upward, last, first)
    lanes = lax.broadcasted_iota(jnp.int32, (across, along), 1)
    first = jnp.zeros((across, along), F32)
    last = jnp.zeros((across, along), F32)
    for k in range(3 * depth):
        c, h = divmod(k, depth)
        turned = fluid_ref[c, h]
        if k:
            turned = pltpu.roll(turned, 2 * k, 1)
        first = jnp.where(lanes == 2 * k, turned, first)
        last = jnp.where(lanes == (2 * k - 1) % along, turned, last)
    first = pltpu.roll(first, along - 1, 1)
    last = pltpu.roll(last, 1, 1)
    for n, out in enumerate(along_outs):
        upward = even[2] if n == 0 else jnp.logical_not(even[2])
        out[...] = jnp.where(upward, last, first)


def local_kernel(
    blocks, local_pair_ref, part_ref, cell_ref, share_ref, fluid_ref, force_ref, next_ref, spread, weights, coupled, spots
):
    depth, across, along = fluid_ref.shape[1:]
    for b in range(blocks):
        spread_block(part_ref[b], spread.at[b])

    for b in range(blocks):
        force = pair_sum(part_ref[b], spread.at[b])
        for c in range(3):
            force_ref[b, c : c + 1, :] = force[c]

    def listed(i, carry):
        a = local_pair_ref[i // 2, i % 2]
        c = local_pair_ref[i // 2, 1 - i % 2]
        force = pair_sum(part_ref[a], spread.at[c])
        for d in range(3):
            force_ref[a, d : d + 1, :] += force[d]
        return carry

    lax.fori_loop(0, 2 * local_pair_ref.shape[0], listed, 0)

    rows = lax.broadcasted_iota(jnp.int32, (across, 128), 0)
    sites = lax.broadcasted_iota(jnp.int32, (along, 128), 0)
    for b in range(blocks):
        height, over, spot = places(cell_ref[b : b + 1, :], across, along)
        share = share_ref[b : b + 1, :]
        index = jnp.broadcast_to(spot, (across, 128))
        mask = rows == over
        near = [
            jnp.where(height == h, 1.0 - share, 0.0) + jnp.where(height == h - 1, share, 0.0)
            for h in range(depth)
        ]
        spots[:, b * 128 : (b + 1) * 128] = jnp.where(sites == spot, 1.0, 0.0).astype(BF16)
        for c in range(3):
            total = jnp.zeros((8, 128), F32)
            for h in range(depth):
                seen = jnp.take_along_axis(fluid_ref[c, h], index, axis=1)
                seen = jnp.where(mask, seen, 0.0)
                total += near[h] * jnp.sum(seen.reshape(across // 8, 8, 128), axis=0)
            met = jnp.sum(total, axis=0, keepdims=True)
            drag = drag_coef * part_ref[b, 6:7, :] * (met - part_ref[b, 3 + c : 4 + c, :])
            force_ref[b, c : c + 1, :] += drag
            for h in range(depth):
                given = (-source_gain) * near[h] * drag
                weights[c * depth + h : c * depth + h + 1, b * 128 : (b + 1) * 128] = given
        ones = jnp.where(mask, 1.0, 0.0).astype(BF16)
        for n, part in enumerate(split_parts(weights[:, b * 128 : (b + 1) * 128])):
            for k in range(3 * depth):
                coupled[n, k * across : (k + 1) * across, b * 128 : (b + 1) * 128] = ones * part[k : k + 1, :]

    lanes = lax.broadcasted_iota(jnp.int32, (across, along), 1)
    downs = lax.broadcasted_iota(jnp.int32, (across, along), 0)
    for c in range(3):
        source = jnp.zeros((depth * across, along), F32)
        for n in range(PARTS):
            source += lax.dot_general(
                coupled[n, c * depth * across : (c + 1) * depth * across, :],
                spots[...],
                (((1,), (1,)), ((), ())),
                preferred_element_type=F32,
            )
        for h in range(depth):
            here = fluid_ref[c, h]
            beside = jnp.where(downs == 0, 0.0, pltpu.roll(here, 1, 0))
            beside += jnp.where(downs == across - 1, 0.0, pltpu.roll(here, across - 1, 0))
            beside += jnp.where(lanes == 0, 0.0, pltpu.roll(here, 1, 1))
            beside += jnp.where(lanes == along - 1, 0.0, pltpu.roll(here, along - 1, 1))
            if h > 0:
                beside += fluid_ref[c, h - 1]
            if h < depth - 1:
                beside += fluid_ref[c, h + 1]
            next_ref[c, h] = (
                here + diffuse * (beside - 6.0 * here) + source[h * across : (h + 1) * across, :]
            )


def finish_kernel(
    blocks, pairs, flag_ref, pair_ref, part_ref, cell_ref, share_ref, fluid_ref, force_ref, next_ref, ins, outs, scratch
):
    out_force, out_next = outs
    spread, coupled, spots = scratch
    depth, across, along = fluid_ref.shape[1:]
    height_ins, across_ins, along_ins = ins
    even = [flag_ref[0, axis] == 0 for axis in range(3)]

    def ordered(refs, axis):
        first = refs[0][...]
        if len(refs) == 1:
            return jnp.where(even[axis], 0.0, first), jnp.where(even[axis], first, 0.0)
        second = refs[1][...]
        return jnp.where(even[axis], second, first), jnp.where(even[axis], first, second)

    across_low, across_high = ordered(across_ins, 1)
    along_low, along_high = ordered(along_ins, 2)
    edges = diffuse * (along_low + along_high)
    across_low = diffuse * across_low
    across_high = diffuse * across_high
    lanes = lax.broadcasted_iota(jnp.int32, (across, along), 1)
    downs = lax.broadcasted_iota(jnp.int32, (across, along), 0)
    rim = jnp.logical_or(lanes == 0, lanes == along - 1)
    for k in range(3 * depth):
        c, h = divmod(k, depth)
        value = next_ref[c, h]
        value += jnp.where(rim, pltpu.roll(edges, (along - 2 * k) % along, 1) if k else edges, 0.0)
        value += jnp.where(downs == 0, across_low[k : k + 1, :], 0.0)
        value += jnp.where(downs == across - 1, across_high[k : k + 1, :], 0.0)
        out_next[c, h] = value
    for b in range(blocks):
        out_force[b] = force_ref[b]

    rows = lax.broadcasted_iota(jnp.int32, (across, 128), 0)
    sites = lax.broadcasted_iota(jnp.int32, (along, 128), 0)
    for n, blob in enumerate(height_ins):
        above = even[0] if n == 0 else jnp.logical_not(even[0])
        own_layer = jnp.where(above, depth - 1, 0)
        base = 3 * across
        there = [blob[base + 8 * b : base + 8 * b + 8, :] for b in range(blocks)]
        base += 8 * blocks
        cells = blob[base : base + blocks, :].astype(jnp.int32)
        shares = blob[base + blocks : base + 2 * blocks, :]
        base += 2 * blocks
        for k in range(pairs):
            theirs = [blob[base + 2 * k + side : base + 2 * k + side + 1, :] for side in range(2)]
            ours = [jnp.full((1, 128), pair_ref[k, side], jnp.int32).astype(F32) for side in range(2)]
            to = jnp.where(above, ours[0], theirs[1])
            by = jnp.where(above, ours[1], theirs[0])
            left = part_ref[0]
            right = there[0]
            for b in range(1, blocks):
                left = jnp.where(to == b, part_ref[b], left)
                right = jnp.where(by == b, there[b], right)
            spread_block(right, spread)
            force = pair_sum(left, spread)
            for b in range(blocks):
                for c in range(3):
                    out_force[b, c : c + 1, :] += jnp.where(to == b, force[c], 0.0)
        for b in range(blocks):
            cell = jnp.where(above, cell_ref[b : b + 1, :], cells[b : b + 1, :])
            share = jnp.where(above, share_ref[b : b + 1, :], shares[b : b + 1, :])
            owner = jnp.where(above, part_ref[b], there[b])
            height, over, spot = places(cell, across, along)
            top = height == depth - 1
            index = jnp.broadcast_to(spot, (across, 128))
            mask = rows == over
            seen_share = jnp.where(top, jnp.where(above, share, 1.0 - share), 0.0)
            home_share = jnp.where(jnp.logical_and(top, jnp.logical_not(above)), share, 0.0)
            given_share = (-source_gain) * jnp.where(above, 1.0 - share, share)
            own_share = jnp.where(jnp.logical_and(top, jnp.logical_not(above)), 1.0, 0.0)
            spots[:, b * 128 : (b + 1) * 128] = jnp.where(sites == spot, 1.0, 0.0).astype(BF16)
            ones = jnp.where(mask, 1.0, 0.0).astype(BF16)
            for c in range(3):
                seen = jnp.take_along_axis(blob[c * across : (c + 1) * across, :], index, axis=1)
                home = jnp.take_along_axis(fluid_ref[c, 0], index, axis=1)
                met = jnp.where(mask, seen_share * seen + home_share * home, 0.0)
                met = jnp.sum(met, axis=0, keepdims=True)
                drag = drag_coef * owner[6:7, :] * (met - own_share * owner[3 + c : 4 + c, :])
                out_force[b, c : c + 1, :] += jnp.where(above, drag, 0.0)
                for m, part in enumerate(split_parts(given_share * drag)):
                    coupled[m, c * across : (c + 1) * across, b * 128 : (b + 1) * 128] = ones * part
        source = jnp.zeros((3 * across, along), F32)
        for m in range(PARTS):
            source += lax.dot_general(
                coupled[m], spots[...], (((1,), (1,)), ((), ())), preferred_element_type=F32
            )
        for c in range(3):
            out_next[c, own_layer] += (
                diffuse * blob[c * across : (c + 1) * across, :] + source[c * across : (c + 1) * across, :]
            )


def exchange(payloads, axis):
    count = lax.axis_size(axis)
    results = []
    for n, payload in enumerate(payloads):
        route = []
        for i in range(n, count - 1, 2):
            route += [(i, i + 1), (i + 1, i)]
        results.append(lax.ppermute(payload, axis, route))
    return results


def body(particles, local_pairs, cross_pairs, drag_cell, drag_share, fluid):
    blocks = particles.shape[0]
    pairs = cross_pairs.shape[0]
    _, depth, across, along = fluid.shape
    axes = ("gx", "gy", "gz")
    flags = jnp.stack([lax.axis_index(axis) % 2 for axis in axes]).astype(jnp.int32).reshape(1, 3)
    counts = [min(2, lax.axis_size(axis) - 1) for axis in axes]
    blob_rows = 3 * across + 10 * blocks + 2 * pairs
    blob_rows += -blob_rows % 8
    shapes = [(blob_rows, along), (3 * depth, along), (across, along)]
    vmem = pl.BlockSpec(memory_space=pltpu.VMEM)
    smem = pl.BlockSpec(memory_space=pltpu.SMEM)

    packed = pl.pallas_call(
        functools.partial(grouped_pack, blocks, pairs, tuple(counts)),
        out_shape=[jax.ShapeDtypeStruct(shape, F32) for shape, n in zip(shapes, counts) for _ in range(n)],
        in_specs=[smem, smem, vmem, vmem, vmem, vmem],
        out_specs=[vmem] * sum(counts),
        name="pack",
    )(cross_pairs, flags, particles, drag_cell, drag_share, fluid)
    received = []
    at = 0
    for axis, n in zip(axes, counts):
        received += exchange(packed[at : at + n], axis)
        at += n

    force, partial = pl.pallas_call(
        functools.partial(local_kernel, blocks),
        out_shape=[
            jax.ShapeDtypeStruct((blocks, 3, 128), F32),
            jax.ShapeDtypeStruct(fluid.shape, F32),
        ],
        in_specs=[smem, vmem, vmem, vmem, vmem],
        out_specs=[vmem, vmem],
        scratch_shapes=[
            pltpu.VMEM((blocks, 9, 128, 128), F32),
            pltpu.VMEM((3 * depth, blocks * 128), F32),
            pltpu.VMEM((PARTS, 3 * depth * across, blocks * 128), BF16),
            pltpu.VMEM((along, blocks * 128), BF16),
        ],
        name="local",
    )(local_pairs, particles, drag_cell, drag_share, fluid)

    return tuple(
        pl.pallas_call(
            functools.partial(grouped_finish, blocks, pairs, tuple(counts)),
            out_shape=[
                jax.ShapeDtypeStruct((blocks, 3, 128), F32),
                jax.ShapeDtypeStruct(fluid.shape, F32),
            ],
            in_specs=[smem, smem] + [vmem] * (6 + len(received)),
            out_specs=[vmem, vmem],
            scratch_shapes=[
                pltpu.VMEM((9, 128, 128), F32),
                pltpu.VMEM((PARTS, 3 * across, blocks * 128), BF16),
                pltpu.VMEM((along, blocks * 128), BF16),
            ],
            name="finish",
        )(flags, cross_pairs, particles, drag_cell, drag_share, fluid, force, partial, *received)
    )


def by_axis(refs, counts):
    groups, at = [], 0
    for n in counts:
        groups.append(refs[at : at + n])
        at += n
    return groups


def grouped_pack(blocks, pairs, counts, *refs):
    pack_kernel(blocks, pairs, *refs[:6], *by_axis(refs[6:], counts))


def grouped_finish(blocks, pairs, counts, *refs):
    n = sum(counts)
    finish_kernel(
        blocks, pairs, *refs[:8], by_axis(refs[8 : 8 + n], counts), refs[8 + n : 10 + n], refs[10 + n :]
    )


def solution(mesh):
    in_specs = (
        P(("gx", "gy", "gz"), None, None),
        P(("gx", "gy", "gz"), None),
        P(("gx", "gy", "gz"), None),
        P(("gx", "gy", "gz"), None),
        P(("gx", "gy", "gz"), None),
        P(None, "gx", "gy", "gz"),
    )
    out_specs = (P(("gx", "gy", "gz"), None, None), P(None, "gx", "gy", "gz"))
    return jax.shard_map(body, mesh=mesh, in_specs=in_specs, out_specs=out_specs, check_vma=False)
```

```python
import functools

import jax
import jax.numpy as jnp
from jax import lax
from jax.experimental import pallas as pl
from jax.experimental.pallas import tpu as pltpu
from jax.sharding import PartitionSpec as P

soft_core = 0.01
damp_normal = 0.3
damp_tangent = 0.2
drag_coef = 1.5
diffuse = 0.1
source_gain = 0.5

F32 = jnp.float32
BF16 = jnp.bfloat16
PARTS = 3
LANES = 128
SUBLANES = 8
AXES = ("gx", "gy", "gz")


def split_parts(value):
    parts = []
    for _ in range(PARTS):
        part = value.astype(BF16).astype(F32)
        parts.append(part)
        value = value - part
    return parts


def places(cell, across, along):
    layer = across * along
    if layer & (layer - 1) or along & (along - 1):
        return cell // layer, cell // along % across, cell % along
    shift = along.bit_length() - 1
    high = layer.bit_length() - 1
    return (
        lax.shift_right_logical(cell, high),
        lax.shift_right_logical(cell, shift) & (across - 1),
        cell & (along - 1),
    )


def turn_rows(tile, sign):
    rows = lax.broadcasted_iota(jnp.int32, (SUBLANES, LANES), 0)
    for bit in (1, 2, 4):
        tile = jnp.where(rows & bit != 0, pltpu.roll(tile, sign * bit % LANES, 1), tile)
    return tile


def spread_block(block, store):
    rows = [block[i : i + 1] for i in range(8)]
    rows.append(rows[7] * jnp.sqrt(rows[6]))
    for i, row in enumerate(rows):
        tile = turn_rows(jnp.broadcast_to(row, (SUBLANES, LANES)), 1)
        for t in range(LANES // SUBLANES):
            store[i, t * SUBLANES : (t + 1) * SUBLANES, :] = pltpu.roll(tile, t * SUBLANES, 1) if t else tile


def pair_sum(left, spread, tiles, back):
    rows = [left[i : i + 1] for i in range(8)]
    rows.append((2.0 * damp_tangent) * rows[7] * jnp.sqrt(rows[6]))
    wide = [jnp.broadcast_to(row, (SUBLANES, LANES)) for row in rows]
    subs = lax.broadcasted_iota(jnp.int32, (SUBLANES, LANES), 0)
    total, react = [None] * 3, [None] * 3
    for tile in reversed(range(tiles)):
        there = [spread[i, tile * SUBLANES : (tile + 1) * SUBLANES, :] for i in range(9)]
        ex, ey, ez, wx, wy, wz = [wide[i] - there[i] for i in range(6)]
        square = (ex * ex + ey * ey) + (ez * ez + soft_core)
        inverse = lax.rsqrt(square)
        reach = wide[6] + there[6]
        delta = jnp.maximum(reach - square * inverse, 0.0)
        mass = wide[7] + there[7]
        under = jnp.maximum((delta * reach) * (mass * mass), 1e-30)
        tangent = (wide[8] * there[8]) * (delta * lax.rsqrt(under))
        speed = ((wx * ex + wy * ey) + wz * ez) * inverse
        along = (
            (2.0 / 3.0 / damp_tangent) * delta - ((damp_normal - damp_tangent) / damp_tangent) * speed
        ) * (tangent * inverse)
        for d, (e, w) in enumerate(((ex, wx), (ey, wy), (ez, wz))):
            force = along * e - tangent * w
            total[d] = force if total[d] is None else total[d] + force
            if back:
                if back == "short" and tile == tiles - 1:
                    force = jnp.where(subs == SUBLANES - 1, 0.0, force)
                react[d] = force if react[d] is None else force + pltpu.roll(react[d], LANES - SUBLANES, 1)
    total = [jnp.sum(item, axis=0, keepdims=True) for item in total]
    if back:
        react = [-jnp.sum(turn_rows(item, -1), axis=0, keepdims=True) for item in react]
    return total, react


def blob_layout(across, blocks, pairs):
    bodies = 3 * across
    cells = bodies + 8 * blocks
    shares = cells + blocks
    lists = shares + blocks
    rows = lists + 2 * pairs
    return bodies, cells, shares, lists, rows + -rows % 8


def parities():
    return [lax.rem(lax.axis_index(axis), 2) == 0 for axis in AXES]


def pack_kernel(counts, pair_ref, part_ref, cell_ref, share_ref, fluid_hbm, *refs):
    fluid_ref, outs, sems = refs[0], refs[1:-1], refs[-1]
    height_outs, across_outs, along_outs = by_axis(outs, counts)
    depth, across, along = fluid_ref.shape[1:]
    blocks, pairs = part_ref.shape[0], pair_ref.shape[0]
    bodies, cells, shares, lists, rows = blob_layout(across, blocks, pairs)
    copies = [pltpu.make_async_copy(fluid_hbm.at[c], fluid_ref.at[c], sems.at[c]) for c in range(3)]
    for copy in copies:
        copy.start()
    even = parities()
    for n, out in enumerate(height_outs):
        for b in range(blocks):
            out[bodies + 8 * b : bodies + 8 * b + 8, :] = part_ref[b]
        out[cells:shares, :] = cell_ref[...].astype(F32)
        out[shares:lists, :] = share_ref[...]
        for k in range(pairs):
            for side in range(2):
                row = lists + 2 * k + side
                out[row : row + 1, :] = jnp.full((1, LANES), pair_ref[k, side], jnp.int32).astype(F32)
        used = lists + 2 * pairs
        if used < rows:
            out[used:rows, :] = jnp.zeros((rows - used, LANES), F32)

    lanes = lax.broadcasted_iota(jnp.int32, (across, along), 1)
    first = jnp.zeros((across, along), F32)
    last = jnp.zeros((across, along), F32)
    for c in range(3):
        copies[c].wait()
        for n, out in enumerate(height_outs):
            upward = even[0] if n == 0 else jnp.logical_not(even[0])
            out[c * across : (c + 1) * across, :] = fluid_ref[c, jnp.where(upward, depth - 1, 0)]
        for h in range(depth):
            k = c * depth + h
            here = fluid_ref[c, h]
            for n, out in enumerate(across_outs):
                upward = even[1] if n == 0 else jnp.logical_not(even[1])
                out[k : k + 1, :] = jnp.where(upward, here[across - 1 : across], here[0:1])
            turned = pltpu.roll(here, 2 * k, 1) if k else here
            first = jnp.where(lanes == 2 * k, turned, first)
            last = jnp.where(lanes == (2 * k - 1) % along, turned, last)
    first = pltpu.roll(first, along - 1, 1)
    last = pltpu.roll(last, 1, 1)
    for n, out in enumerate(along_outs):
        upward = even[2] if n == 0 else jnp.logical_not(even[2])
        out[...] = jnp.where(upward, last, first)


def local_kernel(
    blocks, pairs, pair_hbm, blob_ref, fluid_ref, force_ref, next_ref, spread, found, weights, coupled, spots, pair_ref, sem
):
    depth, across, along = fluid_ref.shape[1:]
    listed = pair_ref.shape[1]
    fold = spots.shape[0] // along
    half = across // fold
    wide = blocks * LANES
    bodies, cells, shares, _, _ = blob_layout(across, blocks, pairs)
    copy = pltpu.make_async_copy(pair_hbm, pair_ref, sem)
    copy.start()
    rows = lax.broadcasted_iota(jnp.int32, (across, LANES), 0)
    halves = lax.broadcasted_iota(jnp.int32, (half, LANES), 0)
    sites = lax.broadcasted_iota(jnp.int32, (fold * along, LANES), 0)

    def body_of(b):
        return blob_ref[bodies + 8 * b : bodies + 8 * b + 8, :]

    for b in range(blocks):
        spread_block(body_of(b), spread.at[b])
    for b in range(blocks):
        ahead, behind = pair_sum(pltpu.roll(body_of(b), LANES - 1, 1), spread.at[b], LANES // 2 // SUBLANES, "short")
        for c in range(3):
            force_ref[c, b : b + 1, :] = pltpu.roll(ahead[c], 1, 1) + behind[c]

        height, over, spot = places(blob_ref[cells + b : cells + b + 1, :].astype(jnp.int32), across, along)
        share = blob_ref[shares + b : shares + b + 1, :]
        index = jnp.broadcast_to(spot, (across, LANES))
        mask = rows == over
        column = slice(b * LANES, (b + 1) * LANES)
        near = [
            jnp.where(height == h, 1.0 - share, jnp.where(height == h - 1, share, 0.0)) for h in range(depth)
        ]
        one_hot = jnp.where(sites == jnp.where(over >= half, along, 0) + spot, 1.0, 0.0).astype(BF16)
        for n in range(PARTS):
            spots[:, n * wide + b * LANES : n * wide + (b + 1) * LANES] = one_hot
        ones = jnp.where(halves == jnp.where(over >= half, over - half, over), 1.0, 0.0).astype(BF16)
        for c in range(3):
            total = jnp.zeros((SUBLANES, LANES), F32)
            for h in range(depth):
                seen = jnp.take_along_axis(fluid_ref[c, h], index, axis=1)
                seen = jnp.where(mask, seen, 0.0)
                total += near[h] * jnp.sum(seen.reshape(across // SUBLANES, SUBLANES, LANES), axis=0)
            met = jnp.sum(total, axis=0, keepdims=True)
            drag = drag_coef * blob_ref[bodies + 8 * b + 6 : bodies + 8 * b + 7, :] * (
                met - blob_ref[bodies + 8 * b + 3 + c : bodies + 8 * b + 4 + c, :]
            )
            force_ref[c, b : b + 1, :] += drag
            for h in range(depth):
                weights[c * depth + h : c * depth + h + 1, column] = (-source_gain) * near[h] * drag
        for n, part in enumerate(split_parts(weights[:, column])):
            for k in range(3 * depth):
                line = jnp.broadcast_to(part[k : k + 1], (16, LANES)).astype(BF16)
                line = jnp.concatenate([line] * (half // 16), axis=0)
                coupled[k * half : (k + 1) * half, n * wide + b * LANES : n * wide + (b + 1) * LANES] = ones * line

    copy.wait()
    for i in range(listed):
        a, c = pair_ref[0, i], pair_ref[1, i]
        left = blob_ref[pl.ds(pl.multiple_of(bodies + 8 * a, 8), 8), :]
        ahead, behind = pair_sum(left, spread.at[c], LANES // SUBLANES, "all")
        for side, (block, forces) in enumerate(((a, ahead), (c, behind))):
            for d in range(3):
                found[2 * i + side, d : d + 1, :] = forces[d]
    for b in range(blocks):
        for d in range(3):
            total = force_ref[d, b : b + 1, :]
            for i in range(listed):
                for side in range(2):
                    total += jnp.where(pair_ref[side, i] == b, found[2 * i + side, d : d + 1, :], 0.0)
            force_ref[d, b : b + 1, :] = total

    lanes = lax.broadcasted_iota(jnp.int32, (across, along), 1)
    downs = lax.broadcasted_iota(jnp.int32, (across, along), 0)
    for c in range(3):
        source = lax.dot_general(
            coupled[c * depth * half : (c + 1) * depth * half, :],
            spots[...],
            (((1,), (1,)), ((), ())),
            preferred_element_type=F32,
        )
        for h in range(depth):
            here = fluid_ref[c, h]
            beside = jnp.where(downs == 0, 0.0, pltpu.roll(here, 1, 0))
            beside += jnp.where(downs == across - 1, 0.0, pltpu.roll(here, across - 1, 0))
            beside += jnp.where(lanes == 0, 0.0, pltpu.roll(here, 1, 1))
            beside += jnp.where(lanes == along - 1, 0.0, pltpu.roll(here, along - 1, 1))
            if h > 0:
                beside += fluid_ref[c, h - 1]
            if h < depth - 1:
                beside += fluid_ref[c, h + 1]
            given = [
                source[h * half : (h + 1) * half, f * along : (f + 1) * along] for f in range(fold)
            ]
            next_ref[c, h] = here + diffuse * (beside - 6.0 * here) + jnp.concatenate(given, axis=0)


def finish_kernel(counts, blocks, pairs, force_ref, partial_ref, *refs):
    n_in = sum(counts)
    sent = refs[: counts[0]]
    height_ins, across_ins, along_ins = by_axis(refs[counts[0] : counts[0] + n_in], counts)
    out_force, next_hbm, next_ref, spread, coupled, spots, sems = refs[counts[0] + n_in :]
    depth, across, along = partial_ref.shape[1:]
    fold = spots.shape[0] // along
    half = across // fold
    wide = blocks * LANES
    bodies, cells, shares, lists, _ = blob_layout(across, blocks, pairs)
    even = parities()

    def ordered(arrived, axis):
        first = arrived[0][...]
        if len(arrived) == 1:
            return jnp.where(even[axis], 0.0, first), jnp.where(even[axis], first, 0.0)
        second = arrived[1][...]
        return jnp.where(even[axis], second, first), jnp.where(even[axis], first, second)

    across_low, across_high = ordered(across_ins, 1)
    across_low = diffuse * across_low
    across_high = diffuse * across_high
    edges = along_ins[0][...]
    if len(along_ins) > 1:
        edges = edges + along_ins[1][...]
    edges = diffuse * edges
    lanes = lax.broadcasted_iota(jnp.int32, (across, along), 1)
    downs = lax.broadcasted_iota(jnp.int32, (across, along), 0)
    rim = jnp.logical_or(lanes == 0, lanes == along - 1)
    copies = []
    for c in range(3):
        for h in range(depth):
            k = c * depth + h
            value = partial_ref[c, h]
            value += jnp.where(rim, pltpu.roll(edges, (along - 2 * k) % along, 1) if k else edges, 0.0)
            value += jnp.where(downs == 0, across_low[k : k + 1, :], 0.0)
            value += jnp.where(downs == across - 1, across_high[k : k + 1, :], 0.0)
            next_ref[c, h] = value
        if depth > 2:
            inner = pl.ds(1, depth - 2)
            copies.append(pltpu.make_async_copy(next_ref.at[c, inner], next_hbm.at[c, inner], sems.at[c]))
            copies[-1].start()

    rows = lax.broadcasted_iota(jnp.int32, (across, LANES), 0)
    halves = lax.broadcasted_iota(jnp.int32, (half, LANES), 0)
    sites = lax.broadcasted_iota(jnp.int32, (fold * along, LANES), 0)
    coupling = [[jnp.zeros((1, LANES), F32)] * blocks for _ in range(3)]
    for n, blob in enumerate(height_ins):
        own = sent[n]
        above = even[0] if n == 0 else jnp.logical_not(even[0])
        own_layer = jnp.where(above, depth - 1, 0)
        for b in range(blocks):
            cell = jnp.where(above, own[cells + b : cells + b + 1, :], blob[cells + b : cells + b + 1, :])
            share = jnp.where(above, own[shares + b : shares + b + 1, :], blob[shares + b : shares + b + 1, :])
            body = slice(bodies + 8 * b, bodies + 8 * b + 8)
            owner = jnp.where(above, own[body, :], blob[body, :])
            height, over, spot = places(cell.astype(jnp.int32), across, along)
            top = height == depth - 1
            below = jnp.logical_not(above)
            index = jnp.broadcast_to(spot, (across, LANES))
            mask = rows == over
            seen_share = jnp.where(top, jnp.where(above, share, 1.0 - share), 0.0)
            home_share = jnp.where(jnp.logical_and(top, below), share, 0.0)
            given_share = (-source_gain) * jnp.where(above, 1.0 - share, share)
            own_share = jnp.where(jnp.logical_and(top, below), 1.0, 0.0)
            one_hot = jnp.where(sites == jnp.where(over >= half, along, 0) + spot, 1.0, 0.0).astype(BF16)
            for m in range(PARTS):
                spots[:, m * wide + b * LANES : m * wide + (b + 1) * LANES] = one_hot
            ones = jnp.where(halves == jnp.where(over >= half, over - half, over), 1.0, 0.0).astype(BF16)
            for c in range(3):
                face = slice(c * across, (c + 1) * across)
                seen = jnp.take_along_axis(blob[face, :], index, axis=1)
                home = jnp.take_along_axis(own[face, :], index, axis=1)
                met = jnp.where(mask, seen_share * seen + home_share * home, 0.0)
                met = jnp.sum(met, axis=0, keepdims=True)
                drag = drag_coef * owner[6:7] * (met - own_share * owner[3 + c : 4 + c])
                coupling[c][b] += jnp.where(above, drag, 0.0)
                for m, part in enumerate(split_parts(given_share * drag)):
                    line = jnp.broadcast_to(part, (16, LANES)).astype(BF16)
                    line = jnp.concatenate([line] * (half // 16), axis=0)
                    coupled[c * half : (c + 1) * half, m * wide + b * LANES : m * wide + (b + 1) * LANES] = (
                        ones * line
                    )
        source = lax.dot_general(
            coupled[...], spots[...], (((1,), (1,)), ((), ())), preferred_element_type=F32
        )
        for c in range(3):
            given = [source[c * half : (c + 1) * half, f * along : (f + 1) * along] for f in range(fold)]
            next_ref[c, own_layer] += diffuse * blob[c * across : (c + 1) * across, :] + jnp.concatenate(given, axis=0)
    for n, h in enumerate(sorted({0, depth - 1})):
        copies.append(pltpu.make_async_copy(next_ref.at[:, h], next_hbm.at[:, h], sems.at[3 + n]))
        copies[-1].start()

    for n, blob in enumerate(height_ins):
        own = sent[n]
        above = even[0] if n == 0 else jnp.logical_not(even[0])
        for k in range(pairs):
            ours = [own[lists + 2 * k + side : lists + 2 * k + side + 1, :] for side in range(2)]
            theirs = [blob[lists + 2 * k + side : lists + 2 * k + side + 1, :] for side in range(2)]
            to = jnp.where(above, ours[0], theirs[1])
            by = jnp.where(above, ours[1], theirs[0])
            left = own[bodies : bodies + 8, :]
            right = blob[bodies : bodies + 8, :]
            for b in range(1, blocks):
                body = slice(bodies + 8 * b, bodies + 8 * b + 8)
                left = jnp.where(to == b, own[body, :], left)
                right = jnp.where(by == b, blob[body, :], right)
            spread_block(right, spread.at[n * pairs + k])
            force, _ = pair_sum(left, spread.at[n * pairs + k], LANES // SUBLANES, None)
            for b in range(blocks):
                for c in range(3):
                    coupling[c][b] += jnp.where(to == b, force[c], 0.0)
    for b in range(blocks):
        for c in range(3):
            out_force[c, b : b + 1, :] = force_ref[c, b : b + 1, :] + coupling[c][b]
    for copy in copies:
        copy.wait()


def by_axis(refs, counts):
    groups, at = [], 0
    for n in counts:
        groups.append(refs[at : at + n])
        at += n
    return groups


def exchange(payloads, axis):
    count = lax.axis_size(axis)
    results = []
    for n, payload in enumerate(payloads):
        route = []
        for i in range(n, count - 1, 2):
            route += [(i, i + 1), (i + 1, i)]
        results.append(lax.ppermute(payload, axis, route))
    return results


def body(particles, local_pairs, cross_pairs, drag_cell, drag_share, fluid):
    blocks = particles.shape[0]
    pairs = cross_pairs.shape[0]
    listed = local_pairs.shape[0]
    _, depth, across, along = fluid.shape
    counts = [min(2, lax.axis_size(axis) - 1) for axis in AXES]
    fold = 2 if across % 32 == 0 else 1
    half = across // fold
    wide = PARTS * blocks * LANES
    rows = blob_layout(across, blocks, pairs)[-1]
    shapes = [(rows, along), (3 * depth, along), (across, along)]
    vmem = pl.BlockSpec(memory_space=pltpu.VMEM)
    smem = pl.BlockSpec(memory_space=pltpu.SMEM)
    hbm = pl.BlockSpec(memory_space=pl.ANY)

    def kept(value):
        return pltpu.with_memory_space_constraint(value, pltpu.VMEM)

    fluid_kept, *packed = pl.pallas_call(
        functools.partial(pack_kernel, counts),
        out_shape=[pltpu.VMEM(fluid.shape, F32)]
        + [pltpu.VMEM(shape, F32) for shape, n in zip(shapes, counts) for _ in range(n)],
        in_specs=[smem, vmem, vmem, vmem, hbm],
        out_specs=[vmem] * (1 + sum(counts)),
        scratch_shapes=[pltpu.SemaphoreType.DMA((3,))],
        name="pack",
    )(cross_pairs, particles, drag_cell, drag_share, fluid)
    received = []
    for axis, payloads in zip(AXES, by_axis(packed, counts)):
        received += exchange(payloads, axis)

    force, partial = pl.pallas_call(
        functools.partial(local_kernel, blocks, pairs),
        out_shape=[pltpu.VMEM((3, blocks, LANES), F32), pltpu.VMEM(fluid.shape, F32)],
        in_specs=[hbm, vmem, vmem],
        out_specs=[vmem, vmem],
        scratch_shapes=[
            pltpu.VMEM((blocks, 9, LANES, LANES), F32),
            pltpu.VMEM((2 * listed, SUBLANES, LANES), F32),
            pltpu.VMEM((3 * depth, blocks * LANES), F32),
            pltpu.VMEM((3 * depth * half, wide), BF16),
            pltpu.VMEM((fold * along, wide), BF16),
            pltpu.SMEM((2, listed), jnp.int32),
            pltpu.SemaphoreType.DMA,
        ],
        name="local",
    )(local_pairs.T, kept(packed[0]), kept(fluid_kept))

    out_force, out_next = pl.pallas_call(
        functools.partial(finish_kernel, counts, blocks, pairs),
        out_shape=[
            jax.ShapeDtypeStruct((3, blocks, LANES), F32),
            jax.ShapeDtypeStruct(fluid.shape, F32),
        ],
        in_specs=[vmem] * (2 + counts[0] + len(received)),
        out_specs=[vmem, hbm],
        scratch_shapes=[
            pltpu.VMEM(fluid.shape, F32),
            pltpu.VMEM((counts[0] * pairs, 9, LANES, LANES), F32),
            pltpu.VMEM((3 * half, wide), BF16),
            pltpu.VMEM((fold * along, wide), BF16),
            pltpu.SemaphoreType.DMA((5,)),
        ],
        name="finish",
    )(*[kept(value) for value in [force, partial, *packed[: counts[0]], *received]])
    return jnp.transpose(out_force, (1, 0, 2)), out_next


def solution(mesh):
    in_specs = (
        P(("gx", "gy", "gz"), None, None),
        P(("gx", "gy", "gz"), None),
        P(("gx", "gy", "gz"), None),
        P(("gx", "gy", "gz"), None),
        P(("gx", "gy", "gz"), None),
        P(None, "gx", "gy", "gz"),
    )
    out_specs = (P(("gx", "gy", "gz"), None, None), P(None, "gx", "gy", "gz"))
    return jax.shard_map(body, mesh=mesh, in_specs=in_specs, out_specs=out_specs, check_vma=False)
```

```python
import functools

import jax
import jax.numpy as jnp
from jax import lax
from jax.experimental import pallas as pl
from jax.experimental.pallas import tpu as pltpu
from jax.sharding import PartitionSpec as P

soft_core = 0.01
damp_normal = 0.3
damp_tangent = 0.2
drag_coef = 1.5
diffuse = 0.1
source_gain = 0.5

F32 = jnp.float32
BF16 = jnp.bfloat16
PARTS = 3
LANES = 128
SUBLANES = 8
AXES = ("gx", "gy", "gz")


def split_parts(value):
    parts = []
    for _ in range(PARTS):
        part = value.astype(BF16).astype(F32)
        parts.append(part)
        value = value - part
    return parts


def places(cell, across, along):
    layer = across * along
    if layer & (layer - 1) or along & (along - 1):
        return cell // layer, cell // along % across, cell % along
    shift = along.bit_length() - 1
    high = layer.bit_length() - 1
    return (
        lax.shift_right_logical(cell, high),
        lax.shift_right_logical(cell, shift) & (across - 1),
        cell & (along - 1),
    )


def parts_of(value):
    return jnp.concatenate([part.astype(BF16) for part in split_parts(value)], axis=1)


def spread_blocks(blocks):
    columns = []
    for block in blocks:
        rows = jnp.concatenate([block, block[7:8] * jnp.sqrt(block[6:7])], axis=0)
        parts = split_parts(rows)
        parts.append(jnp.zeros((32 - 9 * PARTS, LANES), F32))
        columns.append(jnp.transpose(jnp.concatenate(parts, axis=0)).astype(BF16))
    lines = lax.broadcasted_iota(jnp.int32, (32, LANES), 0)
    picks = []
    for i in range(9):
        pick = lines == i
        for n in range(1, PARTS):
            pick = jnp.logical_or(pick, lines == i + 9 * n)
        picks.append(jnp.where(pick, 1.0, 0.0).astype(BF16))
    return jnp.dot(
        jnp.concatenate(columns, axis=0), jnp.concatenate(picks, axis=1), preferred_element_type=F32
    )


def pair_sum(left, spread, start, react):
    rows = [left[i : i + 1] for i in range(8)]
    rows.append((2.0 * damp_tangent) * rows[7] * jnp.sqrt(rows[6]))
    wide = [jnp.broadcast_to(row, (SUBLANES, LANES)) for row in rows]
    lanes = lax.broadcasted_iota(jnp.int32, (SUBLANES, LANES), 1)
    total = [None] * 3
    for tile in range(LANES // SUBLANES):
        place = pl.ds(pl.multiple_of(start + tile * SUBLANES, SUBLANES), SUBLANES)
        there = [spread[place, i * LANES : (i + 1) * LANES] for i in range(9)]
        ex, ey, ez, wx, wy, wz = [wide[i] - there[i] for i in range(6)]
        square = (ex * ex + ey * ey) + (ez * ez + soft_core)
        inverse = lax.rsqrt(square)
        reach = wide[6] + there[6]
        delta = jnp.maximum(reach - square * inverse, 0.0)
        mass = wide[7] + there[7]
        under = jnp.maximum((delta * reach) * (mass * mass), 1e-30)
        tangent = (wide[8] * there[8]) * (delta * lax.rsqrt(under))
        speed = ((wx * ex + wy * ey) + wz * ez) * inverse
        along = (
            (2.0 / 3.0 / damp_tangent) * delta - ((damp_normal - damp_tangent) / damp_tangent) * speed
        ) * (tangent * inverse)
        column = None
        for d, (e, w) in enumerate(((ex, wx), (ey, wy), (ez, wz))):
            force = along * e - tangent * w
            total[d] = force if total[d] is None else total[d] + force
            if react is not None:
                across_sum = jnp.broadcast_to(jnp.sum(force, axis=1, keepdims=True), (SUBLANES, LANES))
                column = across_sum if column is None else jnp.where(lanes == d, across_sum, column)
        if react is not None:
            react[tile * SUBLANES : (tile + 1) * SUBLANES, :] = column
    total = [jnp.sum(item, axis=0, keepdims=True) for item in total]
    if react is None:
        return total, None
    turned = jnp.transpose(react[...])
    return total, [-turned[d : d + 1] for d in range(3)]


def blob_layout(across, blocks, pairs):
    bodies = 3 * across
    cells = bodies + 8 * blocks
    shares = cells + blocks
    lists = shares + blocks
    rows = lists + 2 * pairs
    return bodies, cells, shares, lists, rows + -rows % 8


def parities():
    return [lax.rem(lax.axis_index(axis), 2) == 0 for axis in AXES]


def pack_kernel(counts, pair_hbm, part_hbm, cell_hbm, share_hbm, fluid_hbm, *refs):
    n_out = 1 + sum(counts)
    fluid_ref, outs = refs[0], refs[1:n_out]
    pair_ref, part_ref, cell_ref, share_ref, sems = refs[n_out:]
    height_outs, across_outs, along_outs = by_axis(outs, counts)
    depth, across, along = fluid_ref.shape[1:]
    blocks, pairs = part_ref.shape[0], pair_ref.shape[0]
    bodies, cells, shares, lists, rows = blob_layout(across, blocks, pairs)
    copies = [pltpu.make_async_copy(fluid_hbm.at[c], fluid_ref.at[c], sems.at[c]) for c in range(3)]
    small = [(pair_hbm, pair_ref), (part_hbm, part_ref), (cell_hbm, cell_ref), (share_hbm, share_ref)]
    small = [pltpu.make_async_copy(source, target, sems.at[3 + n]) for n, (source, target) in enumerate(small)]
    for copy in copies + small:
        copy.start()
    even = parities()
    for copy in small:
        copy.wait()
    for n, out in enumerate(height_outs):
        for b in range(blocks):
            out[bodies + 8 * b : bodies + 8 * b + 8, :] = part_ref[b]
        out[cells:shares, :] = cell_ref[...].astype(F32)
        out[shares:lists, :] = share_ref[...]
        for k in range(pairs):
            for side in range(2):
                row = lists + 2 * k + side
                out[row : row + 1, :] = jnp.full((1, LANES), pair_ref[k, side], jnp.int32).astype(F32)
        used = lists + 2 * pairs
        if used < rows:
            out[used:rows, :] = jnp.zeros((rows - used, LANES), F32)

    lanes = lax.broadcasted_iota(jnp.int32, (across, along), 1)
    first = jnp.zeros((across, along), F32)
    last = jnp.zeros((across, along), F32)
    for c in range(3):
        copies[c].wait()
        for n, out in enumerate(height_outs):
            upward = even[0] if n == 0 else jnp.logical_not(even[0])
            out[c * across : (c + 1) * across, :] = fluid_ref[c, jnp.where(upward, depth - 1, 0)]
        for h in range(depth):
            k = c * depth + h
            here = fluid_ref[c, h]
            for n, out in enumerate(across_outs):
                upward = even[1] if n == 0 else jnp.logical_not(even[1])
                out[k : k + 1, :] = jnp.where(upward, here[across - 1 : across], here[0:1])
            turned = pltpu.roll(here, 2 * k, 1) if k else here
            first = jnp.where(lanes == 2 * k, turned, first)
            last = jnp.where(lanes == (2 * k - 1) % along, turned, last)
    first = pltpu.roll(first, along - 1, 1)
    last = pltpu.roll(last, 1, 1)
    for n, out in enumerate(along_outs):
        upward = even[2] if n == 0 else jnp.logical_not(even[2])
        out[...] = jnp.where(upward, last, first)


def lane_one_hot(sites, target):
    return jnp.where(sites == target, 1.0, 0.0).astype(BF16)


def place_lines(ones, part, half):
    line = jnp.broadcast_to(part, (16, LANES)).astype(BF16)
    return ones * jnp.concatenate([line] * (half // 16), axis=0)


def local_kernel(
    blocks, pairs, pair_hbm, blob_ref, fluid_ref, force_ref, next_ref,
    spread, react, pieces, seen_ref, picks, found, weights, coupled, spots, pair_ref, sem,
):
    depth, across, along = fluid_ref.shape[1:]
    listed = pair_ref.shape[1]
    fold = spots.shape[0] // along
    half = across // fold
    wide = blocks * LANES
    bodies, cells, shares, _, _ = blob_layout(across, blocks, pairs)
    copy = pltpu.make_async_copy(pair_hbm, pair_ref, sem)
    copy.start()
    rows = lax.broadcasted_iota(jnp.int32, (across, LANES), 0)
    halves = lax.broadcasted_iota(jnp.int32, (half, LANES), 0)
    sites = lax.broadcasted_iota(jnp.int32, (fold * along, LANES), 0)
    lanes = lax.broadcasted_iota(jnp.int32, (across, along), 1)
    downs = lax.broadcasted_iota(jnp.int32, (across, along), 0)
    slabs = [(c, h) for c in range(3) for h in range(depth)]

    def body_of(b):
        return blob_ref[bodies + 8 * b : bodies + 8 * b + 8, :]

    def spot_of(b):
        return places(blob_ref[cells + b : cells + b + 1, :].astype(jnp.int32), across, along)

    def stencil(c, h):
        here = fluid_ref[c, h]
        beside = jnp.where(downs == 0, 0.0, pltpu.roll(here, 1, 0))
        beside += jnp.where(downs == across - 1, 0.0, pltpu.roll(here, across - 1, 0))
        beside += jnp.where(lanes == 0, 0.0, pltpu.roll(here, 1, 1))
        beside += jnp.where(lanes == along - 1, 0.0, pltpu.roll(here, along - 1, 1))
        if h > 0:
            beside += fluid_ref[c, h - 1]
        if h < depth - 1:
            beside += fluid_ref[c, h + 1]
        next_ref[c, h] = here + diffuse * (beside - 6.0 * here)

    spread[...] = spread_blocks([body_of(b) for b in range(blocks)])
    for k, (c, h) in enumerate(slabs):
        pieces[k * across : (k + 1) * across, :] = parts_of(fluid_ref[c, h])
    for b in range(blocks):
        height, over, spot = spot_of(b)
        column = slice(b * LANES, (b + 1) * LANES)
        one_hot = lane_one_hot(sites[:along], spot)
        for n in range(PARTS):
            picks[n * along : (n + 1) * along, column] = one_hot
        one_hot = lane_one_hot(sites, jnp.where(over >= half, along, 0) + spot)
        for n in range(PARTS):
            spots[:, n * wide + b * LANES : n * wide + (b + 1) * LANES] = one_hot
    seen_ref[...] = jnp.dot(pieces[...], picks[...], preferred_element_type=F32)

    turns = blocks + listed
    share_out = [slabs[i * len(slabs) // turns : (i + 1) * len(slabs) // turns] for i in range(turns)]
    for b in range(blocks):
        for c, h in share_out[b]:
            stencil(c, h)
        force, _ = pair_sum(body_of(b), spread, b * LANES, None)
        for c in range(3):
            force_ref[c, b : b + 1, :] = force[c]

    for b in range(blocks):
        height, over, _ = spot_of(b)
        share = blob_ref[shares + b : shares + b + 1, :]
        mask = rows == over
        column = slice(b * LANES, (b + 1) * LANES)
        near = [
            jnp.where(height == h, 1.0 - share, jnp.where(height == h - 1, share, 0.0)) for h in range(depth)
        ]
        for c in range(3):
            total = jnp.zeros((SUBLANES, LANES), F32)
            for h in range(depth):
                k = c * depth + h
                seen = jnp.where(mask, seen_ref[k * across : (k + 1) * across, column], 0.0)
                total += near[h] * jnp.sum(seen.reshape(across // SUBLANES, SUBLANES, LANES), axis=0)
            met = jnp.sum(total, axis=0, keepdims=True)
            drag = drag_coef * blob_ref[bodies + 8 * b + 6 : bodies + 8 * b + 7, :] * (
                met - blob_ref[bodies + 8 * b + 3 + c : bodies + 8 * b + 4 + c, :]
            )
            force_ref[c, b : b + 1, :] += drag
            for h in range(depth):
                weights[c * depth + h : c * depth + h + 1, column] = (-source_gain) * near[h] * drag
        ones = lane_one_hot(halves, jnp.where(over >= half, over - half, over))
        for n, part in enumerate(split_parts(weights[:, column])):
            for k in range(3 * depth):
                coupled[k * half : (k + 1) * half, n * wide + b * LANES : n * wide + (b + 1) * LANES] = place_lines(
                    ones, part[k : k + 1], half
                )
    sources = [
        lax.dot_general(
            coupled[c * depth * half : (c + 1) * depth * half, :],
            spots[...],
            (((1,), (1,)), ((), ())),
            preferred_element_type=F32,
        )
        for c in range(3)
    ]

    copy.wait()
    for i in range(listed):
        for c, h in share_out[blocks + i]:
            stencil(c, h)
        a, c = pair_ref[0, i], pair_ref[1, i]
        left = blob_ref[pl.ds(pl.multiple_of(bodies + 8 * a, 8), 8), :]
        ahead, behind = pair_sum(left, spread, c * LANES, react.at[i])
        for side, forces in enumerate((ahead, behind)):
            for d in range(3):
                found[2 * i + side, d : d + 1, :] = forces[d]
    for b in range(blocks):
        for d in range(3):
            total = force_ref[d, b : b + 1, :]
            for i in range(listed):
                for side in range(2):
                    total += jnp.where(pair_ref[side, i] == b, found[2 * i + side, d : d + 1, :], 0.0)
            force_ref[d, b : b + 1, :] = total
    for k, (c, h) in enumerate(slabs):
        given = [sources[c][h * half : (h + 1) * half, f * along : (f + 1) * along] for f in range(fold)]
        next_ref[c, h] += jnp.concatenate(given, axis=0)


def finish_kernel(counts, blocks, pairs, force_ref, partial_ref, *refs):
    n_in = sum(counts)
    sent = refs[: counts[0]]
    height_ins, across_ins, along_ins = by_axis(refs[counts[0] : counts[0] + n_in], counts)
    out_force, next_hbm, next_ref, spread, pieces, picks, seen_ref, coupled, spots, sems = refs[counts[0] + n_in :]
    depth, across, along = partial_ref.shape[1:]
    fold = spots.shape[0] // along
    half = across // fold
    wide = blocks * LANES
    bodies, cells, shares, lists, _ = blob_layout(across, blocks, pairs)
    even = parities()

    def ordered(arrived, axis):
        first = arrived[0][...]
        if len(arrived) == 1:
            return jnp.where(even[axis], 0.0, first), jnp.where(even[axis], first, 0.0)
        second = arrived[1][...]
        return jnp.where(even[axis], second, first), jnp.where(even[axis], first, second)

    across_low, across_high = ordered(across_ins, 1)
    across_low = diffuse * across_low
    across_high = diffuse * across_high
    edges = along_ins[0][...]
    if len(along_ins) > 1:
        edges = edges + along_ins[1][...]
    edges = diffuse * edges
    lanes = lax.broadcasted_iota(jnp.int32, (across, along), 1)
    downs = lax.broadcasted_iota(jnp.int32, (across, along), 0)
    rim = jnp.logical_or(lanes == 0, lanes == along - 1)
    copies = []
    for c in range(3):
        for h in range(depth):
            k = c * depth + h
            value = partial_ref[c, h]
            value += jnp.where(rim, pltpu.roll(edges, (along - 2 * k) % along, 1) if k else edges, 0.0)
            value += jnp.where(downs == 0, across_low[k : k + 1, :], 0.0)
            value += jnp.where(downs == across - 1, across_high[k : k + 1, :], 0.0)
            next_ref[c, h] = value
        if depth > 2:
            inner = pl.ds(1, depth - 2)
            copies.append(pltpu.make_async_copy(next_ref.at[c, inner], next_hbm.at[c, inner], sems.at[c]))
            copies[-1].start()

    rows = lax.broadcasted_iota(jnp.int32, (across, LANES), 0)
    halves = lax.broadcasted_iota(jnp.int32, (half, LANES), 0)
    sites = lax.broadcasted_iota(jnp.int32, (fold * along, LANES), 0)
    coupling = [[jnp.zeros((1, LANES), F32)] * blocks for _ in range(3)]
    for n, blob in enumerate(height_ins):
        own = sent[n]
        above = even[0] if n == 0 else jnp.logical_not(even[0])
        own_layer = jnp.where(above, depth - 1, 0)
        below = jnp.logical_not(above)
        for k in range(3):
            face = slice(k * across, (k + 1) * across)
            pieces[face, :] = parts_of(blob[face, :])
            pieces[(3 + k) * across : (4 + k) * across, :] = parts_of(own[face, :])
        lined = []
        for b in range(blocks):
            cell = jnp.where(above, own[cells + b : cells + b + 1, :], blob[cells + b : cells + b + 1, :])
            height, over, spot = places(cell.astype(jnp.int32), across, along)
            lined.append((height, over))
            one_hot = lane_one_hot(sites[:along], spot)
            for m in range(PARTS):
                picks[m * along : (m + 1) * along, b * LANES : (b + 1) * LANES] = one_hot
            one_hot = lane_one_hot(sites, jnp.where(over >= half, along, 0) + spot)
            for m in range(PARTS):
                spots[:, m * wide + b * LANES : m * wide + (b + 1) * LANES] = one_hot
        seen_ref[...] = jnp.dot(pieces[...], picks[...], preferred_element_type=F32)
        for b in range(blocks):
            height, over = lined[b]
            share = jnp.where(above, own[shares + b : shares + b + 1, :], blob[shares + b : shares + b + 1, :])
            body = slice(bodies + 8 * b, bodies + 8 * b + 8)
            owner = jnp.where(above, own[body, :], blob[body, :])
            top = height == depth - 1
            mask = rows == over
            column = slice(b * LANES, (b + 1) * LANES)
            seen_share = jnp.where(top, jnp.where(above, share, 1.0 - share), 0.0)
            home_share = jnp.where(jnp.logical_and(top, below), share, 0.0)
            given_share = (-source_gain) * jnp.where(above, 1.0 - share, share)
            own_share = jnp.where(jnp.logical_and(top, below), 1.0, 0.0)
            ones = lane_one_hot(halves, jnp.where(over >= half, over - half, over))
            for c in range(3):
                seen = seen_ref[c * across : (c + 1) * across, column]
                home = seen_ref[(3 + c) * across : (4 + c) * across, column]
                met = jnp.where(mask, seen_share * seen + home_share * home, 0.0)
                met = jnp.sum(met, axis=0, keepdims=True)
                drag = drag_coef * owner[6:7] * (met - own_share * owner[3 + c : 4 + c])
                coupling[c][b] += jnp.where(above, drag, 0.0)
                for m, part in enumerate(split_parts(given_share * drag)):
                    coupled[c * half : (c + 1) * half, m * wide + b * LANES : m * wide + (b + 1) * LANES] = (
                        place_lines(ones, part, half)
                    )
        source = lax.dot_general(
            coupled[...], spots[...], (((1,), (1,)), ((), ())), preferred_element_type=F32
        )
        for c in range(3):
            given = [source[c * half : (c + 1) * half, f * along : (f + 1) * along] for f in range(fold)]
            next_ref[c, own_layer] += diffuse * blob[c * across : (c + 1) * across, :] + jnp.concatenate(given, axis=0)
    for n, h in enumerate(sorted({0, depth - 1})):
        copies.append(pltpu.make_async_copy(next_ref.at[:, h], next_hbm.at[:, h], sems.at[3 + n]))
        copies[-1].start()

    meetings, partners = [], []
    for n, blob in enumerate(height_ins):
        own = sent[n]
        above = even[0] if n == 0 else jnp.logical_not(even[0])
        for k in range(pairs):
            ours = [own[lists + 2 * k + side : lists + 2 * k + side + 1, :] for side in range(2)]
            theirs = [blob[lists + 2 * k + side : lists + 2 * k + side + 1, :] for side in range(2)]
            to = jnp.where(above, ours[0], theirs[1])
            by = jnp.where(above, ours[1], theirs[0])
            left = own[bodies : bodies + 8, :]
            right = blob[bodies : bodies + 8, :]
            for b in range(1, blocks):
                body = slice(bodies + 8 * b, bodies + 8 * b + 8)
                left = jnp.where(to == b, own[body, :], left)
                right = jnp.where(by == b, blob[body, :], right)
            meetings.append((to, left))
            partners.append(right)
    spread[...] = spread_blocks(partners)
    for i, (to, left) in enumerate(meetings):
        force, _ = pair_sum(left, spread, i * LANES, None)
        for b in range(blocks):
            for c in range(3):
                coupling[c][b] += jnp.where(to == b, force[c], 0.0)
    for b in range(blocks):
        for c in range(3):
            out_force[c, b : b + 1, :] = force_ref[c, b : b + 1, :] + coupling[c][b]
    for copy in copies:
        copy.wait()


def by_axis(refs, counts):
    groups, at = [], 0
    for n in counts:
        groups.append(refs[at : at + n])
        at += n
    return groups


def exchange(payloads, axis):
    count = lax.axis_size(axis)
    results = []
    for n, payload in enumerate(payloads):
        route = []
        for i in range(n, count - 1, 2):
            route += [(i, i + 1), (i + 1, i)]
        results.append(lax.ppermute(payload, axis, route))
    return results


def body(particles, local_pairs, cross_pairs, drag_cell, drag_share, fluid):
    blocks = particles.shape[0]
    pairs = cross_pairs.shape[0]
    listed = local_pairs.shape[0]
    _, depth, across, along = fluid.shape
    counts = [min(2, lax.axis_size(axis) - 1) for axis in AXES]
    fold = 2 if across % 32 == 0 else 1
    half = across // fold
    wide = PARTS * blocks * LANES
    rows = blob_layout(across, blocks, pairs)[-1]
    shapes = [(rows, along), (3 * depth, along), (across, along)]
    vmem = pl.BlockSpec(memory_space=pltpu.VMEM)
    hbm = pl.BlockSpec(memory_space=pl.ANY)

    def kept(value):
        return pltpu.with_memory_space_constraint(value, pltpu.VMEM)

    fluid_kept, *packed = pl.pallas_call(
        functools.partial(pack_kernel, counts),
        out_shape=[pltpu.VMEM(fluid.shape, F32)]
        + [pltpu.VMEM(shape, F32) for shape, n in zip(shapes, counts) for _ in range(n)],
        in_specs=[hbm] * 5,
        out_specs=[vmem] * (1 + sum(counts)),
        scratch_shapes=[
            pltpu.SMEM(cross_pairs.shape, jnp.int32),
            pltpu.VMEM(particles.shape, F32),
            pltpu.VMEM(drag_cell.shape, jnp.int32),
            pltpu.VMEM(drag_share.shape, F32),
            pltpu.SemaphoreType.DMA((7,)),
        ],
        name="pack",
    )(cross_pairs, particles, drag_cell, drag_share, fluid)
    received = []
    for axis, payloads in zip(AXES, by_axis(packed, counts)):
        received += exchange(payloads, axis)

    force, partial = pl.pallas_call(
        functools.partial(local_kernel, blocks, pairs),
        out_shape=[pltpu.VMEM((3, blocks, LANES), F32), pltpu.VMEM(fluid.shape, F32)],
        in_specs=[hbm, vmem, vmem],
        out_specs=[vmem, vmem],
        scratch_shapes=[
            pltpu.VMEM((blocks * LANES, 9 * LANES), F32),
            pltpu.VMEM((listed, LANES, LANES), F32),
            pltpu.VMEM((3 * depth * across, PARTS * along), BF16),
            pltpu.VMEM((3 * depth * across, blocks * LANES), F32),
            pltpu.VMEM((PARTS * along, blocks * LANES), BF16),
            pltpu.VMEM((2 * listed, SUBLANES, LANES), F32),
            pltpu.VMEM((3 * depth, blocks * LANES), F32),
            pltpu.VMEM((3 * depth * half, wide), BF16),
            pltpu.VMEM((fold * along, wide), BF16),
            pltpu.SMEM((2, listed), jnp.int32),
            pltpu.SemaphoreType.DMA,
        ],
        name="local",
    )(local_pairs.T, kept(packed[0]), kept(fluid_kept))

    out_force, out_next = pl.pallas_call(
        functools.partial(finish_kernel, counts, blocks, pairs),
        out_shape=[
            jax.ShapeDtypeStruct((3, blocks, LANES), F32),
            jax.ShapeDtypeStruct(fluid.shape, F32),
        ],
        in_specs=[vmem] * (2 + counts[0] + len(received)),
        out_specs=[vmem, hbm],
        scratch_shapes=[
            pltpu.VMEM(fluid.shape, F32),
            pltpu.VMEM((counts[0] * pairs * LANES, 9 * LANES), F32),
            pltpu.VMEM((6 * across, PARTS * along), BF16),
            pltpu.VMEM((PARTS * along, blocks * LANES), BF16),
            pltpu.VMEM((6 * across, blocks * LANES), F32),
            pltpu.VMEM((3 * half, wide), BF16),
            pltpu.VMEM((fold * along, wide), BF16),
            pltpu.SemaphoreType.DMA((5,)),
        ],
        name="finish",
    )(*[kept(value) for value in [force, partial, *packed[: counts[0]], *received]])
    return jnp.transpose(out_force, (1, 0, 2)), out_next


def solution(mesh):
    in_specs = (
        P(("gx", "gy", "gz"), None, None),
        P(("gx", "gy", "gz"), None),
        P(("gx", "gy", "gz"), None),
        P(("gx", "gy", "gz"), None),
        P(("gx", "gy", "gz"), None),
        P(None, "gx", "gy", "gz"),
    )
    out_specs = (P(("gx", "gy", "gz"), None, None), P(None, "gx", "gy", "gz"))
    return jax.shard_map(body, mesh=mesh, in_specs=in_specs, out_specs=out_specs, check_vma=False)
```

```python
import functools

import jax
import jax.numpy as jnp
from jax import lax
from jax.experimental import pallas as pl
from jax.experimental.pallas import tpu as pltpu
from jax.sharding import PartitionSpec as P

soft_core = 0.01
damp_normal = 0.3
damp_tangent = 0.2
drag_coef = 1.5
diffuse = 0.1
source_gain = 0.5

F32 = jnp.float32
BF16 = jnp.bfloat16
PARTS = 2
EXACT = 3
LANES = 128
SUBLANES = 8
AXES = ("gx", "gy", "gz")


def split_parts(value, count=PARTS):
    parts = []
    for _ in range(count):
        part = value.astype(BF16).astype(F32)
        parts.append(part)
        value = value - part
    return parts


def places(cell, across, along):
    layer = across * along
    if layer & (layer - 1) or along & (along - 1):
        return cell // layer, cell // along % across, cell % along
    shift = along.bit_length() - 1
    high = layer.bit_length() - 1
    return (
        lax.shift_right_logical(cell, high),
        lax.shift_right_logical(cell, shift) & (across - 1),
        cell & (along - 1),
    )


def parts_of(value):
    return jnp.concatenate([part.astype(BF16) for part in split_parts(value)], axis=1)


def spread_blocks(blocks):
    columns = []
    for block in blocks:
        rows = jnp.concatenate([block, block[7:8] * jnp.sqrt(block[6:7])], axis=0)
        parts = split_parts(rows, EXACT)
        parts.append(jnp.zeros((32 - 9 * EXACT, LANES), F32))
        columns.append(jnp.transpose(jnp.concatenate(parts, axis=0)).astype(BF16))
    lines = lax.broadcasted_iota(jnp.int32, (32, LANES), 0)
    picks = []
    for i in range(9):
        pick = lines == i
        for n in range(1, EXACT):
            pick = jnp.logical_or(pick, lines == i + 9 * n)
        picks.append(jnp.where(pick, 1.0, 0.0).astype(BF16))
    return jnp.dot(
        jnp.concatenate(columns, axis=0), jnp.concatenate(picks, axis=1), preferred_element_type=F32
    )


def pair_sum(left, spread, start, react):
    rows = [left[i : i + 1] for i in range(8)]
    rows.append((2.0 * damp_tangent) * rows[7] * jnp.sqrt(rows[6]))
    wide = [jnp.broadcast_to(row, (SUBLANES, LANES)) for row in rows]
    lanes = lax.broadcasted_iota(jnp.int32, (SUBLANES, LANES), 1)
    total = [None] * 3
    for tile in range(LANES // SUBLANES):
        place = pl.ds(pl.multiple_of(start + tile * SUBLANES, SUBLANES), SUBLANES)
        there = [spread[place, i * LANES : (i + 1) * LANES] for i in range(9)]
        ex, ey, ez, wx, wy, wz = [wide[i] - there[i] for i in range(6)]
        square = (ex * ex + ey * ey) + (ez * ez + soft_core)
        inverse = lax.rsqrt(square)
        reach = wide[6] + there[6]
        delta = jnp.maximum(reach - square * inverse, 0.0)
        mass = wide[7] + there[7]
        under = jnp.maximum((delta * reach) * (mass * mass), 1e-30)
        tangent = (wide[8] * there[8]) * (delta * lax.rsqrt(under))
        speed = ((wx * ex + wy * ey) + wz * ez) * inverse
        along = (
            (2.0 / 3.0 / damp_tangent) * delta - ((damp_normal - damp_tangent) / damp_tangent) * speed
        ) * (tangent * inverse)
        column = None
        for d, (e, w) in enumerate(((ex, wx), (ey, wy), (ez, wz))):
            force = along * e - tangent * w
            total[d] = force if total[d] is None else total[d] + force
            if react is not None:
                across_sum = jnp.broadcast_to(jnp.sum(force, axis=1, keepdims=True), (SUBLANES, LANES))
                column = across_sum if column is None else jnp.where(lanes == d, across_sum, column)
        if react is not None:
            react[tile * SUBLANES : (tile + 1) * SUBLANES, :] = column
    total = [jnp.sum(item, axis=0, keepdims=True) for item in total]
    if react is None:
        return total, None
    turned = jnp.transpose(react[...])
    return total, [-turned[d : d + 1] for d in range(3)]


def blob_layout(across, blocks, pairs):
    bodies = 3 * across
    cells = bodies + 8 * blocks
    shares = cells + blocks
    lists = shares + blocks
    rows = lists + 2 * pairs
    return bodies, cells, shares, lists, rows + -rows % 8


def parities():
    return [lax.rem(lax.axis_index(axis), 2) == 0 for axis in AXES]


def pack_kernel(counts, pair_hbm, part_hbm, cell_hbm, share_hbm, fluid_hbm, *refs):
    n_out = 2 + sum(counts)
    fluid_ref, wrap_ref, outs = refs[0], refs[1], refs[2:n_out]
    pair_ref, part_ref, cell_ref, share_ref, sems = refs[n_out:]
    height_outs, across_outs, along_outs = by_axis(outs, counts)
    depth, across, along = fluid_ref.shape[1:]
    blocks, pairs = part_ref.shape[0], pair_ref.shape[0]
    bodies, cells, shares, lists, rows = blob_layout(across, blocks, pairs)
    copies = [pltpu.make_async_copy(fluid_hbm.at[c], fluid_ref.at[c], sems.at[c]) for c in range(3)]
    small = [(pair_hbm, pair_ref), (part_hbm, part_ref), (cell_hbm, cell_ref), (share_hbm, share_ref)]
    small = [pltpu.make_async_copy(source, target, sems.at[3 + n]) for n, (source, target) in enumerate(small)]
    for copy in copies + small:
        copy.start()
    even = parities()
    for copy in small:
        copy.wait()
    for n, out in enumerate(height_outs):
        for b in range(blocks):
            out[bodies + 8 * b : bodies + 8 * b + 8, :] = part_ref[b]
        out[cells:shares, :] = cell_ref[...].astype(F32)
        out[shares:lists, :] = share_ref[...]
        for k in range(pairs):
            for side in range(2):
                row = lists + 2 * k + side
                out[row : row + 1, :] = jnp.full((1, LANES), pair_ref[k, side], jnp.int32).astype(F32)
        used = lists + 2 * pairs
        if used < rows:
            out[used:rows, :] = jnp.zeros((rows - used, LANES), F32)

    lanes = lax.broadcasted_iota(jnp.int32, (across, along), 1)
    first = jnp.zeros((across, along), F32)
    last = jnp.zeros((across, along), F32)
    for c in range(3):
        copies[c].wait()
        for n, out in enumerate(height_outs):
            upward = even[0] if n == 0 else jnp.logical_not(even[0])
            out[c * across : (c + 1) * across, :] = fluid_ref[c, jnp.where(upward, depth - 1, 0)]
        for h in range(depth):
            k = c * depth + h
            here = fluid_ref[c, h]
            for n, out in enumerate(across_outs):
                upward = even[1] if n == 0 else jnp.logical_not(even[1])
                out[k : k + 1, :] = jnp.where(upward, here[across - 1 : across], here[0:1])
            turned = pltpu.roll(here, 2 * k, 1) if k else here
            first = jnp.where(lanes == 2 * k, turned, first)
            last = jnp.where(lanes == (2 * k - 1) % along, turned, last)
    first = pltpu.roll(first, along - 1, 1)
    last = pltpu.roll(last, 1, 1)
    wrap_ref[...] = first + last
    for n, out in enumerate(along_outs):
        upward = even[2] if n == 0 else jnp.logical_not(even[2])
        out[...] = jnp.where(upward, last, first)


def lane_one_hot(sites, target):
    return jnp.where(sites == target, 1.0, 0.0).astype(BF16)


def place_lines(ones, part, half):
    line = jnp.broadcast_to(part, (16, LANES)).astype(BF16)
    line = jnp.concatenate([line] * (half // 16), axis=0)
    return jnp.where(ones > 0, line, jnp.zeros_like(line))


def local_kernel(
    blocks, pairs, pair_hbm, blob_ref, fluid_ref, force_ref, next_ref,
    spread, react, pieces, seen_ref, picks, found, weights, coupled, spots, pair_ref, sem,
):
    depth, across, along = fluid_ref.shape[1:]
    listed = pair_ref.shape[1]
    fold = spots.shape[0] // along
    half = across // fold
    wide = blocks * LANES
    bodies, cells, shares, _, _ = blob_layout(across, blocks, pairs)
    copy = pltpu.make_async_copy(pair_hbm, pair_ref, sem)
    copy.start()
    rows = lax.broadcasted_iota(jnp.int32, (across, LANES), 0)
    halves = lax.broadcasted_iota(jnp.int32, (half, LANES), 0)
    sites = lax.broadcasted_iota(jnp.int32, (fold * along, LANES), 0)
    subs = lax.broadcasted_iota(jnp.int32, (SUBLANES, along), 0)
    slabs = [(c, h) for c in range(3) for h in range(depth)]

    def body_of(b):
        return blob_ref[bodies + 8 * b : bodies + 8 * b + 8, :]

    def spot_of(b):
        return places(blob_ref[cells + b : cells + b + 1, :].astype(jnp.int32), across, along)

    def stencil(c, h):
        for t in range(across // SUBLANES):
            at = t * SUBLANES
            here = fluid_ref[c, h, at : at + SUBLANES, :]
            if t > 0:
                beside = fluid_ref[c, h, at - 1 : at + SUBLANES - 1, :]
            else:
                beside = jnp.where(subs == 0, 0.0, pltpu.roll(here, 1, 0))
            if at + SUBLANES < across:
                beside += fluid_ref[c, h, at + 1 : at + SUBLANES + 1, :]
            else:
                beside += jnp.where(subs == SUBLANES - 1, 0.0, pltpu.roll(here, SUBLANES - 1, 0))
            beside += pltpu.roll(here, 1, 1) + pltpu.roll(here, along - 1, 1)
            if h > 0:
                beside += fluid_ref[c, h - 1, at : at + SUBLANES, :]
            if h < depth - 1:
                beside += fluid_ref[c, h + 1, at : at + SUBLANES, :]
            next_ref[c, h, at : at + SUBLANES, :] = (1.0 - 6.0 * diffuse) * here + diffuse * beside

    spread[...] = spread_blocks([body_of(b) for b in range(blocks)])
    for k, (c, h) in enumerate(slabs):
        pieces[k * across : (k + 1) * across, :] = parts_of(fluid_ref[c, h])
    for b in range(blocks):
        height, over, spot = spot_of(b)
        column = slice(b * LANES, (b + 1) * LANES)
        one_hot = lane_one_hot(sites[:along], spot)
        for n in range(PARTS):
            picks[n * along : (n + 1) * along, column] = one_hot
        one_hot = lane_one_hot(sites, jnp.where(over >= half, along, 0) + spot)
        for n in range(PARTS):
            spots[:, n * wide + b * LANES : n * wide + (b + 1) * LANES] = one_hot
    seen_ref[...] = jnp.dot(pieces[...], picks[...], preferred_element_type=F32)

    turns = blocks + listed
    share_out = [slabs[i * len(slabs) // turns : (i + 1) * len(slabs) // turns] for i in range(turns)]
    for b in range(blocks):
        for c, h in share_out[b]:
            stencil(c, h)
        force, _ = pair_sum(body_of(b), spread, b * LANES, None)
        for c in range(3):
            force_ref[c, b : b + 1, :] = force[c]

    for b in range(blocks):
        height, over, _ = spot_of(b)
        share = blob_ref[shares + b : shares + b + 1, :]
        mask = rows == over
        column = slice(b * LANES, (b + 1) * LANES)
        near = [
            jnp.where(height == h, 1.0 - share, jnp.where(height == h - 1, share, 0.0)) for h in range(depth)
        ]
        for c in range(3):
            total = jnp.zeros((SUBLANES, LANES), F32)
            for h in range(depth):
                k = c * depth + h
                seen = jnp.where(mask, seen_ref[k * across : (k + 1) * across, column], 0.0)
                total += near[h] * jnp.sum(seen.reshape(across // SUBLANES, SUBLANES, LANES), axis=0)
            met = jnp.sum(total, axis=0, keepdims=True)
            drag = drag_coef * blob_ref[bodies + 8 * b + 6 : bodies + 8 * b + 7, :] * (
                met - blob_ref[bodies + 8 * b + 3 + c : bodies + 8 * b + 4 + c, :]
            )
            force_ref[c, b : b + 1, :] += drag
            for h in range(depth):
                weights[c * depth + h : c * depth + h + 1, column] = (-source_gain) * near[h] * drag
        ones = lane_one_hot(halves, jnp.where(over >= half, over - half, over))
        for n, part in enumerate(split_parts(weights[:, column])):
            for k in range(3 * depth):
                coupled[k * half : (k + 1) * half, n * wide + b * LANES : n * wide + (b + 1) * LANES] = place_lines(
                    ones, part[k : k + 1], half
                )
    sources = [
        lax.dot_general(
            coupled[c * depth * half : (c + 1) * depth * half, :],
            spots[...],
            (((1,), (1,)), ((), ())),
            preferred_element_type=F32,
        )
        for c in range(3)
    ]

    copy.wait()
    for i in range(listed):
        for c, h in share_out[blocks + i]:
            stencil(c, h)
        a, c = pair_ref[0, i], pair_ref[1, i]
        left = blob_ref[pl.ds(pl.multiple_of(bodies + 8 * a, 8), 8), :]
        ahead, behind = pair_sum(left, spread, c * LANES, react.at[i])
        for side, forces in enumerate((ahead, behind)):
            for d in range(3):
                found[2 * i + side, d : d + 1, :] = forces[d]
    for b in range(blocks):
        for d in range(3):
            total = force_ref[d, b : b + 1, :]
            for i in range(listed):
                for side in range(2):
                    total += jnp.where(pair_ref[side, i] == b, found[2 * i + side, d : d + 1, :], 0.0)
            force_ref[d, b : b + 1, :] = total
    for k, (c, h) in enumerate(slabs):
        given = [sources[c][h * half : (h + 1) * half, f * along : (f + 1) * along] for f in range(fold)]
        next_ref[c, h] += jnp.concatenate(given, axis=0)


def finish_kernel(counts, blocks, pairs, force_ref, partial_ref, wrap_ref, *refs):
    n_in = sum(counts)
    sent = refs[: counts[0]]
    height_ins, across_ins, along_ins = by_axis(refs[counts[0] : counts[0] + n_in], counts)
    out_force, next_hbm, next_ref, spread, pieces, picks, seen_ref, coupled, spots, sems = refs[counts[0] + n_in :]
    depth, across, along = partial_ref.shape[1:]
    fold = spots.shape[0] // along
    half = across // fold
    wide = blocks * LANES
    bodies, cells, shares, lists, _ = blob_layout(across, blocks, pairs)
    even = parities()

    def ordered(arrived, axis):
        first = arrived[0][...]
        if len(arrived) == 1:
            return jnp.where(even[axis], 0.0, first), jnp.where(even[axis], first, 0.0)
        second = arrived[1][...]
        return jnp.where(even[axis], second, first), jnp.where(even[axis], first, second)

    across_low, across_high = ordered(across_ins, 1)
    across_low = diffuse * across_low
    across_high = diffuse * across_high
    edges = along_ins[0][...]
    if len(along_ins) > 1:
        edges = edges + along_ins[1][...]
    edges = diffuse * (edges - wrap_ref[...])
    lanes = lax.broadcasted_iota(jnp.int32, (across, along), 1)
    subs = lax.broadcasted_iota(jnp.int32, (SUBLANES, along), 0)
    tail = across - SUBLANES
    rim = jnp.logical_or(lanes == 0, lanes == along - 1)
    copies = []
    for c in range(3):
        for h in range(depth):
            k = c * depth + h
            value = partial_ref[c, h]
            value += jnp.where(rim, pltpu.roll(edges, (along - 2 * k) % along, 1) if k else edges, 0.0)
            next_ref[c, h] = value
            next_ref[c, h, :SUBLANES, :] += jnp.where(subs == 0, across_low[k : k + 1, :], 0.0)
            next_ref[c, h, tail:, :] += jnp.where(subs == SUBLANES - 1, across_high[k : k + 1, :], 0.0)
        if depth > 2:
            inner = pl.ds(1, depth - 2)
            copies.append(pltpu.make_async_copy(next_ref.at[c, inner], next_hbm.at[c, inner], sems.at[c]))
            copies[-1].start()

    rows = lax.broadcasted_iota(jnp.int32, (across, LANES), 0)
    halves = lax.broadcasted_iota(jnp.int32, (half, LANES), 0)
    sites = lax.broadcasted_iota(jnp.int32, (fold * along, LANES), 0)
    coupling = [[jnp.zeros((1, LANES), F32)] * blocks for _ in range(3)]
    for n, blob in enumerate(height_ins):
        own = sent[n]
        above = even[0] if n == 0 else jnp.logical_not(even[0])
        own_layer = jnp.where(above, depth - 1, 0)
        below = jnp.logical_not(above)
        for k in range(3):
            face = slice(k * across, (k + 1) * across)
            pieces[face, :] = parts_of(blob[face, :])
            pieces[(3 + k) * across : (4 + k) * across, :] = parts_of(own[face, :])
        lined = []
        for b in range(blocks):
            cell = jnp.where(above, own[cells + b : cells + b + 1, :], blob[cells + b : cells + b + 1, :])
            height, over, spot = places(cell.astype(jnp.int32), across, along)
            lined.append((height, over))
            one_hot = lane_one_hot(sites[:along], spot)
            for m in range(PARTS):
                picks[m * along : (m + 1) * along, b * LANES : (b + 1) * LANES] = one_hot
            one_hot = lane_one_hot(sites, jnp.where(over >= half, along, 0) + spot)
            for m in range(PARTS):
                spots[:, m * wide + b * LANES : m * wide + (b + 1) * LANES] = one_hot
        seen_ref[...] = jnp.dot(pieces[...], picks[...], preferred_element_type=F32)
        for b in range(blocks):
            height, over = lined[b]
            share = jnp.where(above, own[shares + b : shares + b + 1, :], blob[shares + b : shares + b + 1, :])
            body = slice(bodies + 8 * b, bodies + 8 * b + 8)
            owner = jnp.where(above, own[body, :], blob[body, :])
            top = height == depth - 1
            mask = rows == over
            column = slice(b * LANES, (b + 1) * LANES)
            seen_share = jnp.where(top, jnp.where(above, share, 1.0 - share), 0.0)
            home_share = jnp.where(jnp.logical_and(top, below), share, 0.0)
            given_share = (-source_gain) * jnp.where(above, 1.0 - share, share)
            own_share = jnp.where(jnp.logical_and(top, below), 1.0, 0.0)
            ones = lane_one_hot(halves, jnp.where(over >= half, over - half, over))
            for c in range(3):
                seen = seen_ref[c * across : (c + 1) * across, column]
                home = seen_ref[(3 + c) * across : (4 + c) * across, column]
                met = jnp.where(mask, seen_share * seen + home_share * home, 0.0)
                met = jnp.sum(met, axis=0, keepdims=True)
                drag = drag_coef * owner[6:7] * (met - own_share * owner[3 + c : 4 + c])
                coupling[c][b] += jnp.where(above, drag, 0.0)
                for m, part in enumerate(split_parts(given_share * drag)):
                    coupled[c * half : (c + 1) * half, m * wide + b * LANES : m * wide + (b + 1) * LANES] = (
                        place_lines(ones, part, half)
                    )
        source = lax.dot_general(
            coupled[...], spots[...], (((1,), (1,)), ((), ())), preferred_element_type=F32
        )
        for c in range(3):
            given = [source[c * half : (c + 1) * half, f * along : (f + 1) * along] for f in range(fold)]
            next_ref[c, own_layer] += diffuse * blob[c * across : (c + 1) * across, :] + jnp.concatenate(given, axis=0)
    for n, h in enumerate(sorted({0, depth - 1})):
        copies.append(pltpu.make_async_copy(next_ref.at[:, h], next_hbm.at[:, h], sems.at[3 + n]))
        copies[-1].start()

    meetings, partners = [], []
    for n, blob in enumerate(height_ins):
        own = sent[n]
        above = even[0] if n == 0 else jnp.logical_not(even[0])
        for k in range(pairs):
            ours = [own[lists + 2 * k + side : lists + 2 * k + side + 1, :] for side in range(2)]
            theirs = [blob[lists + 2 * k + side : lists + 2 * k + side + 1, :] for side in range(2)]
            to = jnp.where(above, ours[0], theirs[1])
            by = jnp.where(above, ours[1], theirs[0])
            left = own[bodies : bodies + 8, :]
            right = blob[bodies : bodies + 8, :]
            for b in range(1, blocks):
                body = slice(bodies + 8 * b, bodies + 8 * b + 8)
                left = jnp.where(to == b, own[body, :], left)
                right = jnp.where(by == b, blob[body, :], right)
            meetings.append((to, left))
            partners.append(right)
    spread[...] = spread_blocks(partners)
    for i, (to, left) in enumerate(meetings):
        force, _ = pair_sum(left, spread, i * LANES, None)
        for b in range(blocks):
            for c in range(3):
                coupling[c][b] += jnp.where(to == b, force[c], 0.0)
    for b in range(blocks):
        for c in range(3):
            out_force[c, b : b + 1, :] = force_ref[c, b : b + 1, :] + coupling[c][b]
    for copy in copies:
        copy.wait()


def by_axis(refs, counts):
    groups, at = [], 0
    for n in counts:
        groups.append(refs[at : at + n])
        at += n
    return groups


def exchange(payloads, axis):
    count = lax.axis_size(axis)
    results = []
    for n, payload in enumerate(payloads):
        route = []
        for i in range(n, count - 1, 2):
            route += [(i, i + 1), (i + 1, i)]
        results.append(lax.ppermute(payload, axis, route))
    return results


def body(particles, local_pairs, cross_pairs, drag_cell, drag_share, fluid):
    blocks = particles.shape[0]
    pairs = cross_pairs.shape[0]
    listed = local_pairs.shape[0]
    _, depth, across, along = fluid.shape
    counts = [min(2, lax.axis_size(axis) - 1) for axis in AXES]
    fold = 2 if across % 32 == 0 else 1
    half = across // fold
    wide = PARTS * blocks * LANES
    rows = blob_layout(across, blocks, pairs)[-1]
    shapes = [(rows, along), (3 * depth, along), (across, along)]
    vmem = pl.BlockSpec(memory_space=pltpu.VMEM)
    hbm = pl.BlockSpec(memory_space=pl.ANY)

    def kept(value):
        return pltpu.with_memory_space_constraint(value, pltpu.VMEM)

    fluid_kept, wrapped, *packed = pl.pallas_call(
        functools.partial(pack_kernel, counts),
        out_shape=[pltpu.VMEM(fluid.shape, F32), pltpu.VMEM((across, along), F32)]
        + [pltpu.VMEM(shape, F32) for shape, n in zip(shapes, counts) for _ in range(n)],
        in_specs=[hbm] * 5,
        out_specs=[vmem] * (2 + sum(counts)),
        scratch_shapes=[
            pltpu.SMEM(cross_pairs.shape, jnp.int32),
            pltpu.VMEM(particles.shape, F32),
            pltpu.VMEM(drag_cell.shape, jnp.int32),
            pltpu.VMEM(drag_share.shape, F32),
            pltpu.SemaphoreType.DMA((7,)),
        ],
        name="pack",
    )(cross_pairs, particles, drag_cell, drag_share, fluid)
    received = []
    for axis, payloads in zip(AXES, by_axis(packed, counts)):
        received += exchange(payloads, axis)

    force, partial = pl.pallas_call(
        functools.partial(local_kernel, blocks, pairs),
        out_shape=[pltpu.VMEM((3, blocks, LANES), F32), pltpu.VMEM(fluid.shape, F32)],
        in_specs=[hbm, vmem, vmem],
        out_specs=[vmem, vmem],
        scratch_shapes=[
            pltpu.VMEM((blocks * LANES, 9 * LANES), F32),
            pltpu.VMEM((listed, LANES, LANES), F32),
            pltpu.VMEM((3 * depth * across, PARTS * along), BF16),
            pltpu.VMEM((3 * depth * across, blocks * LANES), F32),
            pltpu.VMEM((PARTS * along, blocks * LANES), BF16),
            pltpu.VMEM((2 * listed, SUBLANES, LANES), F32),
            pltpu.VMEM((3 * depth, blocks * LANES), F32),
            pltpu.VMEM((3 * depth * half, wide), BF16),
            pltpu.VMEM((fold * along, wide), BF16),
            pltpu.SMEM((2, listed), jnp.int32),
            pltpu.SemaphoreType.DMA,
        ],
        name="local",
    )(local_pairs.T, kept(packed[0]), kept(fluid_kept))

    out_force, out_next = pl.pallas_call(
        functools.partial(finish_kernel, counts, blocks, pairs),
        out_shape=[
            jax.ShapeDtypeStruct((3, blocks, LANES), F32),
            jax.ShapeDtypeStruct(fluid.shape, F32),
        ],
        in_specs=[vmem] * (3 + counts[0] + len(received)),
        out_specs=[vmem, hbm],
        scratch_shapes=[
            pltpu.VMEM(fluid.shape, F32),
            pltpu.VMEM((counts[0] * pairs * LANES, 9 * LANES), F32),
            pltpu.VMEM((6 * across, PARTS * along), BF16),
            pltpu.VMEM((PARTS * along, blocks * LANES), BF16),
            pltpu.VMEM((6 * across, blocks * LANES), F32),
            pltpu.VMEM((3 * half, wide), BF16),
            pltpu.VMEM((fold * along, wide), BF16),
            pltpu.SemaphoreType.DMA((5,)),
        ],
        name="finish",
    )(*[kept(value) for value in [force, partial, wrapped, *packed[: counts[0]], *received]])
    return jnp.transpose(out_force, (1, 0, 2)), out_next


def solution(mesh):
    in_specs = (
        P(("gx", "gy", "gz"), None, None),
        P(("gx", "gy", "gz"), None),
        P(("gx", "gy", "gz"), None),
        P(("gx", "gy", "gz"), None),
        P(("gx", "gy", "gz"), None),
        P(None, "gx", "gy", "gz"),
    )
    out_specs = (P(("gx", "gy", "gz"), None, None), P(None, "gx", "gy", "gz"))
    return jax.shard_map(body, mesh=mesh, in_specs=in_specs, out_specs=out_specs, check_vma=False)
```

```python
import functools

import jax
import jax.numpy as jnp
from jax import lax
from jax.experimental import pallas as pl
from jax.experimental.pallas import tpu as pltpu
from jax.sharding import PartitionSpec as P

soft_core = 0.01
damp_normal = 0.3
damp_tangent = 0.2
drag_coef = 1.5
diffuse = 0.1
source_gain = 0.5

F32 = jnp.float32
BF16 = jnp.bfloat16
PARTS = 2
EXACT = 3
LANES = 128
SUBLANES = 8
GRANT = 32 * 1024 * 1024
AXES = ("gx", "gy", "gz")


def split_parts(value, count=PARTS):
    parts = []
    for _ in range(count):
        part = value.astype(BF16).astype(F32)
        parts.append(part)
        value = value - part
    return parts


def places(cell, across, along):
    layer = across * along
    if layer & (layer - 1) or along & (along - 1):
        return cell // layer, cell // along % across, cell % along
    shift = along.bit_length() - 1
    high = layer.bit_length() - 1
    return (
        lax.shift_right_logical(cell, high),
        lax.shift_right_logical(cell, shift) & (across - 1),
        cell & (along - 1),
    )


def parts_of(value):
    return jnp.concatenate([part.astype(BF16) for part in split_parts(value)], axis=1)


def spread_blocks(blocks):
    columns = []
    for block in blocks:
        rows = jnp.concatenate([block, block[7:8] * jnp.sqrt(block[6:7])], axis=0)
        parts = split_parts(rows, EXACT)
        parts.append(jnp.zeros((32 - 9 * EXACT, LANES), F32))
        columns.append(jnp.transpose(jnp.concatenate(parts, axis=0)).astype(BF16))
    lines = lax.broadcasted_iota(jnp.int32, (32, LANES), 0)
    picks = []
    for i in range(9):
        pick = lines == i
        for n in range(1, EXACT):
            pick = jnp.logical_or(pick, lines == i + 9 * n)
        picks.append(jnp.where(pick, 1.0, 0.0).astype(BF16))
    return jnp.dot(
        jnp.concatenate(columns, axis=0), jnp.concatenate(picks, axis=1), preferred_element_type=F32
    )


def pair_sum(left, spread, start, react):
    rows = [left[i : i + 1] for i in range(8)]
    rows.append((2.0 * damp_tangent) * rows[7] * jnp.sqrt(rows[6]))
    wide = [jnp.broadcast_to(row, (SUBLANES, LANES)) for row in rows]
    lanes = lax.broadcasted_iota(jnp.int32, (SUBLANES, LANES), 1)
    total = [None] * 3
    for tile in range(LANES // SUBLANES):
        place = pl.ds(pl.multiple_of(start + tile * SUBLANES, SUBLANES), SUBLANES)
        there = [spread[place, i * LANES : (i + 1) * LANES] for i in range(9)]
        ex, ey, ez, wx, wy, wz = [wide[i] - there[i] for i in range(6)]
        square = (ex * ex + ey * ey) + (ez * ez + soft_core)
        inverse = lax.rsqrt(square)
        reach = wide[6] + there[6]
        delta = jnp.maximum(reach - square * inverse, 0.0)
        mass = wide[7] + there[7]
        under = jnp.maximum((delta * reach) * (mass * mass), 1e-30)
        tangent = (wide[8] * there[8]) * (delta * lax.rsqrt(under))
        speed = ((wx * ex + wy * ey) + wz * ez) * inverse
        along = (
            (2.0 / 3.0 / damp_tangent) * delta - ((damp_normal - damp_tangent) / damp_tangent) * speed
        ) * (tangent * inverse)
        column = None
        for d, (e, w) in enumerate(((ex, wx), (ey, wy), (ez, wz))):
            force = along * e - tangent * w
            total[d] = force if total[d] is None else total[d] + force
            if react is not None:
                across_sum = jnp.broadcast_to(jnp.sum(force, axis=1, keepdims=True), (SUBLANES, LANES))
                column = across_sum if column is None else jnp.where(lanes == d, across_sum, column)
        if react is not None:
            react[tile * SUBLANES : (tile + 1) * SUBLANES, :] = column
    total = [jnp.sum(item, axis=0, keepdims=True) for item in total]
    if react is None:
        return total, None
    turned = jnp.transpose(react[...])
    return total, [-turned[d : d + 1] for d in range(3)]


def blob_layout(across, blocks, pairs):
    bodies = 3 * across
    cells = bodies + 8 * blocks
    shares = cells + blocks
    lists = shares + blocks
    rows = lists + 2 * pairs
    return bodies, cells, shares, lists, rows + -rows % 8


def parities():
    return [lax.rem(lax.axis_index(axis), 2) == 0 for axis in AXES]


def pack_kernel(counts, pair_hbm, part_hbm, cell_hbm, share_hbm, fluid_hbm, *refs):
    n_out = 5 + sum(counts)
    fluid_ref, pieces, picks, spots, spread = refs[:5]
    height_outs, across_outs, along_outs = by_axis(refs[5:n_out], counts)
    pair_ref, part_ref, cell_ref, share_ref, sems = refs[n_out:]
    depth, across, along = fluid_ref.shape[1:]
    blocks, pairs = part_ref.shape[0], pair_ref.shape[0]
    fold = spots.shape[0] // along
    half = across // fold
    wide = blocks * LANES
    bodies, cells, shares, lists, rows = blob_layout(across, blocks, pairs)
    small = [(part_hbm, part_ref), (cell_hbm, cell_ref), (share_hbm, share_ref), (pair_hbm, pair_ref)]
    small = [pltpu.make_async_copy(source, target, sems.at[3 + n]) for n, (source, target) in enumerate(small)]
    copies = [pltpu.make_async_copy(fluid_hbm.at[c], fluid_ref.at[c], sems.at[c]) for c in range(3)]
    for copy in small + copies:
        copy.start()
    even = parities()
    for copy in small:
        copy.wait()
    for n, out in enumerate(height_outs):
        for b in range(blocks):
            out[bodies + 8 * b : bodies + 8 * b + 8, :] = part_ref[b]
        out[cells:shares, :] = cell_ref[...].astype(F32)
        out[shares:lists, :] = share_ref[...]
        for k in range(pairs):
            for side in range(2):
                row = lists + 2 * k + side
                out[row : row + 1, :] = jnp.full((1, LANES), pair_ref[k, side], jnp.int32).astype(F32)
        used = lists + 2 * pairs
        if used < rows:
            out[used:rows, :] = jnp.zeros((rows - used, LANES), F32)
    spread[...] = spread_blocks([part_ref[b] for b in range(blocks)])
    for b in range(blocks):
        _, over, spot = places(cell_ref[b : b + 1, :], across, along)
        mark_cells(picks, spots, b, over, spot, half, wide)
    sites = lax.broadcasted_iota(jnp.int32, (along, along), 0)
    lanes = lax.broadcasted_iota(jnp.int32, (along, along), 1)
    near = jnp.where(jnp.abs(sites - lanes) == 1, 1.0, 0.0).astype(BF16)
    for n in range(PARTS):
        picks[n * along : (n + 1) * along, wide : wide + along] = near

    lanes = lax.broadcasted_iota(jnp.int32, (across, along), 1)
    first = jnp.zeros((across, along), F32)
    last = jnp.zeros((across, along), F32)
    for c in range(3):
        copies[c].wait()
        for n, out in enumerate(height_outs):
            upward = even[0] if n == 0 else jnp.logical_not(even[0])
            out[c * across : (c + 1) * across, :] = fluid_ref[c, jnp.where(upward, depth - 1, 0)]
        for h in range(depth):
            k = c * depth + h
            here = fluid_ref[c, h]
            for n, out in enumerate(across_outs):
                upward = even[1] if n == 0 else jnp.logical_not(even[1])
                out[k : k + 1, :] = jnp.where(upward, here[across - 1 : across], here[0:1])
            turned = pltpu.roll(here, 2 * k, 1) if k else here
            first = jnp.where(lanes == 2 * k, turned, first)
            last = jnp.where(lanes == (2 * k - 1) % along, turned, last)
            pieces[k * across : (k + 1) * across, :] = parts_of(here)
    first = pltpu.roll(first, along - 1, 1)
    last = pltpu.roll(last, 1, 1)
    for n, out in enumerate(along_outs):
        upward = even[2] if n == 0 else jnp.logical_not(even[2])
        out[...] = jnp.where(upward, last, first)


def mark_cells(picks, spots, b, over, spot, half, wide):
    along = picks.shape[0] // PARTS
    sites = lax.broadcasted_iota(jnp.int32, (spots.shape[0], LANES), 0)
    one_hot = lane_one_hot(sites[:along], spot)
    for n in range(PARTS):
        picks[n * along : (n + 1) * along, b * LANES : (b + 1) * LANES] = one_hot
    one_hot = lane_one_hot(sites, jnp.where(over >= half, along, 0) + spot)
    for n in range(PARTS):
        spots[:, n * wide + b * LANES : n * wide + (b + 1) * LANES] = one_hot


def lane_one_hot(sites, target):
    return jnp.where(sites == target, 1.0, 0.0).astype(BF16)


def place_lines(ones, part, half):
    line = jnp.broadcast_to(part, (16, LANES)).astype(BF16)
    line = jnp.concatenate([line] * (half // 16), axis=0)
    return jnp.where(ones > 0, line, jnp.zeros_like(line))


def local_kernel(
    blocks, pairs, pair_hbm, blob_ref, fluid_ref, pieces, picks, spots, spread, force_ref, next_ref,
    react, seen_ref, found, weights, coupled, pair_ref, sem,
):
    depth, across, along = fluid_ref.shape[1:]
    listed = pair_ref.shape[1]
    fold = spots.shape[0] // along
    half = across // fold
    wide = blocks * LANES
    bodies, cells, shares, _, _ = blob_layout(across, blocks, pairs)
    copy = pltpu.make_async_copy(pair_hbm, pair_ref, sem)
    copy.start()
    rows = lax.broadcasted_iota(jnp.int32, (across, LANES), 0)
    halves = lax.broadcasted_iota(jnp.int32, (half, LANES), 0)
    subs = lax.broadcasted_iota(jnp.int32, (SUBLANES, along), 0)
    slabs = [(c, h) for c in range(3) for h in range(depth)]

    def body_of(b):
        return blob_ref[bodies + 8 * b : bodies + 8 * b + 8, :]

    def spot_of(b):
        return places(blob_ref[cells + b : cells + b + 1, :].astype(jnp.int32), across, along)

    def stencil(c, h):
        for t in range(across // SUBLANES):
            at = t * SUBLANES
            here = fluid_ref[c, h, at : at + SUBLANES, :]
            if t > 0:
                beside = fluid_ref[c, h, at - 1 : at + SUBLANES - 1, :]
            else:
                beside = jnp.where(subs == 0, 0.0, pltpu.roll(here, 1, 0))
            if at + SUBLANES < across:
                beside += fluid_ref[c, h, at + 1 : at + SUBLANES + 1, :]
            else:
                beside += jnp.where(subs == SUBLANES - 1, 0.0, pltpu.roll(here, SUBLANES - 1, 0))
            line = (c * depth + h) * across + at
            beside += seen_ref[line : line + SUBLANES, wide : wide + along]
            if h > 0:
                beside += fluid_ref[c, h - 1, at : at + SUBLANES, :]
            if h < depth - 1:
                beside += fluid_ref[c, h + 1, at : at + SUBLANES, :]
            next_ref[c, h, at : at + SUBLANES, :] = (1.0 - 6.0 * diffuse) * here + diffuse * beside

    seen_ref[...] = jnp.dot(pieces[...], picks[...], preferred_element_type=F32)

    turns = blocks + listed
    share_out = [slabs[i * len(slabs) // turns : (i + 1) * len(slabs) // turns] for i in range(turns)]
    for b in range(blocks):
        for c, h in share_out[b]:
            stencil(c, h)
        force, _ = pair_sum(body_of(b), spread, b * LANES, None)
        for c in range(3):
            force_ref[c, b : b + 1, :] = force[c]

    for b in range(blocks):
        height, over, _ = spot_of(b)
        share = blob_ref[shares + b : shares + b + 1, :]
        mask = rows == over
        column = slice(b * LANES, (b + 1) * LANES)
        near = [
            jnp.where(height == h, 1.0 - share, jnp.where(height == h - 1, share, 0.0)) for h in range(depth)
        ]
        for c in range(3):
            total = jnp.zeros((SUBLANES, LANES), F32)
            for h in range(depth):
                k = c * depth + h
                seen = jnp.where(mask, seen_ref[k * across : (k + 1) * across, column], 0.0)
                total += near[h] * jnp.sum(seen.reshape(across // SUBLANES, SUBLANES, LANES), axis=0)
            met = jnp.sum(total, axis=0, keepdims=True)
            drag = drag_coef * blob_ref[bodies + 8 * b + 6 : bodies + 8 * b + 7, :] * (
                met - blob_ref[bodies + 8 * b + 3 + c : bodies + 8 * b + 4 + c, :]
            )
            force_ref[c, b : b + 1, :] += drag
            for h in range(depth):
                weights[c * depth + h : c * depth + h + 1, column] = (-source_gain) * near[h] * drag
        ones = lane_one_hot(halves, jnp.where(over >= half, over - half, over))
        for n, part in enumerate(split_parts(weights[:, column])):
            for k in range(3 * depth):
                coupled[k * half : (k + 1) * half, n * wide + b * LANES : n * wide + (b + 1) * LANES] = place_lines(
                    ones, part[k : k + 1], half
                )
    sources = [
        lax.dot_general(
            coupled[c * depth * half : (c + 1) * depth * half, :],
            spots[...],
            (((1,), (1,)), ((), ())),
            preferred_element_type=F32,
        )
        for c in range(3)
    ]

    copy.wait()
    for i in range(listed):
        for c, h in share_out[blocks + i]:
            stencil(c, h)
        a, c = pair_ref[0, i], pair_ref[1, i]
        left = blob_ref[pl.ds(pl.multiple_of(bodies + 8 * a, 8), 8), :]
        ahead, behind = pair_sum(left, spread, c * LANES, react.at[i])
        for side, forces in enumerate((ahead, behind)):
            for d in range(3):
                found[2 * i + side, d : d + 1, :] = forces[d]
    for b in range(blocks):
        for d in range(3):
            total = force_ref[d, b : b + 1, :]
            for i in range(listed):
                for side in range(2):
                    total += jnp.where(pair_ref[side, i] == b, found[2 * i + side, d : d + 1, :], 0.0)
            force_ref[d, b : b + 1, :] = total
    for k, (c, h) in enumerate(slabs):
        given = [sources[c][h * half : (h + 1) * half, f * along : (f + 1) * along] for f in range(fold)]
        next_ref[c, h] += jnp.concatenate(given, axis=0)


def finish_kernel(counts, blocks, pairs, force_ref, partial_ref, *refs):
    n_in = sum(counts)
    sent = refs[: counts[0]]
    height_ins, across_ins, along_ins = by_axis(refs[counts[0] : counts[0] + n_in], counts)
    out_force, next_hbm, next_ref, spread, pieces, picks, seen_ref, coupled, spots, sems = refs[counts[0] + n_in :]
    depth, across, along = partial_ref.shape[1:]
    fold = spots.shape[0] // along
    half = across // fold
    wide = blocks * LANES
    bodies, cells, shares, lists, _ = blob_layout(across, blocks, pairs)
    even = parities()

    def ordered(arrived, axis):
        first = arrived[0][...]
        if len(arrived) == 1:
            return jnp.where(even[axis], 0.0, first), jnp.where(even[axis], first, 0.0)
        second = arrived[1][...]
        return jnp.where(even[axis], second, first), jnp.where(even[axis], first, second)

    across_low, across_high = ordered(across_ins, 1)
    across_low = diffuse * across_low
    across_high = diffuse * across_high
    edges = along_ins[0][...]
    if len(along_ins) > 1:
        edges = edges + along_ins[1][...]
    edges = diffuse * edges
    lanes = lax.broadcasted_iota(jnp.int32, (across, along), 1)
    subs = lax.broadcasted_iota(jnp.int32, (SUBLANES, along), 0)
    tail = across - SUBLANES
    rim = jnp.logical_or(lanes == 0, lanes == along - 1)
    copies = []
    for c in range(3):
        for h in range(depth):
            k = c * depth + h
            value = partial_ref[c, h]
            value += jnp.where(rim, pltpu.roll(edges, (along - 2 * k) % along, 1) if k else edges, 0.0)
            next_ref[c, h] = value
            next_ref[c, h, :SUBLANES, :] += jnp.where(subs == 0, across_low[k : k + 1, :], 0.0)
            next_ref[c, h, tail:, :] += jnp.where(subs == SUBLANES - 1, across_high[k : k + 1, :], 0.0)
        if depth > 2:
            inner = pl.ds(1, depth - 2)
            copies.append(pltpu.make_async_copy(next_ref.at[c, inner], next_hbm.at[c, inner], sems.at[c]))
            copies[-1].start()

    rows = lax.broadcasted_iota(jnp.int32, (across, LANES), 0)
    halves = lax.broadcasted_iota(jnp.int32, (half, LANES), 0)
    coupling = [[jnp.zeros((1, LANES), F32)] * blocks for _ in range(3)]
    for n, blob in enumerate(height_ins):
        own = sent[n]
        above = even[0] if n == 0 else jnp.logical_not(even[0])
        own_layer = jnp.where(above, depth - 1, 0)
        below = jnp.logical_not(above)
        for k in range(3):
            face = slice(k * across, (k + 1) * across)
            pieces[face, :] = parts_of(blob[face, :])
            pieces[(3 + k) * across : (4 + k) * across, :] = parts_of(own[face, :])
        lined = []
        for b in range(blocks):
            cell = jnp.where(above, own[cells + b : cells + b + 1, :], blob[cells + b : cells + b + 1, :])
            height, over, spot = places(cell.astype(jnp.int32), across, along)
            lined.append((height, over))
            mark_cells(picks, spots, b, over, spot, half, wide)
        seen_ref[...] = jnp.dot(pieces[...], picks[...], preferred_element_type=F32)
        for b in range(blocks):
            height, over = lined[b]
            share = jnp.where(above, own[shares + b : shares + b + 1, :], blob[shares + b : shares + b + 1, :])
            body = slice(bodies + 8 * b, bodies + 8 * b + 8)
            owner = jnp.where(above, own[body, :], blob[body, :])
            top = height == depth - 1
            mask = rows == over
            column = slice(b * LANES, (b + 1) * LANES)
            seen_share = jnp.where(top, jnp.where(above, share, 1.0 - share), 0.0)
            home_share = jnp.where(jnp.logical_and(top, below), share, 0.0)
            given_share = (-source_gain) * jnp.where(above, 1.0 - share, share)
            own_share = jnp.where(jnp.logical_and(top, below), 1.0, 0.0)
            ones = lane_one_hot(halves, jnp.where(over >= half, over - half, over))
            for c in range(3):
                seen = seen_ref[c * across : (c + 1) * across, column]
                home = seen_ref[(3 + c) * across : (4 + c) * across, column]
                met = jnp.where(mask, seen_share * seen + home_share * home, 0.0)
                met = jnp.sum(met, axis=0, keepdims=True)
                drag = drag_coef * owner[6:7] * (met - own_share * owner[3 + c : 4 + c])
                coupling[c][b] += jnp.where(above, drag, 0.0)
                for m, part in enumerate(split_parts(given_share * drag)):
                    coupled[c * half : (c + 1) * half, m * wide + b * LANES : m * wide + (b + 1) * LANES] = (
                        place_lines(ones, part, half)
                    )
        source = lax.dot_general(
            coupled[...], spots[...], (((1,), (1,)), ((), ())), preferred_element_type=F32
        )
        for c in range(3):
            given = [source[c * half : (c + 1) * half, f * along : (f + 1) * along] for f in range(fold)]
            next_ref[c, own_layer] += diffuse * blob[c * across : (c + 1) * across, :] + jnp.concatenate(given, axis=0)
    for n, h in enumerate(sorted({0, depth - 1})):
        copies.append(pltpu.make_async_copy(next_ref.at[:, h], next_hbm.at[:, h], sems.at[3 + n]))
        copies[-1].start()

    meetings, partners = [], []
    for n, blob in enumerate(height_ins):
        own = sent[n]
        above = even[0] if n == 0 else jnp.logical_not(even[0])
        for k in range(pairs):
            ours = [own[lists + 2 * k + side : lists + 2 * k + side + 1, :] for side in range(2)]
            theirs = [blob[lists + 2 * k + side : lists + 2 * k + side + 1, :] for side in range(2)]
            to = jnp.where(above, ours[0], theirs[1])
            by = jnp.where(above, ours[1], theirs[0])
            left = own[bodies : bodies + 8, :]
            right = blob[bodies : bodies + 8, :]
            for b in range(1, blocks):
                body = slice(bodies + 8 * b, bodies + 8 * b + 8)
                left = jnp.where(to == b, own[body, :], left)
                right = jnp.where(by == b, blob[body, :], right)
            meetings.append((to, left))
            partners.append(right)
    spread[...] = spread_blocks(partners)
    for i, (to, left) in enumerate(meetings):
        force, _ = pair_sum(left, spread, i * LANES, None)
        for b in range(blocks):
            for c in range(3):
                coupling[c][b] += jnp.where(to == b, force[c], 0.0)
    for b in range(blocks):
        for c in range(3):
            out_force[c, b : b + 1, :] = force_ref[c, b : b + 1, :] + coupling[c][b]
    for copy in copies:
        copy.wait()


def by_axis(refs, counts):
    groups, at = [], 0
    for n in counts:
        groups.append(refs[at : at + n])
        at += n
    return groups


def exchange(payloads, axis):
    count = lax.axis_size(axis)
    results = []
    for n, payload in enumerate(payloads):
        route = []
        for i in range(n, count - 1, 2):
            route += [(i, i + 1), (i + 1, i)]
        results.append(lax.ppermute(payload, axis, route))
    return results


def body(particles, local_pairs, cross_pairs, drag_cell, drag_share, fluid):
    blocks = particles.shape[0]
    pairs = cross_pairs.shape[0]
    listed = local_pairs.shape[0]
    _, depth, across, along = fluid.shape
    counts = [min(2, lax.axis_size(axis) - 1) for axis in AXES]
    fold = 2 if across % 32 == 0 else 1
    half = across // fold
    wide = PARTS * blocks * LANES
    rows = blob_layout(across, blocks, pairs)[-1]
    shapes = [(rows, along), (3 * depth, along), (across, along)]
    vmem = pl.BlockSpec(memory_space=pltpu.VMEM)
    hbm = pl.BlockSpec(memory_space=pl.ANY)

    def kept(value):
        return pltpu.with_memory_space_constraint(value, pltpu.VMEM)

    fluid_kept, pieces, picks, spots, spread, *packed = pl.pallas_call(
        functools.partial(pack_kernel, counts),
        out_shape=[
            pltpu.VMEM(fluid.shape, F32),
            pltpu.VMEM((3 * depth * across, PARTS * along), BF16),
            pltpu.VMEM((PARTS * along, blocks * LANES + along), BF16),
            pltpu.VMEM((fold * along, wide), BF16),
            pltpu.VMEM((blocks * LANES, 9 * LANES), F32),
        ]
        + [pltpu.VMEM(shape, F32) for shape, n in zip(shapes, counts) for _ in range(n)],
        in_specs=[hbm] * 5,
        out_specs=[vmem] * (5 + sum(counts)),
        scratch_shapes=[
            pltpu.SMEM(cross_pairs.shape, jnp.int32),
            pltpu.VMEM(particles.shape, F32),
            pltpu.VMEM(drag_cell.shape, jnp.int32),
            pltpu.VMEM(drag_share.shape, F32),
            pltpu.SemaphoreType.DMA((7,)),
        ],
        compiler_params=pltpu.CompilerParams(vmem_limit_bytes=GRANT),
        name="pack",
    )(cross_pairs, particles, drag_cell, drag_share, fluid)
    received = []
    for axis, payloads in zip(AXES, by_axis(packed, counts)):
        received += exchange(payloads, axis)

    force, partial = pl.pallas_call(
        functools.partial(local_kernel, blocks, pairs),
        out_shape=[pltpu.VMEM((3, blocks, LANES), F32), pltpu.VMEM(fluid.shape, F32)],
        in_specs=[hbm] + [vmem] * 6,
        out_specs=[vmem, vmem],
        scratch_shapes=[
            pltpu.VMEM((listed, LANES, LANES), F32),
            pltpu.VMEM((3 * depth * across, blocks * LANES + along), F32),
            pltpu.VMEM((2 * listed, SUBLANES, LANES), F32),
            pltpu.VMEM((3 * depth, blocks * LANES), F32),
            pltpu.VMEM((3 * depth * half, wide), BF16),
            pltpu.SMEM((2, listed), jnp.int32),
            pltpu.SemaphoreType.DMA,
        ],
        compiler_params=pltpu.CompilerParams(vmem_limit_bytes=GRANT),
        name="local",
    )(local_pairs.T, *[kept(value) for value in (packed[0], fluid_kept, pieces, picks, spots, spread)])

    out_force, out_next = pl.pallas_call(
        functools.partial(finish_kernel, counts, blocks, pairs),
        out_shape=[
            jax.ShapeDtypeStruct((3, blocks, LANES), F32),
            jax.ShapeDtypeStruct(fluid.shape, F32),
        ],
        in_specs=[vmem] * (2 + counts[0] + len(received)),
        out_specs=[vmem, hbm],
        scratch_shapes=[
            pltpu.VMEM(fluid.shape, F32),
            pltpu.VMEM((counts[0] * pairs * LANES, 9 * LANES), F32),
            pltpu.VMEM((6 * across, PARTS * along), BF16),
            pltpu.VMEM((PARTS * along, blocks * LANES), BF16),
            pltpu.VMEM((6 * across, blocks * LANES), F32),
            pltpu.VMEM((3 * half, wide), BF16),
            pltpu.VMEM((fold * along, wide), BF16),
            pltpu.SemaphoreType.DMA((5,)),
        ],
        compiler_params=pltpu.CompilerParams(vmem_limit_bytes=GRANT),
        name="finish",
    )(*[kept(value) for value in [force, partial, *packed[: counts[0]], *received]])
    return jnp.transpose(out_force, (1, 0, 2)), out_next


def solution(mesh):
    in_specs = (
        P(("gx", "gy", "gz"), None, None),
        P(("gx", "gy", "gz"), None),
        P(("gx", "gy", "gz"), None),
        P(("gx", "gy", "gz"), None),
        P(("gx", "gy", "gz"), None),
        P(None, "gx", "gy", "gz"),
    )
    out_specs = (P(("gx", "gy", "gz"), None, None), P(None, "gx", "gy", "gz"))
    return jax.shard_map(body, mesh=mesh, in_specs=in_specs, out_specs=out_specs, check_vma=False)
```

```python
import functools

import jax
import jax.numpy as jnp
from jax import lax
from jax.experimental import pallas as pl
from jax.experimental.pallas import tpu as pltpu
from jax.sharding import PartitionSpec as P

soft_core = 0.01
damp_normal = 0.3
damp_tangent = 0.2
drag_coef = 1.5
diffuse = 0.1
source_gain = 0.5

F32 = jnp.float32
BF16 = jnp.bfloat16
PARTS = 2
EXACT = 3
LANES = 128
SUBLANES = 8
GRANT = 32 * 1024 * 1024
AXES = ("gx", "gy", "gz")


def split_parts(value, count=PARTS):
    parts = []
    for _ in range(count):
        part = value.astype(BF16).astype(F32)
        parts.append(part)
        value = value - part
    return parts


def places(cell, across, along):
    layer = across * along
    if layer & (layer - 1) or along & (along - 1):
        return cell // layer, cell // along % across, cell % along
    shift = along.bit_length() - 1
    high = layer.bit_length() - 1
    return (
        lax.shift_right_logical(cell, high),
        lax.shift_right_logical(cell, shift) & (across - 1),
        cell & (along - 1),
    )


def parts_of(value):
    return jnp.concatenate([part.astype(BF16) for part in split_parts(value)], axis=1)


def spread_blocks(blocks):
    columns = []
    for block in blocks:
        rows = jnp.concatenate([block, block[7:8] * jnp.sqrt(block[6:7])], axis=0)
        parts = split_parts(rows, EXACT)
        parts.append(jnp.zeros((32 - 9 * EXACT, LANES), F32))
        columns.append(jnp.transpose(jnp.concatenate(parts, axis=0)).astype(BF16))
    lines = lax.broadcasted_iota(jnp.int32, (32, LANES), 0)
    picks = []
    for i in range(9):
        pick = lines == i
        for n in range(1, EXACT):
            pick = jnp.logical_or(pick, lines == i + 9 * n)
        picks.append(jnp.where(pick, 1.0, 0.0).astype(BF16))
    return jnp.dot(
        jnp.concatenate(columns, axis=0), jnp.concatenate(picks, axis=1), preferred_element_type=F32
    )


def pair_sum(left, spread, start, react):
    rows = [left[i : i + 1] for i in range(8)]
    rows.append((2.0 * damp_tangent) * rows[7] * jnp.sqrt(rows[6]))
    wide = [jnp.broadcast_to(row, (SUBLANES, LANES)) for row in rows]
    lanes = lax.broadcasted_iota(jnp.int32, (SUBLANES, LANES), 1)
    total = [None] * 3
    for tile in range(LANES // SUBLANES):
        place = pl.ds(pl.multiple_of(start + tile * SUBLANES, SUBLANES), SUBLANES)
        there = [spread[place, i * LANES : (i + 1) * LANES] for i in range(9)]
        ex, ey, ez, wx, wy, wz = [wide[i] - there[i] for i in range(6)]
        square = (ex * ex + ey * ey) + (ez * ez + soft_core)
        inverse = lax.rsqrt(square)
        reach = wide[6] + there[6]
        delta = jnp.maximum(reach - square * inverse, 0.0)
        mass = wide[7] + there[7]
        under = jnp.maximum((delta * reach) * (mass * mass), 1e-30)
        tangent = (wide[8] * there[8]) * (delta * lax.rsqrt(under))
        speed = ((wx * ex + wy * ey) + wz * ez) * inverse
        along = (
            (2.0 / 3.0 / damp_tangent) * delta - ((damp_normal - damp_tangent) / damp_tangent) * speed
        ) * (tangent * inverse)
        column = None
        for d, (e, w) in enumerate(((ex, wx), (ey, wy), (ez, wz))):
            force = along * e - tangent * w
            total[d] = force if total[d] is None else total[d] + force
            if react is not None:
                across_sum = jnp.broadcast_to(jnp.sum(force, axis=1, keepdims=True), (SUBLANES, LANES))
                column = across_sum if column is None else jnp.where(lanes == d, across_sum, column)
        if react is not None:
            react[tile * SUBLANES : (tile + 1) * SUBLANES, :] = column
    total = [jnp.sum(item, axis=0, keepdims=True) for item in total]
    if react is None:
        return total, None
    turned = jnp.transpose(react[...])
    return total, [-turned[d : d + 1] for d in range(3)]


def blob_layout(across, blocks, pairs):
    bodies = 3 * across
    cells = bodies + 8 * blocks
    shares = cells + blocks
    lists = shares + blocks
    rows = lists + 2 * pairs
    return bodies, cells, shares, lists, rows + -rows % 8


def parities():
    return [lax.rem(lax.axis_index(axis), 2) == 0 for axis in AXES]


def pack_kernel(counts, list_hbm, pair_hbm, part_hbm, cell_hbm, share_hbm, fluid_hbm, *refs):
    n_out = 6 + sum(counts)
    list_ref, fluid_ref, pieces, picks, spots, spread = refs[:6]
    height_outs, across_outs, along_outs = by_axis(refs[6:n_out], counts)
    pair_ref, part_ref, cell_ref, share_ref, sems = refs[n_out:]
    depth, across, along = fluid_ref.shape[1:]
    blocks, pairs = part_ref.shape[0], pair_ref.shape[0]
    fold = spots.shape[0] // along
    half = across // fold
    wide = blocks * LANES
    bodies, cells, shares, lists, rows = blob_layout(across, blocks, pairs)
    small = [(part_hbm, part_ref), (cell_hbm, cell_ref), (share_hbm, share_ref), (pair_hbm, pair_ref), (list_hbm, list_ref)]
    small = [pltpu.make_async_copy(source, target, sems.at[3 + n]) for n, (source, target) in enumerate(small)]
    copies = [pltpu.make_async_copy(fluid_hbm.at[c], fluid_ref.at[c], sems.at[c]) for c in range(3)]
    for copy in small + copies:
        copy.start()
    even = parities()
    for copy in small:
        copy.wait()
    for n, out in enumerate(height_outs):
        for b in range(blocks):
            out[bodies + 8 * b : bodies + 8 * b + 8, :] = part_ref[b]
        out[cells:shares, :] = cell_ref[...].astype(F32)
        out[shares:lists, :] = share_ref[...]
        for k in range(pairs):
            for side in range(2):
                row = lists + 2 * k + side
                out[row : row + 1, :] = jnp.full((1, LANES), pair_ref[k, side], jnp.int32).astype(F32)
        used = lists + 2 * pairs
        if used < rows:
            out[used:rows, :] = jnp.zeros((rows - used, LANES), F32)
    spread[...] = spread_blocks([part_ref[b] for b in range(blocks)])
    for b in range(blocks):
        _, over, spot = places(cell_ref[b : b + 1, :], across, along)
        mark_cells(picks, spots, b, over, spot, half, wide)
    sites = lax.broadcasted_iota(jnp.int32, (along, along), 0)
    lanes = lax.broadcasted_iota(jnp.int32, (along, along), 1)
    near = jnp.where(jnp.abs(sites - lanes) == 1, 1.0, 0.0).astype(BF16)
    for n in range(PARTS):
        picks[n * along : (n + 1) * along, wide : wide + along] = near

    lanes = lax.broadcasted_iota(jnp.int32, (across, along), 1)
    first = jnp.zeros((across, along), F32)
    last = jnp.zeros((across, along), F32)
    for c in range(3):
        copies[c].wait()
        for n, out in enumerate(height_outs):
            upward = even[0] if n == 0 else jnp.logical_not(even[0])
            out[c * across : (c + 1) * across, :] = fluid_ref[c, jnp.where(upward, depth - 1, 0)]
        for h in range(depth):
            k = c * depth + h
            here = fluid_ref[c, h]
            for n, out in enumerate(across_outs):
                upward = even[1] if n == 0 else jnp.logical_not(even[1])
                out[k : k + 1, :] = jnp.where(upward, here[across - 1 : across], here[0:1])
            turned = pltpu.roll(here, 2 * k, 1) if k else here
            first = jnp.where(lanes == 2 * k, turned, first)
            last = jnp.where(lanes == (2 * k - 1) % along, turned, last)
            pieces[k * across : (k + 1) * across, :] = parts_of(here)
    first = pltpu.roll(first, along - 1, 1)
    last = pltpu.roll(last, 1, 1)
    for n, out in enumerate(along_outs):
        upward = even[2] if n == 0 else jnp.logical_not(even[2])
        out[...] = jnp.where(upward, last, first)


def mark_cells(picks, spots, b, over, spot, half, wide):
    along = picks.shape[0] // PARTS
    sites = lax.broadcasted_iota(jnp.int32, (spots.shape[0], LANES), 0)
    one_hot = lane_one_hot(sites[:along], spot)
    for n in range(PARTS):
        picks[n * along : (n + 1) * along, b * LANES : (b + 1) * LANES] = one_hot
    one_hot = lane_one_hot(sites, jnp.where(over >= half, along, 0) + spot)
    for n in range(PARTS):
        spots[:, n * wide + b * LANES : n * wide + (b + 1) * LANES] = one_hot


def lane_one_hot(sites, target):
    return jnp.where(sites == target, 1.0, 0.0).astype(BF16)


def place_lines(ones, part, half):
    line = jnp.broadcast_to(part, (16, LANES)).astype(BF16)
    line = jnp.concatenate([line] * (half // 16), axis=0)
    return jnp.where(ones > 0, line, jnp.zeros_like(line))


def local_kernel(
    blocks, pairs, pair_ref, blob_ref, fluid_ref, pieces, picks, spots, spread, force_ref, next_ref, source_ref,
    react, seen_ref, found, weights, coupled,
):
    depth, across, along = fluid_ref.shape[1:]
    listed = pair_ref.shape[1]
    fold = spots.shape[0] // along
    half = across // fold
    wide = blocks * LANES
    bodies, cells, shares, _, _ = blob_layout(across, blocks, pairs)
    rows = lax.broadcasted_iota(jnp.int32, (across, LANES), 0)
    halves = lax.broadcasted_iota(jnp.int32, (half, LANES), 0)
    subs = lax.broadcasted_iota(jnp.int32, (SUBLANES, along), 0)
    slabs = [(c, h) for c in range(3) for h in range(depth)]

    def body_of(b):
        return blob_ref[bodies + 8 * b : bodies + 8 * b + 8, :]

    def spot_of(b):
        return places(blob_ref[cells + b : cells + b + 1, :].astype(jnp.int32), across, along)

    def stencil(c, h):
        for t in range(across // SUBLANES):
            at = t * SUBLANES
            here = fluid_ref[c, h, at : at + SUBLANES, :]
            if t > 0:
                beside = fluid_ref[c, h, at - 1 : at + SUBLANES - 1, :]
            else:
                beside = jnp.where(subs == 0, 0.0, pltpu.roll(here, 1, 0))
            if at + SUBLANES < across:
                beside += fluid_ref[c, h, at + 1 : at + SUBLANES + 1, :]
            else:
                beside += jnp.where(subs == SUBLANES - 1, 0.0, pltpu.roll(here, SUBLANES - 1, 0))
            line = (c * depth + h) * across + at
            beside += seen_ref[line : line + SUBLANES, wide : wide + along]
            if h > 0:
                beside += fluid_ref[c, h - 1, at : at + SUBLANES, :]
            if h < depth - 1:
                beside += fluid_ref[c, h + 1, at : at + SUBLANES, :]
            next_ref[c, h, at : at + SUBLANES, :] = (1.0 - 6.0 * diffuse) * here + diffuse * beside

    seen_ref[...] = jnp.dot(pieces[...], picks[...], preferred_element_type=F32)

    turns = blocks + listed
    share_out = [slabs[i * len(slabs) // turns : (i + 1) * len(slabs) // turns] for i in range(turns)]
    for b in range(blocks):
        for c, h in share_out[b]:
            stencil(c, h)
        force, _ = pair_sum(body_of(b), spread, b * LANES, None)
        for c in range(3):
            force_ref[c, b : b + 1, :] = force[c]

    for b in range(blocks):
        height, over, _ = spot_of(b)
        share = blob_ref[shares + b : shares + b + 1, :]
        mask = rows == over
        column = slice(b * LANES, (b + 1) * LANES)
        near = [
            jnp.where(height == h, 1.0 - share, jnp.where(height == h - 1, share, 0.0)) for h in range(depth)
        ]
        for c in range(3):
            total = jnp.zeros((SUBLANES, LANES), F32)
            for h in range(depth):
                k = c * depth + h
                seen = jnp.where(mask, seen_ref[k * across : (k + 1) * across, column], 0.0)
                total += near[h] * jnp.sum(seen.reshape(across // SUBLANES, SUBLANES, LANES), axis=0)
            met = jnp.sum(total, axis=0, keepdims=True)
            drag = drag_coef * blob_ref[bodies + 8 * b + 6 : bodies + 8 * b + 7, :] * (
                met - blob_ref[bodies + 8 * b + 3 + c : bodies + 8 * b + 4 + c, :]
            )
            force_ref[c, b : b + 1, :] += drag
            for h in range(depth):
                weights[c * depth + h : c * depth + h + 1, column] = (-source_gain) * near[h] * drag
        ones = lane_one_hot(halves, jnp.where(over >= half, over - half, over))
        for n, part in enumerate(split_parts(weights[:, column])):
            for k in range(3 * depth):
                coupled[k * half : (k + 1) * half, n * wide + b * LANES : n * wide + (b + 1) * LANES] = place_lines(
                    ones, part[k : k + 1], half
                )
    for c in range(3):
        face = slice(c * depth * half, (c + 1) * depth * half)
        source_ref[face, :] = lax.dot_general(
            coupled[face, :], spots[...], (((1,), (1,)), ((), ())), preferred_element_type=F32
        )

    for i in range(listed):
        for c, h in share_out[blocks + i]:
            stencil(c, h)
        a, c = pair_ref[0, i], pair_ref[1, i]
        left = blob_ref[pl.ds(pl.multiple_of(bodies + 8 * a, 8), 8), :]
        ahead, behind = pair_sum(left, spread, c * LANES, react.at[i])
        for side, forces in enumerate((ahead, behind)):
            for d in range(3):
                found[2 * i + side, d : d + 1, :] = forces[d]
    for b in range(blocks):
        for d in range(3):
            total = force_ref[d, b : b + 1, :]
            for i in range(listed):
                for side in range(2):
                    total += jnp.where(pair_ref[side, i] == b, found[2 * i + side, d : d + 1, :], 0.0)
            force_ref[d, b : b + 1, :] = total


def finish_kernel(counts, blocks, pairs, force_ref, partial_ref, source_ref, *refs):
    n_in = sum(counts)
    sent = refs[: counts[0]]
    height_ins, across_ins, along_ins = by_axis(refs[counts[0] : counts[0] + n_in], counts)
    out_force, next_hbm, next_ref, spread, pieces, picks, seen_ref, coupled, spots, sems = refs[counts[0] + n_in :]
    depth, across, along = partial_ref.shape[1:]
    fold = spots.shape[0] // along
    half = across // fold
    wide = blocks * LANES
    bodies, cells, shares, lists, _ = blob_layout(across, blocks, pairs)
    even = parities()

    def ordered(arrived, axis):
        first = arrived[0][...]
        if len(arrived) == 1:
            return jnp.where(even[axis], 0.0, first), jnp.where(even[axis], first, 0.0)
        second = arrived[1][...]
        return jnp.where(even[axis], second, first), jnp.where(even[axis], first, second)

    across_low, across_high = ordered(across_ins, 1)
    across_low = diffuse * across_low
    across_high = diffuse * across_high
    edges = along_ins[0][...]
    if len(along_ins) > 1:
        edges = edges + along_ins[1][...]
    edges = diffuse * edges
    lanes = lax.broadcasted_iota(jnp.int32, (across, along), 1)
    subs = lax.broadcasted_iota(jnp.int32, (SUBLANES, along), 0)
    tail = across - SUBLANES
    rim = jnp.logical_or(lanes == 0, lanes == along - 1)
    copies = []
    for c in range(3):
        for h in range(depth):
            k = c * depth + h
            given = [
                source_ref[k * half : (k + 1) * half, f * along : (f + 1) * along] for f in range(fold)
            ]
            value = partial_ref[c, h] + jnp.concatenate(given, axis=0)
            value += jnp.where(rim, pltpu.roll(edges, (along - 2 * k) % along, 1) if k else edges, 0.0)
            next_ref[c, h] = value
            next_ref[c, h, :SUBLANES, :] += jnp.where(subs == 0, across_low[k : k + 1, :], 0.0)
            next_ref[c, h, tail:, :] += jnp.where(subs == SUBLANES - 1, across_high[k : k + 1, :], 0.0)
        if depth > 2:
            inner = pl.ds(1, depth - 2)
            copies.append(pltpu.make_async_copy(next_ref.at[c, inner], next_hbm.at[c, inner], sems.at[c]))
            copies[-1].start()

    rows = lax.broadcasted_iota(jnp.int32, (across, LANES), 0)
    halves = lax.broadcasted_iota(jnp.int32, (half, LANES), 0)
    coupling = [[jnp.zeros((1, LANES), F32)] * blocks for _ in range(3)]
    for n, blob in enumerate(height_ins):
        own = sent[n]
        above = even[0] if n == 0 else jnp.logical_not(even[0])
        own_layer = jnp.where(above, depth - 1, 0)
        below = jnp.logical_not(above)
        for k in range(3):
            face = slice(k * across, (k + 1) * across)
            pieces[face, :] = parts_of(blob[face, :])
            pieces[(3 + k) * across : (4 + k) * across, :] = parts_of(own[face, :])
        lined = []
        for b in range(blocks):
            cell = jnp.where(above, own[cells + b : cells + b + 1, :], blob[cells + b : cells + b + 1, :])
            height, over, spot = places(cell.astype(jnp.int32), across, along)
            lined.append((height, over))
            mark_cells(picks, spots, b, over, spot, half, wide)
        seen_ref[...] = jnp.dot(pieces[...], picks[...], preferred_element_type=F32)
        for b in range(blocks):
            height, over = lined[b]
            share = jnp.where(above, own[shares + b : shares + b + 1, :], blob[shares + b : shares + b + 1, :])
            body = slice(bodies + 8 * b, bodies + 8 * b + 8)
            owner = jnp.where(above, own[body, :], blob[body, :])
            top = height == depth - 1
            mask = rows == over
            column = slice(b * LANES, (b + 1) * LANES)
            seen_share = jnp.where(top, jnp.where(above, share, 1.0 - share), 0.0)
            home_share = jnp.where(jnp.logical_and(top, below), share, 0.0)
            given_share = (-source_gain) * jnp.where(above, 1.0 - share, share)
            own_share = jnp.where(jnp.logical_and(top, below), 1.0, 0.0)
            ones = lane_one_hot(halves, jnp.where(over >= half, over - half, over))
            for c in range(3):
                seen = seen_ref[c * across : (c + 1) * across, column]
                home = seen_ref[(3 + c) * across : (4 + c) * across, column]
                met = jnp.where(mask, seen_share * seen + home_share * home, 0.0)
                met = jnp.sum(met, axis=0, keepdims=True)
                drag = drag_coef * owner[6:7] * (met - own_share * owner[3 + c : 4 + c])
                coupling[c][b] += jnp.where(above, drag, 0.0)
                for m, part in enumerate(split_parts(given_share * drag)):
                    coupled[c * half : (c + 1) * half, m * wide + b * LANES : m * wide + (b + 1) * LANES] = (
                        place_lines(ones, part, half)
                    )
        source = lax.dot_general(
            coupled[...], spots[...], (((1,), (1,)), ((), ())), preferred_element_type=F32
        )
        for c in range(3):
            given = [source[c * half : (c + 1) * half, f * along : (f + 1) * along] for f in range(fold)]
            next_ref[c, own_layer] += diffuse * blob[c * across : (c + 1) * across, :] + jnp.concatenate(given, axis=0)
    for n, h in enumerate(sorted({0, depth - 1})):
        copies.append(pltpu.make_async_copy(next_ref.at[:, h], next_hbm.at[:, h], sems.at[3 + n]))
        copies[-1].start()

    meetings, partners = [], []
    for n, blob in enumerate(height_ins):
        own = sent[n]
        above = even[0] if n == 0 else jnp.logical_not(even[0])
        for k in range(pairs):
            ours = [own[lists + 2 * k + side : lists + 2 * k + side + 1, :] for side in range(2)]
            theirs = [blob[lists + 2 * k + side : lists + 2 * k + side + 1, :] for side in range(2)]
            to = jnp.where(above, ours[0], theirs[1])
            by = jnp.where(above, ours[1], theirs[0])
            left = own[bodies : bodies + 8, :]
            right = blob[bodies : bodies + 8, :]
            for b in range(1, blocks):
                body = slice(bodies + 8 * b, bodies + 8 * b + 8)
                left = jnp.where(to == b, own[body, :], left)
                right = jnp.where(by == b, blob[body, :], right)
            meetings.append((to, left))
            partners.append(right)
    spread[...] = spread_blocks(partners)
    for i, (to, left) in enumerate(meetings):
        force, _ = pair_sum(left, spread, i * LANES, None)
        for b in range(blocks):
            for c in range(3):
                coupling[c][b] += jnp.where(to == b, force[c], 0.0)
    for b in range(blocks):
        for c in range(3):
            out_force[c, b : b + 1, :] = force_ref[c, b : b + 1, :] + coupling[c][b]
    for copy in copies:
        copy.wait()


def by_axis(refs, counts):
    groups, at = [], 0
    for n in counts:
        groups.append(refs[at : at + n])
        at += n
    return groups


def exchange(payloads, axis):
    count = lax.axis_size(axis)
    results = []
    for n, payload in enumerate(payloads):
        route = []
        for i in range(n, count - 1, 2):
            route += [(i, i + 1), (i + 1, i)]
        results.append(lax.ppermute(payload, axis, route))
    return results


def body(particles, local_pairs, cross_pairs, drag_cell, drag_share, fluid):
    blocks = particles.shape[0]
    pairs = cross_pairs.shape[0]
    listed = local_pairs.shape[0]
    _, depth, across, along = fluid.shape
    counts = [min(2, lax.axis_size(axis) - 1) for axis in AXES]
    fold = 2 if across % 32 == 0 else 1
    half = across // fold
    wide = PARTS * blocks * LANES
    rows = blob_layout(across, blocks, pairs)[-1]
    shapes = [(rows, along), (3 * depth, along), (across, along)]
    vmem = pl.BlockSpec(memory_space=pltpu.VMEM)
    hbm = pl.BlockSpec(memory_space=pltpu.HBM)
    smem = pl.BlockSpec(memory_space=pltpu.SMEM)

    def kept(value):
        return pltpu.with_memory_space_constraint(value, pltpu.VMEM)

    listing, fluid_kept, pieces, picks, spots, spread, *packed = pl.pallas_call(
        functools.partial(pack_kernel, counts),
        out_shape=[
            pltpu.SMEM((2, listed), jnp.int32),
            pltpu.VMEM(fluid.shape, F32),
            pltpu.VMEM((3 * depth * across, PARTS * along), BF16),
            pltpu.VMEM((PARTS * along, blocks * LANES + along), BF16),
            pltpu.VMEM((fold * along, wide), BF16),
            pltpu.VMEM((blocks * LANES, 9 * LANES), F32),
        ]
        + [pltpu.VMEM(shape, F32) for shape, n in zip(shapes, counts) for _ in range(n)],
        in_specs=[hbm] * 6,
        out_specs=[smem] + [vmem] * (5 + sum(counts)),
        scratch_shapes=[
            pltpu.SMEM(cross_pairs.shape, jnp.int32),
            pltpu.VMEM(particles.shape, F32),
            pltpu.VMEM(drag_cell.shape, jnp.int32),
            pltpu.VMEM(drag_share.shape, F32),
            pltpu.SemaphoreType.DMA((8,)),
        ],
        compiler_params=pltpu.CompilerParams(vmem_limit_bytes=GRANT),
        name="pack",
    )(
        *[
            pltpu.with_memory_space_constraint(value, pltpu.HBM)
            for value in (local_pairs.T, cross_pairs, particles, drag_cell, drag_share, fluid)
        ]
    )
    received = []
    for axis, payloads in zip(AXES, by_axis(packed, counts)):
        received += exchange(payloads, axis)

    force, partial, source = pl.pallas_call(
        functools.partial(local_kernel, blocks, pairs),
        out_shape=[
            pltpu.VMEM((3, blocks, LANES), F32),
            pltpu.VMEM(fluid.shape, F32),
            pltpu.VMEM((3 * depth * half, fold * along), F32),
        ],
        in_specs=[smem] + [vmem] * 6,
        out_specs=[vmem] * 3,
        scratch_shapes=[
            pltpu.VMEM((listed, LANES, LANES), F32),
            pltpu.VMEM((3 * depth * across, blocks * LANES + along), F32),
            pltpu.VMEM((2 * listed, SUBLANES, LANES), F32),
            pltpu.VMEM((3 * depth, blocks * LANES), F32),
            pltpu.VMEM((3 * depth * half, wide), BF16),
        ],
        compiler_params=pltpu.CompilerParams(vmem_limit_bytes=GRANT),
        name="local",
    )(
        pltpu.with_memory_space_constraint(listing, pltpu.SMEM),
        *[kept(value) for value in (packed[0], fluid_kept, pieces, picks, spots, spread)],
    )

    out_force, out_next = pl.pallas_call(
        functools.partial(finish_kernel, counts, blocks, pairs),
        out_shape=[
            jax.ShapeDtypeStruct((3, blocks, LANES), F32),
            jax.ShapeDtypeStruct(fluid.shape, F32),
        ],
        in_specs=[vmem] * (3 + counts[0] + len(received)),
        out_specs=[vmem, hbm],
        scratch_shapes=[
            pltpu.VMEM(fluid.shape, F32),
            pltpu.VMEM((counts[0] * pairs * LANES, 9 * LANES), F32),
            pltpu.VMEM((6 * across, PARTS * along), BF16),
            pltpu.VMEM((PARTS * along, blocks * LANES), BF16),
            pltpu.VMEM((6 * across, blocks * LANES), F32),
            pltpu.VMEM((3 * half, wide), BF16),
            pltpu.VMEM((fold * along, wide), BF16),
            pltpu.SemaphoreType.DMA((5,)),
        ],
        compiler_params=pltpu.CompilerParams(vmem_limit_bytes=GRANT),
        name="finish",
    )(*[kept(value) for value in [force, partial, source, *packed[: counts[0]], *received]])
    return jnp.transpose(out_force, (1, 0, 2)), out_next


def solution(mesh):
    in_specs = (
        P(("gx", "gy", "gz"), None, None),
        P(("gx", "gy", "gz"), None),
        P(("gx", "gy", "gz"), None),
        P(("gx", "gy", "gz"), None),
        P(("gx", "gy", "gz"), None),
        P(None, "gx", "gy", "gz"),
    )
    out_specs = (P(("gx", "gy", "gz"), None, None), P(None, "gx", "gy", "gz"))
    return jax.shard_map(body, mesh=mesh, in_specs=in_specs, out_specs=out_specs, check_vma=False)
```

```python
import functools

import jax
import jax.numpy as jnp
from jax import lax
from jax.experimental import pallas as pl
from jax.experimental.pallas import tpu as pltpu
from jax.sharding import PartitionSpec as P


soft_core = 0.01
damp_normal = 0.3
damp_tangent = 0.2
drag_coef = 1.5
diffuse = 0.1
source_gain = 0.5

F32 = jnp.float32
BF16 = jnp.bfloat16
PARTS = 2
EXACT = 3
LANES = 128
SUBLANES = 8
GRANT = 32 * 1024 * 1024
AXES = ("gx", "gy", "gz")


def split_parts(value, count=PARTS):
    parts = []
    for _ in range(count):
        part = value.astype(BF16).astype(F32)
        parts.append(part)
        value = value - part
    return parts


def places(cell, across, along):
    layer = across * along
    if layer & (layer - 1) or along & (along - 1):
        return cell // layer, cell // along % across, cell % along
    shift = along.bit_length() - 1
    high = layer.bit_length() - 1
    return (
        lax.shift_right_logical(cell, high),
        lax.shift_right_logical(cell, shift) & (across - 1),
        cell & (along - 1),
    )


def parts_of(value):
    return jnp.concatenate([part.astype(BF16) for part in split_parts(value)], axis=1)


def spread_blocks(blocks):
    columns = []
    for block in blocks:
        rows = jnp.concatenate([block, block[7:8] * jnp.sqrt(block[6:7])], axis=0)
        parts = split_parts(rows, EXACT)
        parts.append(jnp.zeros((32 - 9 * EXACT, LANES), F32))
        columns.append(jnp.transpose(jnp.concatenate(parts, axis=0)).astype(BF16))
    lines = lax.broadcasted_iota(jnp.int32, (32, LANES), 0)
    picks = []
    for i in range(9):
        pick = lines == i
        for n in range(1, EXACT):
            pick = jnp.logical_or(pick, lines == i + 9 * n)
        picks.append(jnp.where(pick, 1.0, 0.0).astype(BF16))
    return jnp.dot(
        jnp.concatenate(columns, axis=0), jnp.concatenate(picks, axis=1), preferred_element_type=F32
    )


def pair_sum(left, spread, start, react):
    rows = [left[i : i + 1] for i in range(8)]
    rows.append((2.0 * damp_tangent) * rows[7] * jnp.sqrt(rows[6]))
    wide = [jnp.broadcast_to(row, (SUBLANES, LANES)) for row in rows]
    lanes = lax.broadcasted_iota(jnp.int32, (SUBLANES, LANES), 1)
    total = [None] * 3
    for tile in range(LANES // SUBLANES):
        place = pl.ds(pl.multiple_of(start + tile * SUBLANES, SUBLANES), SUBLANES)
        there = [spread[place, i * LANES : (i + 1) * LANES] for i in range(9)]
        ex, ey, ez, wx, wy, wz = [wide[i] - there[i] for i in range(6)]
        square = (ex * ex + ey * ey) + (ez * ez + soft_core)
        inverse = lax.rsqrt(square)
        reach = wide[6] + there[6]
        delta = jnp.maximum(reach - square * inverse, 0.0)
        mass = wide[7] + there[7]
        under = jnp.maximum((delta * reach) * (mass * mass), 1e-30)
        tangent = (wide[8] * there[8]) * (delta * lax.rsqrt(under))
        speed = ((wx * ex + wy * ey) + wz * ez) * inverse
        along = (
            (2.0 / 3.0 / damp_tangent) * delta - ((damp_normal - damp_tangent) / damp_tangent) * speed
        ) * (tangent * inverse)
        column = None
        for d, (e, w) in enumerate(((ex, wx), (ey, wy), (ez, wz))):
            force = along * e - tangent * w
            total[d] = force if total[d] is None else total[d] + force
            if react is not None:
                across_sum = jnp.broadcast_to(jnp.sum(force, axis=1, keepdims=True), (SUBLANES, LANES))
                column = across_sum if column is None else jnp.where(lanes == d, across_sum, column)
        if react is not None:
            react[tile * SUBLANES : (tile + 1) * SUBLANES, :] = column
    total = [jnp.sum(item, axis=0, keepdims=True) for item in total]
    if react is None:
        return total, None
    turned = jnp.transpose(react[...])
    return total, [-turned[d : d + 1] for d in range(3)]


def blob_layout(across, blocks, pairs):
    bodies = 3 * across
    cells = bodies + 8 * blocks
    shares = cells + blocks
    lists = shares + blocks
    rows = lists + 2 * pairs
    return bodies, cells, shares, lists, rows + -rows % 8


def parities():
    return [lax.rem(lax.axis_index(axis), 2) == 0 for axis in AXES]


def pack_kernel(counts, list_hbm, pair_hbm, part_hbm, cell_hbm, share_hbm, fluid_hbm, *refs):
    n_out = 6 + sum(counts)
    list_ref, fluid_ref, pieces, picks, spots, spread = refs[:6]
    height_outs, across_outs, along_outs = by_axis(refs[6:n_out], counts)
    pair_ref, part_ref, cell_ref, share_ref, sems = refs[n_out:]
    depth, across, along = fluid_ref.shape[1:]
    blocks, pairs = part_ref.shape[0], pair_ref.shape[0]
    fold = spots.shape[0] // along
    half = across // fold
    wide = blocks * LANES
    bodies, cells, shares, lists, rows = blob_layout(across, blocks, pairs)
    small = [(part_hbm, part_ref), (cell_hbm, cell_ref), (share_hbm, share_ref), (pair_hbm, pair_ref), (list_hbm, list_ref)]
    small = [pltpu.make_async_copy(source, target, sems.at[3 + n]) for n, (source, target) in enumerate(small)]
    copies = [pltpu.make_async_copy(fluid_hbm.at[c], fluid_ref.at[c], sems.at[c]) for c in range(3)]
    for copy in small + copies:
        copy.start()
    even = parities()
    for copy in small + copies:
        copy.wait()
    for out in height_outs:
        for b in range(blocks):
            out[bodies + 8 * b : bodies + 8 * b + 8, :] = part_ref[b]
        out[cells:shares, :] = cell_ref[...].astype(F32)
        out[shares:lists, :] = share_ref[...]
        for k in range(pairs):
            for side in range(2):
                row = lists + 2 * k + side
                out[row : row + 1, :] = jnp.full((1, LANES), pair_ref[k, side], jnp.int32).astype(F32)
        used = lists + 2 * pairs
        if used < rows:
            out[used:rows, :] = jnp.zeros((rows - used, LANES), F32)
    spread[...] = spread_blocks([part_ref[b] for b in range(blocks)])
    for b in range(blocks):
        _, over, spot = places(cell_ref[b : b + 1, :], across, along)
        mark_cells(picks, spots, b, over, spot, half, wide)
    sites = lax.broadcasted_iota(jnp.int32, (along, along), 0)
    lanes = lax.broadcasted_iota(jnp.int32, (along, along), 1)
    near = jnp.where(jnp.abs(sites - lanes) == 1, 1.0, 0.0).astype(BF16)
    for n in range(PARTS):
        picks[n * along : (n + 1) * along, wide : wide + along] = near

    lanes = lax.broadcasted_iota(jnp.int32, (across, along), 1)
    first = jnp.zeros((across, along), F32)
    last = jnp.zeros((across, along), F32)
    for c in range(3):
        for n, out in enumerate(height_outs):
            upward = even[0] if n == 0 else jnp.logical_not(even[0])
            out[c * across : (c + 1) * across, :] = fluid_ref[c, jnp.where(upward, depth - 1, 0)]
        for h in range(depth):
            k = c * depth + h
            here = fluid_ref[c, h]
            for n, out in enumerate(across_outs):
                upward = even[1] if n == 0 else jnp.logical_not(even[1])
                out[k : k + 1, :] = jnp.where(upward, here[across - 1 : across], here[0:1])
            turned = pltpu.roll(here, 2 * k, 1) if k else here
            first = jnp.where(lanes == 2 * k, turned, first)
            last = jnp.where(lanes == (2 * k - 1) % along, turned, last)
            pieces[k * across : (k + 1) * across, :] = parts_of(here)
    first = pltpu.roll(first, along - 1, 1)
    last = pltpu.roll(last, 1, 1)
    for n, out in enumerate(along_outs):
        upward = even[2] if n == 0 else jnp.logical_not(even[2])
        out[...] = jnp.where(upward, last, first)


def mark_cells(picks, spots, b, over, spot, half, wide):
    along = picks.shape[0] // PARTS
    sites = lax.broadcasted_iota(jnp.int32, (spots.shape[0], LANES), 0)
    one_hot = lane_one_hot(sites[:along], spot)
    for n in range(PARTS):
        picks[n * along : (n + 1) * along, b * LANES : (b + 1) * LANES] = one_hot
    one_hot = lane_one_hot(sites, jnp.where(over >= half, along, 0) + spot)
    for n in range(PARTS):
        spots[:, n * wide + b * LANES : n * wide + (b + 1) * LANES] = one_hot


def lane_one_hot(sites, target):
    return jnp.where(sites == target, 1.0, 0.0).astype(BF16)


def place_lines(ones, part, half):
    line = jnp.broadcast_to(part, (16, LANES)).astype(BF16)
    line = jnp.concatenate([line] * (half // 16), axis=0)
    return jnp.where(ones > 0, line, jnp.zeros_like(line))


def local_kernel(
    blocks, pairs, pair_ref, blob_ref, fluid_ref, pieces, picks, spots, spread, force_ref, next_ref, source_ref,
    react, seen_ref, found, weights, coupled,
):
    depth, across, along = fluid_ref.shape[1:]
    listed = pair_ref.shape[1]
    fold = spots.shape[0] // along
    half = across // fold
    wide = blocks * LANES
    bodies, cells, shares, _, _ = blob_layout(across, blocks, pairs)
    rows = lax.broadcasted_iota(jnp.int32, (across, LANES), 0)
    halves = lax.broadcasted_iota(jnp.int32, (half, LANES), 0)
    subs = lax.broadcasted_iota(jnp.int32, (SUBLANES, along), 0)
    slabs = [(c, h) for c in range(3) for h in range(depth)]

    def body_of(b):
        return blob_ref[bodies + 8 * b : bodies + 8 * b + 8, :]

    def spot_of(b):
        return places(blob_ref[cells + b : cells + b + 1, :].astype(jnp.int32), across, along)

    def stencil(c, h):
        for t in range(across // SUBLANES):
            at = t * SUBLANES
            here = fluid_ref[c, h, at : at + SUBLANES, :]
            if t > 0:
                beside = fluid_ref[c, h, at - 1 : at + SUBLANES - 1, :]
            else:
                beside = jnp.where(subs == 0, 0.0, pltpu.roll(here, 1, 0))
            if at + SUBLANES < across:
                beside += fluid_ref[c, h, at + 1 : at + SUBLANES + 1, :]
            else:
                beside += jnp.where(subs == SUBLANES - 1, 0.0, pltpu.roll(here, SUBLANES - 1, 0))
            line = (c * depth + h) * across + at
            beside += seen_ref[line : line + SUBLANES, wide : wide + along]
            if h > 0:
                beside += fluid_ref[c, h - 1, at : at + SUBLANES, :]
            if h < depth - 1:
                beside += fluid_ref[c, h + 1, at : at + SUBLANES, :]
            next_ref[c, h, at : at + SUBLANES, :] = (1.0 - 6.0 * diffuse) * here + diffuse * beside

    seen_ref[...] = jnp.dot(pieces[...], picks[...], preferred_element_type=F32)

    turns = blocks + listed
    share_out = [slabs[i * len(slabs) // turns : (i + 1) * len(slabs) // turns] for i in range(turns)]
    for b in range(blocks):
        for c, h in share_out[b]:
            stencil(c, h)
        force, _ = pair_sum(body_of(b), spread, b * LANES, None)
        for c in range(3):
            force_ref[c, b : b + 1, :] = force[c]

    for b in range(blocks):
        height, over, _ = spot_of(b)
        share = blob_ref[shares + b : shares + b + 1, :]
        mask = rows == over
        column = slice(b * LANES, (b + 1) * LANES)
        near = [
            jnp.where(height == h, 1.0 - share, jnp.where(height == h - 1, share, 0.0)) for h in range(depth)
        ]
        for c in range(3):
            total = jnp.zeros((SUBLANES, LANES), F32)
            for h in range(depth):
                k = c * depth + h
                seen = jnp.where(mask, seen_ref[k * across : (k + 1) * across, column], 0.0)
                total += near[h] * jnp.sum(seen.reshape(across // SUBLANES, SUBLANES, LANES), axis=0)
            met = jnp.sum(total, axis=0, keepdims=True)
            drag = drag_coef * blob_ref[bodies + 8 * b + 6 : bodies + 8 * b + 7, :] * (
                met - blob_ref[bodies + 8 * b + 3 + c : bodies + 8 * b + 4 + c, :]
            )
            force_ref[c, b : b + 1, :] += drag
            for h in range(depth):
                weights[c * depth + h : c * depth + h + 1, column] = (-source_gain) * near[h] * drag
        ones = lane_one_hot(halves, jnp.where(over >= half, over - half, over))
        for n, part in enumerate(split_parts(weights[:, column])):
            for k in range(3 * depth):
                coupled[k * half : (k + 1) * half, n * wide + b * LANES : n * wide + (b + 1) * LANES] = place_lines(
                    ones, part[k : k + 1], half
                )
    for c in range(3):
        face = slice(c * depth * half, (c + 1) * depth * half)
        source_ref[face, :] = lax.dot_general(
            coupled[face, :], spots[...], (((1,), (1,)), ((), ())), preferred_element_type=F32
        )

    for i in range(listed):
        for c, h in share_out[blocks + i]:
            stencil(c, h)
        a, c = pair_ref[0, i], pair_ref[1, i]
        left = blob_ref[pl.ds(pl.multiple_of(bodies + 8 * a, 8), 8), :]
        ahead, behind = pair_sum(left, spread, c * LANES, react.at[i])
        for side, forces in enumerate((ahead, behind)):
            for d in range(3):
                found[2 * i + side, d : d + 1, :] = forces[d]
    for b in range(blocks):
        for d in range(3):
            total = force_ref[d, b : b + 1, :]
            for i in range(listed):
                for side in range(2):
                    total += jnp.where(pair_ref[side, i] == b, found[2 * i + side, d : d + 1, :], 0.0)
            force_ref[d, b : b + 1, :] = total


def finish_kernel(counts, blocks, pairs, force_ref, partial_ref, source_ref, *refs):
    n_in = sum(counts)
    sent = refs[: counts[0]]
    height_ins, across_ins, along_ins = by_axis(refs[counts[0] : counts[0] + n_in], counts)
    out_force, next_hbm, next_ref, spread, pieces, picks, seen_ref, coupled, spots, sems = refs[counts[0] + n_in :]
    depth, across, along = partial_ref.shape[1:]
    fold = spots.shape[0] // along
    half = across // fold
    wide = blocks * LANES
    bodies, cells, shares, lists, _ = blob_layout(across, blocks, pairs)
    even = parities()

    def ordered(arrived, axis):
        first = arrived[0][...]
        if len(arrived) == 1:
            return jnp.where(even[axis], 0.0, first), jnp.where(even[axis], first, 0.0)
        second = arrived[1][...]
        return jnp.where(even[axis], second, first), jnp.where(even[axis], first, second)

    across_low, across_high = ordered(across_ins, 1)
    across_low = diffuse * across_low
    across_high = diffuse * across_high
    edges = along_ins[0][...]
    if len(along_ins) > 1:
        edges = edges + along_ins[1][...]
    edges = diffuse * edges
    lanes = lax.broadcasted_iota(jnp.int32, (across, along), 1)
    subs = lax.broadcasted_iota(jnp.int32, (SUBLANES, along), 0)
    tail = across - SUBLANES
    rim = jnp.logical_or(lanes == 0, lanes == along - 1)
    copies = []
    for c in range(3):
        for h in range(depth):
            k = c * depth + h
            given = [
                source_ref[k * half : (k + 1) * half, f * along : (f + 1) * along] for f in range(fold)
            ]
            value = partial_ref[c, h] + jnp.concatenate(given, axis=0)
            value += jnp.where(rim, pltpu.roll(edges, (along - 2 * k) % along, 1) if k else edges, 0.0)
            next_ref[c, h] = value
            next_ref[c, h, :SUBLANES, :] += jnp.where(subs == 0, across_low[k : k + 1, :], 0.0)
            next_ref[c, h, tail:, :] += jnp.where(subs == SUBLANES - 1, across_high[k : k + 1, :], 0.0)
        if depth > 2:
            inner = pl.ds(1, depth - 2)
            copies.append(pltpu.make_async_copy(next_ref.at[c, inner], next_hbm.at[c, inner], sems.at[c]))
            copies[-1].start()

    rows = lax.broadcasted_iota(jnp.int32, (across, LANES), 0)
    halves = lax.broadcasted_iota(jnp.int32, (half, LANES), 0)
    coupling = [[jnp.zeros((1, LANES), F32)] * blocks for _ in range(3)]
    for n, blob in enumerate(height_ins):
        own = sent[n]
        above = even[0] if n == 0 else jnp.logical_not(even[0])
        own_layer = jnp.where(above, depth - 1, 0)
        below = jnp.logical_not(above)
        for k in range(3):
            face = slice(k * across, (k + 1) * across)
            pieces[face, :] = parts_of(blob[face, :])
            pieces[(3 + k) * across : (4 + k) * across, :] = parts_of(own[face, :])
        lined = []
        for b in range(blocks):
            cell = jnp.where(above, own[cells + b : cells + b + 1, :], blob[cells + b : cells + b + 1, :])
            height, over, spot = places(cell.astype(jnp.int32), across, along)
            lined.append((height, over))
            mark_cells(picks, spots, b, over, spot, half, wide)
        seen_ref[...] = jnp.dot(pieces[...], picks[...], preferred_element_type=F32)
        for b in range(blocks):
            height, over = lined[b]
            share = jnp.where(above, own[shares + b : shares + b + 1, :], blob[shares + b : shares + b + 1, :])
            body = slice(bodies + 8 * b, bodies + 8 * b + 8)
            owner = jnp.where(above, own[body, :], blob[body, :])
            top = height == depth - 1
            mask = rows == over
            column = slice(b * LANES, (b + 1) * LANES)
            seen_share = jnp.where(top, jnp.where(above, share, 1.0 - share), 0.0)
            home_share = jnp.where(jnp.logical_and(top, below), share, 0.0)
            given_share = (-source_gain) * jnp.where(above, 1.0 - share, share)
            own_share = jnp.where(jnp.logical_and(top, below), 1.0, 0.0)
            ones = lane_one_hot(halves, jnp.where(over >= half, over - half, over))
            for c in range(3):
                seen = seen_ref[c * across : (c + 1) * across, column]
                home = seen_ref[(3 + c) * across : (4 + c) * across, column]
                met = jnp.where(mask, seen_share * seen + home_share * home, 0.0)
                met = jnp.sum(met, axis=0, keepdims=True)
                drag = drag_coef * owner[6:7] * (met - own_share * owner[3 + c : 4 + c])
                coupling[c][b] += jnp.where(above, drag, 0.0)
                for m, part in enumerate(split_parts(given_share * drag)):
                    coupled[c * half : (c + 1) * half, m * wide + b * LANES : m * wide + (b + 1) * LANES] = (
                        place_lines(ones, part, half)
                    )
        source = lax.dot_general(
            coupled[...], spots[...], (((1,), (1,)), ((), ())), preferred_element_type=F32
        )
        for c in range(3):
            given = [source[c * half : (c + 1) * half, f * along : (f + 1) * along] for f in range(fold)]
            next_ref[c, own_layer] += diffuse * blob[c * across : (c + 1) * across, :] + jnp.concatenate(given, axis=0)
    for n, h in enumerate(sorted({0, depth - 1})):
        copies.append(pltpu.make_async_copy(next_ref.at[:, h], next_hbm.at[:, h], sems.at[3 + n]))
        copies[-1].start()

    meetings, partners = [], []
    for n, blob in enumerate(height_ins):
        own = sent[n]
        above = even[0] if n == 0 else jnp.logical_not(even[0])
        for k in range(pairs):
            ours = [own[lists + 2 * k + side : lists + 2 * k + side + 1, :] for side in range(2)]
            theirs = [blob[lists + 2 * k + side : lists + 2 * k + side + 1, :] for side in range(2)]
            to = jnp.where(above, ours[0], theirs[1])
            by = jnp.where(above, ours[1], theirs[0])
            left = own[bodies : bodies + 8, :]
            right = blob[bodies : bodies + 8, :]
            for b in range(1, blocks):
                body = slice(bodies + 8 * b, bodies + 8 * b + 8)
                left = jnp.where(to == b, own[body, :], left)
                right = jnp.where(by == b, blob[body, :], right)
            meetings.append((to, left))
            partners.append(right)
    spread[...] = spread_blocks(partners)
    for i, (to, left) in enumerate(meetings):
        force, _ = pair_sum(left, spread, i * LANES, None)
        for b in range(blocks):
            for c in range(3):
                coupling[c][b] += jnp.where(to == b, force[c], 0.0)
    for b in range(blocks):
        for c in range(3):
            out_force[c, b : b + 1, :] = force_ref[c, b : b + 1, :] + coupling[c][b]
    for copy in copies:
        copy.wait()


def by_axis(refs, counts):
    groups, at = [], 0
    for n in counts:
        groups.append(refs[at : at + n])
        at += n
    return groups


def exchange(payloads, axis):
    count = lax.axis_size(axis)
    results = []
    for n, payload in enumerate(payloads):
        route = []
        for i in range(n, count - 1, 2):
            route += [(i, i + 1), (i + 1, i)]
        results.append(lax.ppermute(payload, axis, route))
    return results


def body(particles, local_pairs, cross_pairs, drag_cell, drag_share, fluid):
    blocks = particles.shape[0]
    pairs = cross_pairs.shape[0]
    listed = local_pairs.shape[0]
    _, depth, across, along = fluid.shape
    counts = [min(2, lax.axis_size(axis) - 1) for axis in AXES]
    fold = 2 if across % 32 == 0 else 1
    half = across // fold
    wide = PARTS * blocks * LANES
    rows = blob_layout(across, blocks, pairs)[-1]
    shapes = [(rows, along), (3 * depth, along), (across, along)]
    vmem = pl.BlockSpec(memory_space=pltpu.VMEM)
    hbm = pl.BlockSpec(memory_space=pltpu.HBM)
    smem = pl.BlockSpec(memory_space=pltpu.SMEM)

    def kept(value):
        return pltpu.with_memory_space_constraint(value, pltpu.VMEM)

    listing, fluid_kept, pieces, picks, spots, spread, *packed = pl.pallas_call(
        functools.partial(pack_kernel, counts),
        out_shape=[
            pltpu.SMEM((2, listed), jnp.int32),
            pltpu.VMEM(fluid.shape, F32),
            pltpu.VMEM((3 * depth * across, PARTS * along), BF16),
            pltpu.VMEM((PARTS * along, blocks * LANES + along), BF16),
            pltpu.VMEM((fold * along, wide), BF16),
            pltpu.VMEM((blocks * LANES, 9 * LANES), F32),
        ]
        + [pltpu.VMEM(shape, F32) for shape, n in zip(shapes, counts) for _ in range(n)],
        in_specs=[hbm] * 6,
        out_specs=[smem] + [vmem] * (5 + sum(counts)),
        scratch_shapes=[
            pltpu.SMEM(cross_pairs.shape, jnp.int32),
            pltpu.VMEM(particles.shape, F32),
            pltpu.VMEM(drag_cell.shape, jnp.int32),
            pltpu.VMEM(drag_share.shape, F32),
            pltpu.SemaphoreType.DMA((8,)),
        ],
        compiler_params=pltpu.CompilerParams(vmem_limit_bytes=GRANT),
        name="pack",
    )(
        *[
            pltpu.with_memory_space_constraint(value, pltpu.HBM)
            for value in (local_pairs.T, cross_pairs, particles, drag_cell, drag_share, fluid)
        ]
    )
    received = []
    for axis, payloads in zip(AXES, by_axis(packed, counts)):
        received += exchange(payloads, axis)

    force, partial, source = pl.pallas_call(
        functools.partial(local_kernel, blocks, pairs),
        out_shape=[
            pltpu.VMEM((3, blocks, LANES), F32),
            pltpu.VMEM(fluid.shape, F32),
            pltpu.VMEM((3 * depth * half, fold * along), F32),
        ],
        in_specs=[smem] + [vmem] * 6,
        out_specs=[vmem] * 3,
        scratch_shapes=[
            pltpu.VMEM((listed, LANES, LANES), F32),
            pltpu.VMEM((3 * depth * across, blocks * LANES + along), F32),
            pltpu.VMEM((2 * listed, SUBLANES, LANES), F32),
            pltpu.VMEM((3 * depth, blocks * LANES), F32),
            pltpu.VMEM((3 * depth * half, wide), BF16),
        ],
        compiler_params=pltpu.CompilerParams(vmem_limit_bytes=GRANT),
        name="local",
    )(
        pltpu.with_memory_space_constraint(listing, pltpu.SMEM),
        *[kept(value) for value in (packed[0], fluid_kept, pieces, picks, spots, spread)],
    )

    out_force, out_next = pl.pallas_call(
        functools.partial(finish_kernel, counts, blocks, pairs),
        out_shape=[
            jax.ShapeDtypeStruct((3, blocks, LANES), F32),
            jax.ShapeDtypeStruct(fluid.shape, F32),
        ],
        in_specs=[vmem] * (3 + counts[0] + len(received)),
        out_specs=[vmem, hbm],
        scratch_shapes=[
            pltpu.VMEM(fluid.shape, F32),
            pltpu.VMEM((counts[0] * pairs * LANES, 9 * LANES), F32),
            pltpu.VMEM((6 * across, PARTS * along), BF16),
            pltpu.VMEM((PARTS * along, blocks * LANES), BF16),
            pltpu.VMEM((6 * across, blocks * LANES), F32),
            pltpu.VMEM((3 * half, wide), BF16),
            pltpu.VMEM((fold * along, wide), BF16),
            pltpu.SemaphoreType.DMA((5,)),
        ],
        compiler_params=pltpu.CompilerParams(vmem_limit_bytes=GRANT),
        name="finish",
    )(*[kept(value) for value in [force, partial, source, *packed[: counts[0]], *received]])
    return jnp.transpose(out_force, (1, 0, 2)), out_next


def solution(mesh):
    in_specs = (
        P(("gx", "gy", "gz"), None, None),
        P(("gx", "gy", "gz"), None),
        P(("gx", "gy", "gz"), None),
        P(("gx", "gy", "gz"), None),
        P(("gx", "gy", "gz"), None),
        P(None, "gx", "gy", "gz"),
    )
    out_specs = (P(("gx", "gy", "gz"), None, None), P(None, "gx", "gy", "gz"))
    return jax.shard_map(body, mesh=mesh, in_specs=in_specs, out_specs=out_specs, check_vma=False)
```

```python
import functools

import jax
import jax.numpy as jnp
from jax import lax
from jax.experimental import pallas as pl
from jax.experimental.pallas import tpu as pltpu
from jax.sharding import PartitionSpec as P


soft_core = 0.01
damp_normal = 0.3
damp_tangent = 0.2
drag_coef = 1.5
diffuse = 0.1
source_gain = 0.5

F32 = jnp.float32
BF16 = jnp.bfloat16
PARTS = 2
EXACT = 3
LANES = 128
SUBLANES = 8
GRANT = 32 * 1024 * 1024
AXES = ("gx", "gy", "gz")


def split_parts(value, count=PARTS):
    parts = []
    for _ in range(count):
        part = value.astype(BF16).astype(F32)
        parts.append(part)
        value = value - part
    return parts


def places(cell, across, along):
    layer = across * along
    if layer & (layer - 1) or along & (along - 1):
        return cell // layer, cell // along % across, cell % along
    shift = along.bit_length() - 1
    high = layer.bit_length() - 1
    return (
        lax.shift_right_logical(cell, high),
        lax.shift_right_logical(cell, shift) & (across - 1),
        cell & (along - 1),
    )


def parts_of(value):
    return jnp.concatenate([part.astype(BF16) for part in split_parts(value)], axis=1)


def spread_blocks(blocks):
    columns = []
    for block in blocks:
        rows = jnp.concatenate([block, block[7:8] * jnp.sqrt(block[6:7])], axis=0)
        parts = split_parts(rows, EXACT)
        parts.append(jnp.zeros((32 - 9 * EXACT, LANES), F32))
        columns.append(jnp.transpose(jnp.concatenate(parts, axis=0)).astype(BF16))
    lines = lax.broadcasted_iota(jnp.int32, (32, LANES), 0)
    picks = []
    for i in range(9):
        pick = lines == i
        for n in range(1, EXACT):
            pick = jnp.logical_or(pick, lines == i + 9 * n)
        picks.append(jnp.where(pick, 1.0, 0.0).astype(BF16))
    return jnp.dot(
        jnp.concatenate(columns, axis=0), jnp.concatenate(picks, axis=1), preferred_element_type=F32
    )


def pair_sum(left, spread, start, react):
    rows = [left[i : i + 1] for i in range(8)]
    rows.append((2.0 * damp_tangent) * rows[7] * jnp.sqrt(rows[6]))
    wide = [jnp.broadcast_to(row, (SUBLANES, LANES)) for row in rows]
    lanes = lax.broadcasted_iota(jnp.int32, (SUBLANES, LANES), 1)
    total = [None] * 3
    for tile in range(LANES // SUBLANES):
        place = pl.ds(pl.multiple_of(start + tile * SUBLANES, SUBLANES), SUBLANES)
        there = [spread[place, i * LANES : (i + 1) * LANES] for i in range(9)]
        ex, ey, ez, wx, wy, wz = [wide[i] - there[i] for i in range(6)]
        square = (ex * ex + ey * ey) + (ez * ez + soft_core)
        inverse = lax.rsqrt(square)
        reach = wide[6] + there[6]
        delta = jnp.maximum(reach - square * inverse, 0.0)
        mass = wide[7] + there[7]
        under = jnp.maximum((delta * reach) * (mass * mass), 1e-30)
        tangent = (wide[8] * there[8]) * (delta * lax.rsqrt(under))
        speed = ((wx * ex + wy * ey) + wz * ez) * inverse
        along = (
            (2.0 / 3.0 / damp_tangent) * delta - ((damp_normal - damp_tangent) / damp_tangent) * speed
        ) * (tangent * inverse)
        column = None
        for d, (e, w) in enumerate(((ex, wx), (ey, wy), (ez, wz))):
            force = along * e - tangent * w
            total[d] = force if total[d] is None else total[d] + force
            if react is not None:
                across_sum = jnp.broadcast_to(jnp.sum(force, axis=1, keepdims=True), (SUBLANES, LANES))
                column = across_sum if column is None else jnp.where(lanes == d, across_sum, column)
        if react is not None:
            react[tile * SUBLANES : (tile + 1) * SUBLANES, :] = column
    total = [jnp.sum(item, axis=0, keepdims=True) for item in total]
    if react is None:
        return total, None
    turned = jnp.transpose(react[...])
    return total, [-turned[d : d + 1] for d in range(3)]


def blob_layout(across, blocks, pairs):
    bodies = 3 * across
    cells = bodies + 8 * blocks
    shares = cells + blocks
    lists = shares + blocks
    rows = lists + 2 * pairs
    return bodies, cells, shares, lists, rows + -rows % 8


def parities():
    return [lax.rem(lax.axis_index(axis), 2) == 0 for axis in AXES]


def pack_kernel(counts, list_hbm, pair_hbm, part_hbm, cell_hbm, share_hbm, fluid_hbm, *refs):
    n_out = 2 + sum(counts)
    list_ref, fluid_ref = refs[:2]
    height_outs, across_outs, along_outs = by_axis(refs[2:n_out], counts)
    pair_ref, part_ref, cell_ref, share_ref, sems = refs[n_out:]
    depth, across, along = fluid_ref.shape[1:]
    blocks, pairs = part_ref.shape[0], pair_ref.shape[0]
    bodies, cells, shares, lists, rows = blob_layout(across, blocks, pairs)
    small = [(part_hbm, part_ref), (cell_hbm, cell_ref), (share_hbm, share_ref), (pair_hbm, pair_ref), (list_hbm, list_ref)]
    small = [pltpu.make_async_copy(source, target, sems.at[3 + n]) for n, (source, target) in enumerate(small)]
    copies = [pltpu.make_async_copy(fluid_hbm.at[c], fluid_ref.at[c], sems.at[c]) for c in range(3)]
    for copy in small + copies:
        copy.start()
    even = parities()
    for copy in small + copies:
        copy.wait()
    for out in height_outs:
        for b in range(blocks):
            out[bodies + 8 * b : bodies + 8 * b + 8, :] = part_ref[b]
        out[cells:shares, :] = cell_ref[...].astype(F32)
        out[shares:lists, :] = share_ref[...]
        for k in range(pairs):
            for side in range(2):
                row = lists + 2 * k + side
                out[row : row + 1, :] = jnp.full((1, LANES), pair_ref[k, side], jnp.int32).astype(F32)
        used = lists + 2 * pairs
        if used < rows:
            out[used:rows, :] = jnp.zeros((rows - used, LANES), F32)
    lanes = lax.broadcasted_iota(jnp.int32, (across, along), 1)
    first = jnp.zeros((across, along), F32)
    last = jnp.zeros((across, along), F32)
    for c in range(3):
        for n, out in enumerate(height_outs):
            upward = even[0] if n == 0 else jnp.logical_not(even[0])
            out[c * across : (c + 1) * across, :] = fluid_ref[c, jnp.where(upward, depth - 1, 0)]
        for h in range(depth):
            k = c * depth + h
            here = fluid_ref[c, h]
            for n, out in enumerate(across_outs):
                upward = even[1] if n == 0 else jnp.logical_not(even[1])
                out[k : k + 1, :] = jnp.where(upward, here[across - 1 : across], here[0:1])
            turned = pltpu.roll(here, 2 * k, 1) if k else here
            first = jnp.where(lanes == 2 * k, turned, first)
            last = jnp.where(lanes == (2 * k - 1) % along, turned, last)
    first = pltpu.roll(first, along - 1, 1)
    last = pltpu.roll(last, 1, 1)
    for n, out in enumerate(along_outs):
        upward = even[2] if n == 0 else jnp.logical_not(even[2])
        out[...] = jnp.where(upward, last, first)


def mark_cells(picks, spots, b, over, spot, half, wide):
    along = picks.shape[0] // PARTS
    sites = lax.broadcasted_iota(jnp.int32, (spots.shape[0], LANES), 0)
    one_hot = lane_one_hot(sites[:along], spot)
    for n in range(PARTS):
        picks[n * along : (n + 1) * along, b * LANES : (b + 1) * LANES] = one_hot
    one_hot = lane_one_hot(sites, jnp.where(over >= half, along, 0) + spot)
    for n in range(PARTS):
        spots[:, n * wide + b * LANES : n * wide + (b + 1) * LANES] = one_hot


def lane_one_hot(sites, target):
    return jnp.where(sites == target, 1.0, 0.0).astype(BF16)


def place_lines(ones, part, half):
    line = jnp.broadcast_to(part, (16, LANES)).astype(BF16)
    line = jnp.concatenate([line] * (half // 16), axis=0)
    return jnp.where(ones > 0, line, jnp.zeros_like(line))


def rim_kernel_part(blocks, pairs, half, fold, sent, height_ins, next_ref, scratch):
    spread, pieces, picks, seen_ref, coupled, spots = scratch
    depth, across, along = next_ref.shape[1:]
    wide = blocks * LANES
    bodies, cells, shares, lists, _ = blob_layout(across, blocks, pairs)
    even = parities()
    rows = lax.broadcasted_iota(jnp.int32, (across, LANES), 0)
    halves = lax.broadcasted_iota(jnp.int32, (half, LANES), 0)
    coupling = [[jnp.zeros((1, LANES), F32)] * blocks for _ in range(3)]
    meetings, partners = [], []
    for n, blob in enumerate(height_ins):
        own = sent[n]
        above = even[0] if n == 0 else jnp.logical_not(even[0])
        for k in range(pairs):
            ours = [own[lists + 2 * k + side : lists + 2 * k + side + 1, :] for side in range(2)]
            theirs = [blob[lists + 2 * k + side : lists + 2 * k + side + 1, :] for side in range(2)]
            to = jnp.where(above, ours[0], theirs[1])
            by = jnp.where(above, ours[1], theirs[0])
            left = own[bodies : bodies + 8, :]
            right = blob[bodies : bodies + 8, :]
            for b in range(1, blocks):
                body = slice(bodies + 8 * b, bodies + 8 * b + 8)
                left = jnp.where(to == b, own[body, :], left)
                right = jnp.where(by == b, blob[body, :], right)
            meetings.append((to, left))
            partners.append(right)
    spread[...] = spread_blocks(partners)
    for i, (to, left) in enumerate(meetings):
        force, _ = pair_sum(left, spread, i * LANES, None)
        for b in range(blocks):
            for c in range(3):
                coupling[c][b] += jnp.where(to == b, force[c], 0.0)
    for n, blob in enumerate(height_ins):
        own = sent[n]
        above = even[0] if n == 0 else jnp.logical_not(even[0])
        own_layer = jnp.where(above, depth - 1, 0)
        below = jnp.logical_not(above)
        for k in range(3):
            face = slice(k * across, (k + 1) * across)
            pieces[face, :] = parts_of(blob[face, :])
            pieces[(3 + k) * across : (4 + k) * across, :] = parts_of(own[face, :])
        lined = []
        for b in range(blocks):
            cell = jnp.where(above, own[cells + b : cells + b + 1, :], blob[cells + b : cells + b + 1, :])
            height, over, spot = places(cell.astype(jnp.int32), across, along)
            lined.append((height, over))
            mark_cells(picks, spots, b, over, spot, half, wide)
        seen_ref[...] = jnp.dot(pieces[...], picks[...], preferred_element_type=F32)
        for b in range(blocks):
            height, over = lined[b]
            share = jnp.where(above, own[shares + b : shares + b + 1, :], blob[shares + b : shares + b + 1, :])
            body = slice(bodies + 8 * b, bodies + 8 * b + 8)
            owner = jnp.where(above, own[body, :], blob[body, :])
            top = height == depth - 1
            mask = rows == over
            column = slice(b * LANES, (b + 1) * LANES)
            seen_share = jnp.where(top, jnp.where(above, share, 1.0 - share), 0.0)
            home_share = jnp.where(jnp.logical_and(top, below), share, 0.0)
            given_share = (-source_gain) * jnp.where(above, 1.0 - share, share)
            own_share = jnp.where(jnp.logical_and(top, below), 1.0, 0.0)
            ones = lane_one_hot(halves, jnp.where(over >= half, over - half, over))
            for c in range(3):
                seen = seen_ref[c * across : (c + 1) * across, column]
                home = seen_ref[(3 + c) * across : (4 + c) * across, column]
                met = jnp.where(mask, seen_share * seen + home_share * home, 0.0)
                met = jnp.sum(met, axis=0, keepdims=True)
                drag = drag_coef * owner[6:7] * (met - own_share * owner[3 + c : 4 + c])
                coupling[c][b] += jnp.where(above, drag, 0.0)
                for m, part in enumerate(split_parts(given_share * drag)):
                    coupled[c * half : (c + 1) * half, m * wide + b * LANES : m * wide + (b + 1) * LANES] = (
                        place_lines(ones, part, half)
                    )
        source = lax.dot_general(
            coupled[...], spots[...], (((1,), (1,)), ((), ())), preferred_element_type=F32
        )
        for c in range(3):
            given = [source[c * half : (c + 1) * half, f * along : (f + 1) * along] for f in range(fold)]
            next_ref[c, own_layer] += diffuse * blob[c * across : (c + 1) * across, :] + jnp.concatenate(given, axis=0)
    return coupling


def local_kernel(blocks, pairs, pair_ref, fluid_ref, *refs):
    count = (len(refs) - 18) // 2
    sent, height_ins = refs[:count], refs[count : 2 * count]
    force_ref, next_ref, source_ref = refs[2 * count : 2 * count + 3]
    spread, pieces, picks, spots, react, seen_ref, found, weights, coupled = refs[2 * count + 3 : 2 * count + 12]
    rim_refs = refs[2 * count + 12 :]
    blob_ref = sent[0]
    depth, across, along = fluid_ref.shape[1:]
    listed = pair_ref.shape[1]
    fold = spots.shape[0] // along
    half = across // fold
    wide = blocks * LANES
    bodies, cells, shares, _, _ = blob_layout(across, blocks, pairs)
    rows = lax.broadcasted_iota(jnp.int32, (across, LANES), 0)
    halves = lax.broadcasted_iota(jnp.int32, (half, LANES), 0)
    subs = lax.broadcasted_iota(jnp.int32, (SUBLANES, along), 0)
    slabs = [(c, h) for c in range(3) for h in range(depth)]

    def body_of(b):
        return blob_ref[bodies + 8 * b : bodies + 8 * b + 8, :]

    def spot_of(b):
        return places(blob_ref[cells + b : cells + b + 1, :].astype(jnp.int32), across, along)

    def stencil(c, h):
        for t in range(across // SUBLANES):
            at = t * SUBLANES
            here = fluid_ref[c, h, at : at + SUBLANES, :]
            if t > 0:
                beside = fluid_ref[c, h, at - 1 : at + SUBLANES - 1, :]
            else:
                beside = jnp.where(subs == 0, 0.0, pltpu.roll(here, 1, 0))
            if at + SUBLANES < across:
                beside += fluid_ref[c, h, at + 1 : at + SUBLANES + 1, :]
            else:
                beside += jnp.where(subs == SUBLANES - 1, 0.0, pltpu.roll(here, SUBLANES - 1, 0))
            line = (c * depth + h) * across + at
            beside += seen_ref[line : line + SUBLANES, wide : wide + along]
            if h > 0:
                beside += fluid_ref[c, h - 1, at : at + SUBLANES, :]
            if h < depth - 1:
                beside += fluid_ref[c, h + 1, at : at + SUBLANES, :]
            next_ref[c, h, at : at + SUBLANES, :] = (1.0 - 6.0 * diffuse) * here + diffuse * beside

    spread[...] = spread_blocks([body_of(b) for b in range(blocks)])
    for k, (c, h) in enumerate(slabs):
        pieces[k * across : (k + 1) * across, :] = parts_of(fluid_ref[c, h])
    for b in range(blocks):
        _, over, spot = spot_of(b)
        mark_cells(picks, spots, b, over, spot, half, wide)
    here = lax.broadcasted_iota(jnp.int32, (along, along), 0)
    there = lax.broadcasted_iota(jnp.int32, (along, along), 1)
    near = jnp.where(jnp.abs(here - there) == 1, 1.0, 0.0).astype(BF16)
    for n in range(PARTS):
        picks[n * along : (n + 1) * along, wide : wide + along] = near
    seen_ref[...] = jnp.dot(pieces[...], picks[...], preferred_element_type=F32)

    turns = blocks + listed
    share_out = [slabs[i * len(slabs) // turns : (i + 1) * len(slabs) // turns] for i in range(turns)]
    for b in range(blocks):
        for c, h in share_out[b]:
            stencil(c, h)
        force, _ = pair_sum(body_of(b), spread, b * LANES, None)
        for c in range(3):
            force_ref[c, b : b + 1, :] = force[c]

    for b in range(blocks):
        height, over, _ = spot_of(b)
        share = blob_ref[shares + b : shares + b + 1, :]
        mask = rows == over
        column = slice(b * LANES, (b + 1) * LANES)
        near = [
            jnp.where(height == h, 1.0 - share, jnp.where(height == h - 1, share, 0.0)) for h in range(depth)
        ]
        for c in range(3):
            total = jnp.zeros((SUBLANES, LANES), F32)
            for h in range(depth):
                k = c * depth + h
                seen = jnp.where(mask, seen_ref[k * across : (k + 1) * across, column], 0.0)
                total += near[h] * jnp.sum(seen.reshape(across // SUBLANES, SUBLANES, LANES), axis=0)
            met = jnp.sum(total, axis=0, keepdims=True)
            drag = drag_coef * blob_ref[bodies + 8 * b + 6 : bodies + 8 * b + 7, :] * (
                met - blob_ref[bodies + 8 * b + 3 + c : bodies + 8 * b + 4 + c, :]
            )
            force_ref[c, b : b + 1, :] += drag
            for h in range(depth):
                weights[c * depth + h : c * depth + h + 1, column] = (-source_gain) * near[h] * drag
        ones = lane_one_hot(halves, jnp.where(over >= half, over - half, over))
        for n, part in enumerate(split_parts(weights[:, column])):
            for k in range(3 * depth):
                coupled[k * half : (k + 1) * half, n * wide + b * LANES : n * wide + (b + 1) * LANES] = place_lines(
                    ones, part[k : k + 1], half
                )
    for c in range(3):
        face = slice(c * depth * half, (c + 1) * depth * half)
        source_ref[face, :] = lax.dot_general(
            coupled[face, :], spots[...], (((1,), (1,)), ((), ())), preferred_element_type=F32
        )

    for i in range(listed):
        for c, h in share_out[blocks + i]:
            stencil(c, h)
        a, c = pair_ref[0, i], pair_ref[1, i]
        left = blob_ref[pl.ds(pl.multiple_of(bodies + 8 * a, 8), 8), :]
        ahead, behind = pair_sum(left, spread, c * LANES, react.at[i])
        for side, forces in enumerate((ahead, behind)):
            for d in range(3):
                found[2 * i + side, d : d + 1, :] = forces[d]
    coupling = rim_kernel_part(blocks, pairs, half, fold, sent, height_ins, next_ref, rim_refs)
    for b in range(blocks):
        for d in range(3):
            total = force_ref[d, b : b + 1, :]
            for i in range(listed):
                for side in range(2):
                    total += jnp.where(pair_ref[side, i] == b, found[2 * i + side, d : d + 1, :], 0.0)
            force_ref[d, b : b + 1, :] = total + coupling[d][b]


def finish_kernel(counts, sizes, partial_ref, source_ref, *refs):
    n_in = sum(counts[1:])
    across_ins, along_ins = by_axis(refs[:n_in], counts[1:])
    next_hbm, next_ref, sems = refs[n_in:]
    depth, across, along = partial_ref.shape[1:]
    fold = source_ref.shape[1] // along
    half = across // fold
    even = parities()

    def second_of(arrived, axis):
        second = arrived[1][...]
        if sizes[axis] % 2:
            return second
        place = lax.axis_index(AXES[axis])
        inside = jnp.logical_and(place > 0, place < sizes[axis] - 1)
        return jnp.where(inside, second, 0.0)

    def ordered(arrived, axis):
        first = arrived[0][...]
        if len(arrived) == 1:
            return jnp.where(even[axis], 0.0, first), jnp.where(even[axis], first, 0.0)
        second = second_of(arrived, axis)
        return jnp.where(even[axis], second, first), jnp.where(even[axis], first, second)

    across_low, across_high = ordered(across_ins, 1)
    across_low = diffuse * across_low
    across_high = diffuse * across_high
    edges = along_ins[0][...]
    if len(along_ins) > 1:
        edges = edges + second_of(along_ins, 2)
    edges = diffuse * edges
    lanes = lax.broadcasted_iota(jnp.int32, (across, along), 1)
    subs = lax.broadcasted_iota(jnp.int32, (SUBLANES, along), 0)
    tail = across - SUBLANES
    rim = jnp.logical_or(lanes == 0, lanes == along - 1)
    copies = []
    for c in range(3):
        for h in range(depth):
            k = c * depth + h
            given = [
                source_ref[k * half : (k + 1) * half, f * along : (f + 1) * along] for f in range(fold)
            ]
            value = partial_ref[c, h] + jnp.concatenate(given, axis=0)
            value += jnp.where(rim, pltpu.roll(edges, (along - 2 * k) % along, 1) if k else edges, 0.0)
            next_ref[c, h] = value
            next_ref[c, h, :SUBLANES, :] += jnp.where(subs == 0, across_low[k : k + 1, :], 0.0)
            next_ref[c, h, tail:, :] += jnp.where(subs == SUBLANES - 1, across_high[k : k + 1, :], 0.0)
        copies.append(pltpu.make_async_copy(next_ref.at[c], next_hbm.at[c], sems.at[c]))
        copies[-1].start()
    for copy in copies:
        copy.wait()


def by_axis(refs, counts):
    groups, at = [], 0
    for n in counts:
        groups.append(refs[at : at + n])
        at += n
    return groups


def exchange(payloads, axis, closed):
    count = lax.axis_size(axis)
    results = []
    for n, payload in enumerate(payloads):
        route = []
        for i in range(n, count - 1, 2):
            route += [(i, i + 1), (i + 1, i)]
        if closed and n == 1 and count % 2 == 0:
            route += [(0, count - 1), (count - 1, 0)]
        results.append(lax.ppermute(payload, axis, route))
    return results


def body(particles, local_pairs, cross_pairs, drag_cell, drag_share, fluid):
    blocks = particles.shape[0]
    pairs = cross_pairs.shape[0]
    listed = local_pairs.shape[0]
    _, depth, across, along = fluid.shape
    counts = [min(2, lax.axis_size(axis) - 1) for axis in AXES]
    fold = 2 if across % 32 == 0 else 1
    half = across // fold
    wide = PARTS * blocks * LANES
    rows = blob_layout(across, blocks, pairs)[-1]
    shapes = [(rows, along), (3 * depth, along), (across, along)]
    vmem = pl.BlockSpec(memory_space=pltpu.VMEM)
    hbm = pl.BlockSpec(memory_space=pltpu.HBM)
    smem = pl.BlockSpec(memory_space=pltpu.SMEM)

    def kept(value):
        return pltpu.with_memory_space_constraint(value, pltpu.VMEM)

    listing, fluid_kept, *packed = pl.pallas_call(
        functools.partial(pack_kernel, counts),
        out_shape=[
            pltpu.SMEM((2, listed), jnp.int32),
            pltpu.VMEM(fluid.shape, F32),
        ]
        + [pltpu.VMEM(shape, F32) for shape, n in zip(shapes, counts) for _ in range(n)],
        in_specs=[hbm] * 6,
        out_specs=[smem] + [vmem] * (1 + sum(counts)),
        scratch_shapes=[
            pltpu.SMEM(cross_pairs.shape, jnp.int32),
            pltpu.VMEM(particles.shape, F32),
            pltpu.VMEM(drag_cell.shape, jnp.int32),
            pltpu.VMEM(drag_share.shape, F32),
            pltpu.SemaphoreType.DMA((8,)),
        ],
        compiler_params=pltpu.CompilerParams(vmem_limit_bytes=GRANT),
        name="pack",
    )(
        *[
            pltpu.with_memory_space_constraint(value, pltpu.HBM)
            for value in (local_pairs.T, cross_pairs, particles, drag_cell, drag_share, fluid)
        ]
    )
    received = []
    for axis, payloads in zip(AXES, by_axis(packed, counts)):
        received += exchange(payloads, axis, axis != AXES[0])

    height_count = counts[0]
    out_force, partial, source = pl.pallas_call(
        functools.partial(local_kernel, blocks, pairs),
        out_shape=[
            jax.ShapeDtypeStruct((3, blocks, LANES), F32),
            pltpu.VMEM(fluid.shape, F32),
            pltpu.VMEM((3 * depth * half, fold * along), F32),
        ],
        in_specs=[smem] + [vmem] * (1 + 2 * height_count),
        out_specs=[vmem] * 3,
        scratch_shapes=[
            pltpu.VMEM((blocks * LANES, 9 * LANES), F32),
            pltpu.VMEM((3 * depth * across, PARTS * along), BF16),
            pltpu.VMEM((PARTS * along, blocks * LANES + along), BF16),
            pltpu.VMEM((fold * along, wide), BF16),
            pltpu.VMEM((listed, LANES, LANES), F32),
            pltpu.VMEM((3 * depth * across, blocks * LANES + along), F32),
            pltpu.VMEM((2 * listed, SUBLANES, LANES), F32),
            pltpu.VMEM((3 * depth, blocks * LANES), F32),
            pltpu.VMEM((3 * depth * half, wide), BF16),
            pltpu.VMEM((height_count * pairs * LANES, 9 * LANES), F32),
            pltpu.VMEM((6 * across, PARTS * along), BF16),
            pltpu.VMEM((PARTS * along, blocks * LANES), BF16),
            pltpu.VMEM((6 * across, blocks * LANES), F32),
            pltpu.VMEM((3 * half, wide), BF16),
            pltpu.VMEM((fold * along, wide), BF16),
        ],
        compiler_params=pltpu.CompilerParams(vmem_limit_bytes=GRANT),
        name="local",
    )(
        pltpu.with_memory_space_constraint(listing, pltpu.SMEM),
        *[kept(value) for value in (fluid_kept, *packed[:height_count], *received[:height_count])],
    )

    rest = received[height_count:]
    out_next = pl.pallas_call(
        functools.partial(finish_kernel, counts, [lax.axis_size(axis) for axis in AXES]),
        out_shape=jax.ShapeDtypeStruct(fluid.shape, F32),
        in_specs=[vmem] * (2 + len(rest)),
        out_specs=hbm,
        scratch_shapes=[pltpu.VMEM(fluid.shape, F32), pltpu.SemaphoreType.DMA((3,))],
        compiler_params=pltpu.CompilerParams(vmem_limit_bytes=GRANT),
        name="finish",
    )(*[kept(value) for value in [partial, source, *rest]])
    return jnp.transpose(out_force, (1, 0, 2)), out_next


def solution(mesh):
    in_specs = (
        P(("gx", "gy", "gz"), None, None),
        P(("gx", "gy", "gz"), None),
        P(("gx", "gy", "gz"), None),
        P(("gx", "gy", "gz"), None),
        P(("gx", "gy", "gz"), None),
        P(None, "gx", "gy", "gz"),
    )
    out_specs = (P(("gx", "gy", "gz"), None, None), P(None, "gx", "gy", "gz"))
    return jax.shard_map(body, mesh=mesh, in_specs=in_specs, out_specs=out_specs, check_vma=False)
```

```python
import functools

import jax
import jax.numpy as jnp
from jax import lax
from jax.experimental import pallas as pl
from jax.experimental.pallas import tpu as pltpu
from jax.sharding import PartitionSpec as P


soft_core = 0.01
damp_normal = 0.3
damp_tangent = 0.2
drag_coef = 1.5
diffuse = 0.1
source_gain = 0.5

F32 = jnp.float32
BF16 = jnp.bfloat16
PARTS = 2
EXACT = 3
LANES = 128
SUBLANES = 8
GRANT = 32 * 1024 * 1024
AXES = ("gx", "gy", "gz")


def split_parts(value, count=PARTS):
    parts = []
    for _ in range(count):
        part = value.astype(BF16).astype(F32)
        parts.append(part)
        value = value - part
    return parts


def places(cell, across, along):
    layer = across * along
    if layer & (layer - 1) or along & (along - 1):
        return cell // layer, cell // along % across, cell % along
    shift = along.bit_length() - 1
    high = layer.bit_length() - 1
    return (
        lax.shift_right_logical(cell, high),
        lax.shift_right_logical(cell, shift) & (across - 1),
        cell & (along - 1),
    )


def parts_of(value):
    return jnp.concatenate([part.astype(BF16) for part in split_parts(value)], axis=1)


def spread_blocks(blocks):
    columns = []
    for block in blocks:
        rows = jnp.concatenate([block, block[7:8] * jnp.sqrt(block[6:7])], axis=0)
        parts = split_parts(rows, EXACT)
        parts.append(jnp.zeros((32 - 9 * EXACT, LANES), F32))
        columns.append(jnp.transpose(jnp.concatenate(parts, axis=0)).astype(BF16))
    lines = lax.broadcasted_iota(jnp.int32, (32, LANES), 0)
    picks = []
    for i in range(9):
        pick = lines == i
        for n in range(1, EXACT):
            pick = jnp.logical_or(pick, lines == i + 9 * n)
        picks.append(jnp.where(pick, 1.0, 0.0).astype(BF16))
    return jnp.dot(
        jnp.concatenate(columns, axis=0), jnp.concatenate(picks, axis=1), preferred_element_type=F32
    )


def pair_sum(left, spread, start, react):
    rows = [left[i : i + 1] for i in range(8)]
    rows.append((2.0 * damp_tangent) * rows[7] * jnp.sqrt(rows[6]))
    wide = [jnp.broadcast_to(row, (SUBLANES, LANES)) for row in rows]
    lanes = lax.broadcasted_iota(jnp.int32, (SUBLANES, LANES), 1)
    total = [None] * 3
    for tile in range(LANES // SUBLANES):
        place = pl.ds(pl.multiple_of(start + tile * SUBLANES, SUBLANES), SUBLANES)
        there = [spread[place, i * LANES : (i + 1) * LANES] for i in range(9)]
        ex, ey, ez, wx, wy, wz = [wide[i] - there[i] for i in range(6)]
        square = (ex * ex + ey * ey) + (ez * ez + soft_core)
        inverse = lax.rsqrt(square)
        reach = wide[6] + there[6]
        delta = jnp.maximum(reach - square * inverse, 0.0)
        mass = wide[7] + there[7]
        under = jnp.maximum((delta * reach) * (mass * mass), 1e-30)
        tangent = (wide[8] * there[8]) * (delta * lax.rsqrt(under))
        speed = ((wx * ex + wy * ey) + wz * ez) * inverse
        along = (
            (2.0 / 3.0 / damp_tangent) * delta - ((damp_normal - damp_tangent) / damp_tangent) * speed
        ) * (tangent * inverse)
        column = None
        for d, (e, w) in enumerate(((ex, wx), (ey, wy), (ez, wz))):
            force = along * e - tangent * w
            total[d] = force if total[d] is None else total[d] + force
            if react is not None:
                across_sum = jnp.broadcast_to(jnp.sum(force, axis=1, keepdims=True), (SUBLANES, LANES))
                column = across_sum if column is None else jnp.where(lanes == d, across_sum, column)
        if react is not None:
            react[tile * SUBLANES : (tile + 1) * SUBLANES, :] = column
    total = [jnp.sum(item, axis=0, keepdims=True) for item in total]
    if react is None:
        return total, None
    turned = jnp.transpose(react[...])
    return total, [-turned[d : d + 1] for d in range(3)]


def blob_layout(across, blocks, pairs):
    bodies = 3 * across
    cells = bodies + 8 * blocks
    shares = cells + blocks
    lists = shares + blocks
    rows = lists + 2 * pairs
    return bodies, cells, shares, lists, rows + -rows % 8


def parities():
    return [lax.rem(lax.axis_index(axis), 2) == 0 for axis in AXES]


def pack_kernel(counts, list_hbm, pair_hbm, part_hbm, cell_hbm, share_hbm, fluid_hbm, *refs):
    n_out = 2 + sum(counts)
    list_ref, fluid_ref = refs[:2]
    height_outs, across_outs, along_outs = by_axis(refs[2:n_out], counts)
    pair_ref, part_ref, cell_ref, share_ref, sems = refs[n_out:]
    depth, across, along = fluid_ref.shape[1:]
    blocks, pairs = part_ref.shape[0], pair_ref.shape[0]
    bodies, cells, shares, lists, rows = blob_layout(across, blocks, pairs)
    small = [(part_hbm, part_ref), (cell_hbm, cell_ref), (share_hbm, share_ref), (pair_hbm, pair_ref), (list_hbm, list_ref)]
    small = [pltpu.make_async_copy(source, target, sems.at[3 + n]) for n, (source, target) in enumerate(small)]
    copies = [pltpu.make_async_copy(fluid_hbm.at[c], fluid_ref.at[c], sems.at[c]) for c in range(3)]
    for copy in small + copies:
        copy.start()
    even = parities()
    for copy in small + copies:
        copy.wait()
    for out in height_outs:
        for b in range(blocks):
            out[bodies + 8 * b : bodies + 8 * b + 8, :] = part_ref[b]
        out[cells:shares, :] = cell_ref[...].astype(F32)
        out[shares:lists, :] = share_ref[...]
        for k in range(pairs):
            for side in range(2):
                row = lists + 2 * k + side
                out[row : row + 1, :] = jnp.full((1, LANES), pair_ref[k, side], jnp.int32).astype(F32)
        used = lists + 2 * pairs
        if used < rows:
            out[used:rows, :] = jnp.zeros((rows - used, LANES), F32)
    lanes = lax.broadcasted_iota(jnp.int32, (across, along), 1)
    first = jnp.zeros((across, along), F32)
    last = jnp.zeros((across, along), F32)
    for c in range(3):
        for n, out in enumerate(height_outs):
            upward = even[0] if n == 0 else jnp.logical_not(even[0])
            out[c * across : (c + 1) * across, :] = fluid_ref[c, jnp.where(upward, depth - 1, 0)]
        for h in range(depth):
            k = c * depth + h
            here = fluid_ref[c, h]
            for n, out in enumerate(across_outs):
                upward = even[1] if n == 0 else jnp.logical_not(even[1])
                out[k : k + 1, :] = jnp.where(upward, here[across - 1 : across], here[0:1])
            turned = pltpu.roll(here, 2 * k, 1) if k else here
            first = jnp.where(lanes == 2 * k, turned, first)
            last = jnp.where(lanes == (2 * k - 1) % along, turned, last)
    first = pltpu.roll(first, along - 1, 1)
    last = pltpu.roll(last, 1, 1)
    for n, out in enumerate(along_outs):
        upward = even[2] if n == 0 else jnp.logical_not(even[2])
        out[...] = jnp.where(upward, last, first)


def mark_cells(picks, spots, b, over, spot, half, wide):
    along = picks.shape[0] // PARTS
    sites = lax.broadcasted_iota(jnp.int32, (spots.shape[0], LANES), 0)
    one_hot = lane_one_hot(sites[:along], spot)
    for n in range(PARTS):
        picks[n * along : (n + 1) * along, b * LANES : (b + 1) * LANES] = one_hot
    one_hot = lane_one_hot(sites, jnp.where(over >= half, along, 0) + spot)
    for n in range(PARTS):
        spots[:, n * wide + b * LANES : n * wide + (b + 1) * LANES] = one_hot


def lane_one_hot(sites, target):
    return jnp.where(sites == target, 1.0, 0.0).astype(BF16)


def place_lines(ones, part, half):
    line = jnp.broadcast_to(part, (16, LANES)).astype(BF16)
    line = jnp.concatenate([line] * (half // 16), axis=0)
    return jnp.where(ones > 0, line, jnp.zeros_like(line))


def rim_kernel_part(blocks, pairs, half, fold, sent, height_ins, next_ref, scratch):
    spread, pieces, picks, seen_ref, coupled, spots = scratch
    depth, across, along = next_ref.shape[1:]
    wide = blocks * LANES
    bodies, cells, shares, lists, _ = blob_layout(across, blocks, pairs)
    even = parities()
    rows = lax.broadcasted_iota(jnp.int32, (across, LANES), 0)
    halves = lax.broadcasted_iota(jnp.int32, (half, LANES), 0)
    coupling = [[jnp.zeros((1, LANES), F32)] * blocks for _ in range(3)]
    meetings, partners = [], []
    for n, blob in enumerate(height_ins):
        own = sent[n]
        above = even[0] if n == 0 else jnp.logical_not(even[0])
        for k in range(pairs):
            ours = [own[lists + 2 * k + side : lists + 2 * k + side + 1, :] for side in range(2)]
            theirs = [blob[lists + 2 * k + side : lists + 2 * k + side + 1, :] for side in range(2)]
            to = jnp.where(above, ours[0], theirs[1])
            by = jnp.where(above, ours[1], theirs[0])
            left = own[bodies : bodies + 8, :]
            right = blob[bodies : bodies + 8, :]
            for b in range(1, blocks):
                body = slice(bodies + 8 * b, bodies + 8 * b + 8)
                left = jnp.where(to == b, own[body, :], left)
                right = jnp.where(by == b, blob[body, :], right)
            meetings.append((to, left))
            partners.append(right)
    spread[...] = spread_blocks(partners)
    for i, (to, left) in enumerate(meetings):
        force, _ = pair_sum(left, spread, i * LANES, None)
        for b in range(blocks):
            for c in range(3):
                coupling[c][b] += jnp.where(to == b, force[c], 0.0)
    for n, blob in enumerate(height_ins):
        own = sent[n]
        above = even[0] if n == 0 else jnp.logical_not(even[0])
        own_layer = jnp.where(above, depth - 1, 0)
        below = jnp.logical_not(above)
        for k in range(3):
            face = slice(k * across, (k + 1) * across)
            pieces[face, :] = parts_of(blob[face, :])
            pieces[(3 + k) * across : (4 + k) * across, :] = parts_of(own[face, :])
        lined = []
        for b in range(blocks):
            cell = jnp.where(above, own[cells + b : cells + b + 1, :], blob[cells + b : cells + b + 1, :])
            height, over, spot = places(cell.astype(jnp.int32), across, along)
            lined.append((height, over))
            mark_cells(picks, spots, b, over, spot, half, wide)
        seen_ref[...] = jnp.dot(pieces[...], picks[...], preferred_element_type=F32)
        for b in range(blocks):
            height, over = lined[b]
            share = jnp.where(above, own[shares + b : shares + b + 1, :], blob[shares + b : shares + b + 1, :])
            body = slice(bodies + 8 * b, bodies + 8 * b + 8)
            owner = jnp.where(above, own[body, :], blob[body, :])
            top = height == depth - 1
            mask = rows == over
            column = slice(b * LANES, (b + 1) * LANES)
            seen_share = jnp.where(top, jnp.where(above, share, 1.0 - share), 0.0)
            home_share = jnp.where(jnp.logical_and(top, below), share, 0.0)
            given_share = (-source_gain) * jnp.where(above, 1.0 - share, share)
            own_share = jnp.where(jnp.logical_and(top, below), 1.0, 0.0)
            ones = lane_one_hot(halves, jnp.where(over >= half, over - half, over))
            for c in range(3):
                seen = seen_ref[c * across : (c + 1) * across, column]
                home = seen_ref[(3 + c) * across : (4 + c) * across, column]
                met = jnp.where(mask, seen_share * seen + home_share * home, 0.0)
                met = jnp.sum(met, axis=0, keepdims=True)
                drag = drag_coef * owner[6:7] * (met - own_share * owner[3 + c : 4 + c])
                coupling[c][b] += jnp.where(above, drag, 0.0)
                for m, part in enumerate(split_parts(given_share * drag)):
                    coupled[c * half : (c + 1) * half, m * wide + b * LANES : m * wide + (b + 1) * LANES] = (
                        place_lines(ones, part, half)
                    )
        source = lax.dot_general(
            coupled[...], spots[...], (((1,), (1,)), ((), ())), preferred_element_type=F32
        )
        for c in range(3):
            given = [source[c * half : (c + 1) * half, f * along : (f + 1) * along] for f in range(fold)]
            next_ref[c, own_layer] += diffuse * blob[c * across : (c + 1) * across, :] + jnp.concatenate(given, axis=0)
    return coupling


def local_kernel(blocks, pairs, pair_ref, fluid_ref, *refs):
    count = (len(refs) - 18) // 2
    sent, height_ins = refs[:count], refs[count : 2 * count]
    force_ref, next_ref, source_ref = refs[2 * count : 2 * count + 3]
    spread, pieces, picks, spots, react, seen_ref, found, weights, coupled = refs[2 * count + 3 : 2 * count + 12]
    rim_refs = refs[2 * count + 12 :]
    blob_ref = sent[0]
    depth, across, along = fluid_ref.shape[1:]
    listed = pair_ref.shape[1]
    fold = spots.shape[0] // along
    half = across // fold
    wide = blocks * LANES
    bodies, cells, shares, _, _ = blob_layout(across, blocks, pairs)
    rows = lax.broadcasted_iota(jnp.int32, (across, LANES), 0)
    halves = lax.broadcasted_iota(jnp.int32, (half, LANES), 0)
    subs = lax.broadcasted_iota(jnp.int32, (SUBLANES, along), 0)
    slabs = [(c, h) for c in range(3) for h in range(depth)]

    def body_of(b):
        return blob_ref[bodies + 8 * b : bodies + 8 * b + 8, :]

    def spot_of(b):
        return places(blob_ref[cells + b : cells + b + 1, :].astype(jnp.int32), across, along)

    def stencil(c, h):
        for t in range(across // SUBLANES):
            at = t * SUBLANES
            here = fluid_ref[c, h, at : at + SUBLANES, :]
            if t > 0:
                beside = fluid_ref[c, h, at - 1 : at + SUBLANES - 1, :]
            else:
                beside = jnp.where(subs == 0, 0.0, pltpu.roll(here, 1, 0))
            if at + SUBLANES < across:
                beside += fluid_ref[c, h, at + 1 : at + SUBLANES + 1, :]
            else:
                beside += jnp.where(subs == SUBLANES - 1, 0.0, pltpu.roll(here, SUBLANES - 1, 0))
            line = (c * depth + h) * across + at
            beside += seen_ref[line : line + SUBLANES, wide : wide + along]
            if h > 0:
                beside += fluid_ref[c, h - 1, at : at + SUBLANES, :]
            if h < depth - 1:
                beside += fluid_ref[c, h + 1, at : at + SUBLANES, :]
            next_ref[c, h, at : at + SUBLANES, :] = (1.0 - 6.0 * diffuse) * here + diffuse * beside

    spread[...] = spread_blocks([body_of(b) for b in range(blocks)])
    for k, (c, h) in enumerate(slabs):
        pieces[k * across : (k + 1) * across, :] = parts_of(fluid_ref[c, h])
    for b in range(blocks):
        _, over, spot = spot_of(b)
        mark_cells(picks, spots, b, over, spot, half, wide)
    here = lax.broadcasted_iota(jnp.int32, (along, along), 0)
    there = lax.broadcasted_iota(jnp.int32, (along, along), 1)
    near = jnp.where(jnp.abs(here - there) == 1, 1.0, 0.0).astype(BF16)
    for n in range(PARTS):
        picks[n * along : (n + 1) * along, wide : wide + along] = near
    seen_ref[...] = jnp.dot(pieces[...], picks[...], preferred_element_type=F32)

    turns = blocks + listed
    share_out = [slabs[i * len(slabs) // turns : (i + 1) * len(slabs) // turns] for i in range(turns)]
    for b in range(blocks):
        for c, h in share_out[b]:
            stencil(c, h)
        force, _ = pair_sum(body_of(b), spread, b * LANES, None)
        for c in range(3):
            force_ref[c, b : b + 1, :] = force[c]

    for b in range(blocks):
        height, over, _ = spot_of(b)
        share = blob_ref[shares + b : shares + b + 1, :]
        mask = rows == over
        column = slice(b * LANES, (b + 1) * LANES)
        near = [
            jnp.where(height == h, 1.0 - share, jnp.where(height == h - 1, share, 0.0)) for h in range(depth)
        ]
        for c in range(3):
            total = jnp.zeros((SUBLANES, LANES), F32)
            for h in range(depth):
                k = c * depth + h
                seen = jnp.where(mask, seen_ref[k * across : (k + 1) * across, column], 0.0)
                total += near[h] * jnp.sum(seen.reshape(across // SUBLANES, SUBLANES, LANES), axis=0)
            met = jnp.sum(total, axis=0, keepdims=True)
            drag = drag_coef * blob_ref[bodies + 8 * b + 6 : bodies + 8 * b + 7, :] * (
                met - blob_ref[bodies + 8 * b + 3 + c : bodies + 8 * b + 4 + c, :]
            )
            force_ref[c, b : b + 1, :] += drag
            for h in range(depth):
                weights[c * depth + h : c * depth + h + 1, column] = (-source_gain) * near[h] * drag
        ones = lane_one_hot(halves, jnp.where(over >= half, over - half, over))
        for n, part in enumerate(split_parts(weights[:, column])):
            for k in range(3 * depth):
                coupled[k * half : (k + 1) * half, n * wide + b * LANES : n * wide + (b + 1) * LANES] = place_lines(
                    ones, part[k : k + 1], half
                )
    for c in range(3):
        face = slice(c * depth * half, (c + 1) * depth * half)
        source_ref[face, :] = lax.dot_general(
            coupled[face, :], spots[...], (((1,), (1,)), ((), ())), preferred_element_type=F32
        )

    for i in range(listed):
        for c, h in share_out[blocks + i]:
            stencil(c, h)
        a, c = pair_ref[0, i], pair_ref[1, i]
        left = blob_ref[pl.ds(pl.multiple_of(bodies + 8 * a, 8), 8), :]
        ahead, behind = pair_sum(left, spread, c * LANES, react.at[i])
        for side, forces in enumerate((ahead, behind)):
            for d in range(3):
                found[2 * i + side, d : d + 1, :] = forces[d]
    coupling = rim_kernel_part(blocks, pairs, half, fold, sent, height_ins, next_ref, rim_refs)
    for b in range(blocks):
        for d in range(3):
            total = force_ref[d, b : b + 1, :]
            for i in range(listed):
                for side in range(2):
                    total += jnp.where(pair_ref[side, i] == b, found[2 * i + side, d : d + 1, :], 0.0)
            force_ref[d, b : b + 1, :] = total + coupling[d][b]


def finish_kernel(counts, sizes, force_ref, partial_ref, source_ref, *refs):
    n_in = sum(counts[1:])
    across_ins, along_ins = by_axis(refs[:n_in], counts[1:])
    force_hbm, next_hbm, next_ref, sems = refs[n_in:]
    copies = [pltpu.make_async_copy(force_ref, force_hbm, sems.at[3])]
    copies[0].start()
    depth, across, along = partial_ref.shape[1:]
    fold = source_ref.shape[1] // along
    half = across // fold
    even = parities()

    def second_of(arrived, axis):
        second = arrived[1][...]
        if sizes[axis] % 2:
            return second
        place = lax.axis_index(AXES[axis])
        inside = jnp.logical_and(place > 0, place < sizes[axis] - 1)
        return jnp.where(inside, second, 0.0)

    def ordered(arrived, axis):
        first = arrived[0][...]
        if len(arrived) == 1:
            return jnp.where(even[axis], 0.0, first), jnp.where(even[axis], first, 0.0)
        second = second_of(arrived, axis)
        return jnp.where(even[axis], second, first), jnp.where(even[axis], first, second)

    across_low, across_high = ordered(across_ins, 1)
    across_low = diffuse * across_low
    across_high = diffuse * across_high
    edges = along_ins[0][...]
    if len(along_ins) > 1:
        edges = edges + second_of(along_ins, 2)
    edges = diffuse * edges
    lanes = lax.broadcasted_iota(jnp.int32, (across, along), 1)
    subs = lax.broadcasted_iota(jnp.int32, (SUBLANES, along), 0)
    tail = across - SUBLANES
    rim = jnp.logical_or(lanes == 0, lanes == along - 1)
    for c in range(3):
        for h in range(depth):
            k = c * depth + h
            given = [
                source_ref[k * half : (k + 1) * half, f * along : (f + 1) * along] for f in range(fold)
            ]
            value = partial_ref[c, h] + jnp.concatenate(given, axis=0)
            value += jnp.where(rim, pltpu.roll(edges, (along - 2 * k) % along, 1) if k else edges, 0.0)
            next_ref[c, h] = value
            next_ref[c, h, :SUBLANES, :] += jnp.where(subs == 0, across_low[k : k + 1, :], 0.0)
            next_ref[c, h, tail:, :] += jnp.where(subs == SUBLANES - 1, across_high[k : k + 1, :], 0.0)
        copies.append(pltpu.make_async_copy(next_ref.at[c], next_hbm.at[c], sems.at[c]))
        copies[-1].start()
    for copy in copies:
        copy.wait()


def by_axis(refs, counts):
    groups, at = [], 0
    for n in counts:
        groups.append(refs[at : at + n])
        at += n
    return groups


def exchange(payloads, axis, closed):
    count = lax.axis_size(axis)
    results = []
    for n, payload in enumerate(payloads):
        route = []
        for i in range(n, count - 1, 2):
            route += [(i, i + 1), (i + 1, i)]
        if closed and n == 1 and count % 2 == 0:
            route += [(0, count - 1), (count - 1, 0)]
        results.append(lax.ppermute(payload, axis, route))
    return results


def body(particles, local_pairs, cross_pairs, drag_cell, drag_share, fluid):
    blocks = particles.shape[0]
    pairs = cross_pairs.shape[0]
    listed = local_pairs.shape[0]
    _, depth, across, along = fluid.shape
    counts = [min(2, lax.axis_size(axis) - 1) for axis in AXES]
    fold = 2 if across % 32 == 0 else 1
    half = across // fold
    wide = PARTS * blocks * LANES
    rows = blob_layout(across, blocks, pairs)[-1]
    shapes = [(rows, along), (3 * depth, along), (across, along)]
    vmem = pl.BlockSpec(memory_space=pltpu.VMEM)
    hbm = pl.BlockSpec(memory_space=pltpu.HBM)
    smem = pl.BlockSpec(memory_space=pltpu.SMEM)

    def kept(value):
        return pltpu.with_memory_space_constraint(value, pltpu.VMEM)

    listing, fluid_kept, *packed = pl.pallas_call(
        functools.partial(pack_kernel, counts),
        out_shape=[
            pltpu.SMEM((2, listed), jnp.int32),
            pltpu.VMEM(fluid.shape, F32),
        ]
        + [pltpu.VMEM(shape, F32) for shape, n in zip(shapes, counts) for _ in range(n)],
        in_specs=[hbm] * 6,
        out_specs=[smem] + [vmem] * (1 + sum(counts)),
        scratch_shapes=[
            pltpu.SMEM(cross_pairs.shape, jnp.int32),
            pltpu.VMEM(particles.shape, F32),
            pltpu.VMEM(drag_cell.shape, jnp.int32),
            pltpu.VMEM(drag_share.shape, F32),
            pltpu.SemaphoreType.DMA((8,)),
        ],
        compiler_params=pltpu.CompilerParams(vmem_limit_bytes=GRANT),
        name="pack",
    )(
        *[
            pltpu.with_memory_space_constraint(value, pltpu.HBM)
            for value in (local_pairs.T, cross_pairs, particles, drag_cell, drag_share, fluid)
        ]
    )
    received = []
    for axis, payloads in zip(AXES, by_axis(packed, counts)):
        received += exchange(payloads, axis, axis != AXES[0])

    height_count = counts[0]
    force, partial, source = pl.pallas_call(
        functools.partial(local_kernel, blocks, pairs),
        out_shape=[
            pltpu.VMEM((3, blocks, LANES), F32),
            pltpu.VMEM(fluid.shape, F32),
            pltpu.VMEM((3 * depth * half, fold * along), F32),
        ],
        in_specs=[smem] + [vmem] * (1 + 2 * height_count),
        out_specs=[vmem] * 3,
        scratch_shapes=[
            pltpu.VMEM((blocks * LANES, 9 * LANES), F32),
            pltpu.VMEM((3 * depth * across, PARTS * along), BF16),
            pltpu.VMEM((PARTS * along, blocks * LANES + along), BF16),
            pltpu.VMEM((fold * along, wide), BF16),
            pltpu.VMEM((listed, LANES, LANES), F32),
            pltpu.VMEM((3 * depth * across, blocks * LANES + along), F32),
            pltpu.VMEM((2 * listed, SUBLANES, LANES), F32),
            pltpu.VMEM((3 * depth, blocks * LANES), F32),
            pltpu.VMEM((3 * depth * half, wide), BF16),
            pltpu.VMEM((height_count * pairs * LANES, 9 * LANES), F32),
            pltpu.VMEM((6 * across, PARTS * along), BF16),
            pltpu.VMEM((PARTS * along, blocks * LANES), BF16),
            pltpu.VMEM((6 * across, blocks * LANES), F32),
            pltpu.VMEM((3 * half, wide), BF16),
            pltpu.VMEM((fold * along, wide), BF16),
        ],
        compiler_params=pltpu.CompilerParams(vmem_limit_bytes=GRANT),
        name="local",
    )(
        pltpu.with_memory_space_constraint(listing, pltpu.SMEM),
        *[kept(value) for value in (fluid_kept, *packed[:height_count], *received[:height_count])],
    )

    rest = received[height_count:]
    out_force, out_next = pl.pallas_call(
        functools.partial(finish_kernel, counts, [lax.axis_size(axis) for axis in AXES]),
        out_shape=[
            jax.ShapeDtypeStruct((3, blocks, LANES), F32),
            jax.ShapeDtypeStruct(fluid.shape, F32),
        ],
        in_specs=[vmem] * (3 + len(rest)),
        out_specs=[hbm, hbm],
        scratch_shapes=[pltpu.VMEM(fluid.shape, F32), pltpu.SemaphoreType.DMA((4,))],
        compiler_params=pltpu.CompilerParams(vmem_limit_bytes=GRANT),
        name="finish",
    )(*[kept(value) for value in [force, partial, source, *rest]])
    return jnp.transpose(out_force, (1, 0, 2)), out_next


def solution(mesh):
    in_specs = (
        P(("gx", "gy", "gz"), None, None),
        P(("gx", "gy", "gz"), None),
        P(("gx", "gy", "gz"), None),
        P(("gx", "gy", "gz"), None),
        P(("gx", "gy", "gz"), None),
        P(None, "gx", "gy", "gz"),
    )
    out_specs = (P(("gx", "gy", "gz"), None, None), P(None, "gx", "gy", "gz"))
    return jax.shard_map(body, mesh=mesh, in_specs=in_specs, out_specs=out_specs, check_vma=False)
```

```python
import functools

import jax
import jax.numpy as jnp
from jax import lax
from jax.experimental import pallas as pl
from jax.experimental.pallas import tpu as pltpu
from jax.sharding import PartitionSpec as P


soft_core = 0.01
damp_normal = 0.3
damp_tangent = 0.2
drag_coef = 1.5
diffuse = 0.1
source_gain = 0.5

F32 = jnp.float32
BF16 = jnp.bfloat16
PARTS = 2
EXACT = 3
LANES = 128
SUBLANES = 8
GRANT = 32 * 1024 * 1024
AXES = ("gx", "gy", "gz")


def split_parts(value, count=PARTS):
    parts = []
    for _ in range(count):
        part = value.astype(BF16).astype(F32)
        parts.append(part)
        value = value - part
    return parts


def places(cell, across, along):
    layer = across * along
    if layer & (layer - 1) or along & (along - 1):
        return cell // layer, cell // along % across, cell % along
    shift = along.bit_length() - 1
    high = layer.bit_length() - 1
    return (
        lax.shift_right_logical(cell, high),
        lax.shift_right_logical(cell, shift) & (across - 1),
        cell & (along - 1),
    )


def parts_of(value):
    return jnp.concatenate([part.astype(BF16) for part in split_parts(value)], axis=1)


def spread_blocks(blocks):
    columns = []
    for block in blocks:
        rows = jnp.concatenate([block, block[7:8] * jnp.sqrt(block[6:7])], axis=0)
        parts = split_parts(rows, EXACT)
        parts.append(jnp.zeros((32 - 9 * EXACT, LANES), F32))
        columns.append(jnp.transpose(jnp.concatenate(parts, axis=0)).astype(BF16))
    lines = lax.broadcasted_iota(jnp.int32, (32, LANES), 0)
    picks = []
    for i in range(9):
        pick = lines == i
        for n in range(1, EXACT):
            pick = jnp.logical_or(pick, lines == i + 9 * n)
        picks.append(jnp.where(pick, 1.0, 0.0).astype(BF16))
    return jnp.dot(
        jnp.concatenate(columns, axis=0), jnp.concatenate(picks, axis=1), preferred_element_type=F32
    )


def pair_sum(left, spread, start, react):
    rows = [left[i : i + 1] for i in range(8)]
    rows.append((2.0 * damp_tangent) * rows[7] * jnp.sqrt(rows[6]))
    wide = [jnp.broadcast_to(row, (SUBLANES, LANES)) for row in rows]
    lanes = lax.broadcasted_iota(jnp.int32, (SUBLANES, LANES), 1)
    total = [None] * 3
    for tile in range(LANES // SUBLANES):
        place = pl.ds(pl.multiple_of(start + tile * SUBLANES, SUBLANES), SUBLANES)
        there = [spread[place, i * LANES : (i + 1) * LANES] for i in range(9)]
        ex, ey, ez, wx, wy, wz = [wide[i] - there[i] for i in range(6)]
        square = (ex * ex + ey * ey) + (ez * ez + soft_core)
        inverse = lax.rsqrt(square)
        reach = wide[6] + there[6]
        delta = jnp.maximum(reach - square * inverse, 0.0)
        mass = wide[7] + there[7]
        under = jnp.maximum((delta * reach) * (mass * mass), 1e-30)
        tangent = (wide[8] * there[8]) * (delta * lax.rsqrt(under))
        speed = ((wx * ex + wy * ey) + wz * ez) * inverse
        along = (
            (2.0 / 3.0 / damp_tangent) * delta - ((damp_normal - damp_tangent) / damp_tangent) * speed
        ) * (tangent * inverse)
        column = None
        for d, (e, w) in enumerate(((ex, wx), (ey, wy), (ez, wz))):
            force = along * e - tangent * w
            total[d] = force if total[d] is None else total[d] + force
            if react is not None:
                across_sum = jnp.broadcast_to(jnp.sum(force, axis=1, keepdims=True), (SUBLANES, LANES))
                column = across_sum if column is None else jnp.where(lanes == d, across_sum, column)
        if react is not None:
            react[tile * SUBLANES : (tile + 1) * SUBLANES, :] = column
    total = [jnp.sum(item, axis=0, keepdims=True) for item in total]
    if react is None:
        return total, None
    turned = jnp.transpose(react[...])
    return total, [-turned[d : d + 1] for d in range(3)]


def blob_layout(across, blocks, pairs):
    bodies = 3 * across
    cells = bodies + 8 * blocks
    shares = cells + blocks
    lists = shares + blocks
    rows = lists + 2 * pairs
    return bodies, cells, shares, lists, rows + -rows % 8


def parities():
    return [lax.rem(lax.axis_index(axis), 2) == 0 for axis in AXES]


def pack_kernel(counts, list_hbm, pair_hbm, part_hbm, cell_hbm, share_hbm, fluid_hbm, *refs):
    n_out = 2 + sum(counts)
    list_ref, fluid_ref = refs[:2]
    height_outs, across_outs, along_outs = by_axis(refs[2:n_out], counts)
    pair_ref, part_ref, cell_ref, share_ref, sems = refs[n_out:]
    depth, across, along = fluid_ref.shape[1:]
    blocks, pairs = part_ref.shape[0], pair_ref.shape[0]
    bodies, cells, shares, lists, rows = blob_layout(across, blocks, pairs)
    small = [(part_hbm, part_ref), (cell_hbm, cell_ref), (share_hbm, share_ref), (pair_hbm, pair_ref), (list_hbm, list_ref)]
    small = [pltpu.make_async_copy(source, target, sems.at[3 + n]) for n, (source, target) in enumerate(small)]
    copies = [pltpu.make_async_copy(fluid_hbm.at[c], fluid_ref.at[c], sems.at[c]) for c in range(3)]
    for copy in small + copies:
        copy.start()
    even = parities()
    for copy in small + copies:
        copy.wait()
    for out in height_outs:
        for b in range(blocks):
            out[bodies + 8 * b : bodies + 8 * b + 8, :] = part_ref[b]
        out[cells:shares, :] = cell_ref[...].astype(F32)
        out[shares:lists, :] = share_ref[...]
        for k in range(pairs):
            for side in range(2):
                row = lists + 2 * k + side
                out[row : row + 1, :] = jnp.full((1, LANES), pair_ref[k, side], jnp.int32).astype(F32)
        used = lists + 2 * pairs
        if used < rows:
            out[used:rows, :] = jnp.zeros((rows - used, LANES), F32)
    lanes = lax.broadcasted_iota(jnp.int32, (across, along), 1)
    first = jnp.zeros((across, along), F32)
    last = jnp.zeros((across, along), F32)
    for c in range(3):
        for n, out in enumerate(height_outs):
            upward = even[0] if n == 0 else jnp.logical_not(even[0])
            out[c * across : (c + 1) * across, :] = fluid_ref[c, jnp.where(upward, depth - 1, 0)]
        for h in range(depth):
            k = c * depth + h
            here = fluid_ref[c, h]
            for n, out in enumerate(across_outs):
                upward = even[1] if n == 0 else jnp.logical_not(even[1])
                out[k : k + 1, :] = jnp.where(upward, here[across - 1 : across], here[0:1])
            turned = pltpu.roll(here, 2 * k, 1) if k else here
            first = jnp.where(lanes == 2 * k, turned, first)
            last = jnp.where(lanes == (2 * k - 1) % along, turned, last)
    first = pltpu.roll(first, along - 1, 1)
    last = pltpu.roll(last, 1, 1)
    for n, out in enumerate(along_outs):
        upward = even[2] if n == 0 else jnp.logical_not(even[2])
        out[...] = jnp.where(upward, last, first)


def mark_cells(picks, spots, b, over, spot, half, wide):
    along = picks.shape[0] // PARTS
    sites = lax.broadcasted_iota(jnp.int32, (spots.shape[0], LANES), 0)
    one_hot = lane_one_hot(sites[:along], spot)
    for n in range(PARTS):
        picks[n * along : (n + 1) * along, b * LANES : (b + 1) * LANES] = one_hot
    one_hot = lane_one_hot(sites, jnp.where(over >= half, along, 0) + spot)
    for n in range(PARTS):
        spots[:, n * wide + b * LANES : n * wide + (b + 1) * LANES] = one_hot


def lane_one_hot(sites, target):
    return jnp.where(sites == target, 1.0, 0.0).astype(BF16)


def place_lines(ones, part, half):
    line = jnp.broadcast_to(part, (16, LANES)).astype(BF16)
    line = jnp.concatenate([line] * (half // 16), axis=0)
    return jnp.where(ones > 0, line, jnp.zeros_like(line))


def rim_kernel_part(blocks, pairs, half, fold, sent, height_ins, next_ref, scratch):
    spread, pieces, picks, seen_ref, coupled, spots = scratch
    depth, across, along = next_ref.shape[1:]
    wide = blocks * LANES
    bodies, cells, shares, lists, _ = blob_layout(across, blocks, pairs)
    even = parities()
    rows = lax.broadcasted_iota(jnp.int32, (across, LANES), 0)
    halves = lax.broadcasted_iota(jnp.int32, (half, LANES), 0)
    coupling = [[jnp.zeros((1, LANES), F32)] * blocks for _ in range(3)]
    meetings, partners = [], []
    for n, blob in enumerate(height_ins):
        own = sent[n]
        above = even[0] if n == 0 else jnp.logical_not(even[0])
        for k in range(pairs):
            ours = [own[lists + 2 * k + side : lists + 2 * k + side + 1, :] for side in range(2)]
            theirs = [blob[lists + 2 * k + side : lists + 2 * k + side + 1, :] for side in range(2)]
            to = jnp.where(above, ours[0], theirs[1])
            by = jnp.where(above, ours[1], theirs[0])
            left = own[bodies : bodies + 8, :]
            right = blob[bodies : bodies + 8, :]
            for b in range(1, blocks):
                body = slice(bodies + 8 * b, bodies + 8 * b + 8)
                left = jnp.where(to == b, own[body, :], left)
                right = jnp.where(by == b, blob[body, :], right)
            meetings.append((to, left))
            partners.append(right)
    spread[...] = spread_blocks(partners)
    for i, (to, left) in enumerate(meetings):
        force, _ = pair_sum(left, spread, i * LANES, None)
        for b in range(blocks):
            for c in range(3):
                coupling[c][b] += jnp.where(to == b, force[c], 0.0)
    for n, blob in enumerate(height_ins):
        own = sent[n]
        above = even[0] if n == 0 else jnp.logical_not(even[0])
        own_layer = jnp.where(above, depth - 1, 0)
        below = jnp.logical_not(above)
        for k in range(3):
            face = slice(k * across, (k + 1) * across)
            pieces[face, :] = parts_of(blob[face, :])
            pieces[(3 + k) * across : (4 + k) * across, :] = parts_of(own[face, :])
        lined = []
        for b in range(blocks):
            cell = jnp.where(above, own[cells + b : cells + b + 1, :], blob[cells + b : cells + b + 1, :])
            height, over, spot = places(cell.astype(jnp.int32), across, along)
            lined.append((height, over))
            mark_cells(picks, spots, b, over, spot, half, wide)
        seen_ref[...] = jnp.dot(pieces[...], picks[...], preferred_element_type=F32)
        for b in range(blocks):
            height, over = lined[b]
            share = jnp.where(above, own[shares + b : shares + b + 1, :], blob[shares + b : shares + b + 1, :])
            body = slice(bodies + 8 * b, bodies + 8 * b + 8)
            owner = jnp.where(above, own[body, :], blob[body, :])
            top = height == depth - 1
            mask = rows == over
            column = slice(b * LANES, (b + 1) * LANES)
            seen_share = jnp.where(top, jnp.where(above, share, 1.0 - share), 0.0)
            home_share = jnp.where(jnp.logical_and(top, below), share, 0.0)
            given_share = (-source_gain) * jnp.where(above, 1.0 - share, share)
            own_share = jnp.where(jnp.logical_and(top, below), 1.0, 0.0)
            ones = lane_one_hot(halves, jnp.where(over >= half, over - half, over))
            for c in range(3):
                seen = seen_ref[c * across : (c + 1) * across, column]
                home = seen_ref[(3 + c) * across : (4 + c) * across, column]
                met = jnp.where(mask, seen_share * seen + home_share * home, 0.0)
                met = jnp.sum(met, axis=0, keepdims=True)
                drag = drag_coef * owner[6:7] * (met - own_share * owner[3 + c : 4 + c])
                coupling[c][b] += jnp.where(above, drag, 0.0)
                for m, part in enumerate(split_parts(given_share * drag)):
                    coupled[c * half : (c + 1) * half, m * wide + b * LANES : m * wide + (b + 1) * LANES] = (
                        place_lines(ones, part, half)
                    )
        source = lax.dot_general(
            coupled[...], spots[...], (((1,), (1,)), ((), ())), preferred_element_type=F32
        )
        for c in range(3):
            given = [source[c * half : (c + 1) * half, f * along : (f + 1) * along] for f in range(fold)]
            next_ref[c, own_layer] += diffuse * blob[c * across : (c + 1) * across, :] + jnp.concatenate(given, axis=0)
    return coupling


def local_kernel(blocks, pairs, pair_ref, fluid_ref, *refs):
    count = (len(refs) - 18) // 2
    sent, height_ins = refs[:count], refs[count : 2 * count]
    force_ref, next_ref, source_ref = refs[2 * count : 2 * count + 3]
    spread, pieces, picks, spots, react, seen_ref, found, weights, coupled = refs[2 * count + 3 : 2 * count + 12]
    rim_refs = refs[2 * count + 12 :]
    blob_ref = sent[0]
    depth, across, along = fluid_ref.shape[1:]
    listed = pair_ref.shape[1]
    fold = spots.shape[0] // along
    half = across // fold
    wide = blocks * LANES
    bodies, cells, shares, _, _ = blob_layout(across, blocks, pairs)
    rows = lax.broadcasted_iota(jnp.int32, (across, LANES), 0)
    halves = lax.broadcasted_iota(jnp.int32, (half, LANES), 0)
    subs = lax.broadcasted_iota(jnp.int32, (SUBLANES, along), 0)
    slabs = [(c, h) for c in range(3) for h in range(depth)]

    def body_of(b):
        return blob_ref[bodies + 8 * b : bodies + 8 * b + 8, :]

    def spot_of(b):
        return places(blob_ref[cells + b : cells + b + 1, :].astype(jnp.int32), across, along)

    def stencil(c, h):
        for t in range(across // SUBLANES):
            at = t * SUBLANES
            here = fluid_ref[c, h, at : at + SUBLANES, :]
            if t > 0:
                beside = fluid_ref[c, h, at - 1 : at + SUBLANES - 1, :]
            else:
                beside = jnp.where(subs == 0, 0.0, pltpu.roll(here, 1, 0))
            if at + SUBLANES < across:
                beside += fluid_ref[c, h, at + 1 : at + SUBLANES + 1, :]
            else:
                beside += jnp.where(subs == SUBLANES - 1, 0.0, pltpu.roll(here, SUBLANES - 1, 0))
            line = (c * depth + h) * across + at
            beside += seen_ref[line : line + SUBLANES, wide : wide + along]
            if h > 0:
                beside += fluid_ref[c, h - 1, at : at + SUBLANES, :]
            if h < depth - 1:
                beside += fluid_ref[c, h + 1, at : at + SUBLANES, :]
            next_ref[c, h, at : at + SUBLANES, :] = (1.0 - 6.0 * diffuse) * here + diffuse * beside

    spread[...] = spread_blocks([body_of(b) for b in range(blocks)])
    for k, (c, h) in enumerate(slabs):
        pieces[k * across : (k + 1) * across, :] = parts_of(fluid_ref[c, h])
    for b in range(blocks):
        _, over, spot = spot_of(b)
        mark_cells(picks, spots, b, over, spot, half, wide)
    here = lax.broadcasted_iota(jnp.int32, (along, along), 0)
    there = lax.broadcasted_iota(jnp.int32, (along, along), 1)
    near = jnp.where(jnp.abs(here - there) == 1, 1.0, 0.0).astype(BF16)
    for n in range(PARTS):
        picks[n * along : (n + 1) * along, wide : wide + along] = near
    seen_ref[...] = jnp.dot(pieces[...], picks[...], preferred_element_type=F32)

    turns = blocks + listed
    share_out = [slabs[i * len(slabs) // turns : (i + 1) * len(slabs) // turns] for i in range(turns)]
    for b in range(blocks):
        for c, h in share_out[b]:
            stencil(c, h)
        force, _ = pair_sum(body_of(b), spread, b * LANES, None)
        for c in range(3):
            force_ref[c, b : b + 1, :] = force[c]

    for b in range(blocks):
        height, over, _ = spot_of(b)
        share = blob_ref[shares + b : shares + b + 1, :]
        mask = rows == over
        column = slice(b * LANES, (b + 1) * LANES)
        near = [
            jnp.where(height == h, 1.0 - share, jnp.where(height == h - 1, share, 0.0)) for h in range(depth)
        ]
        for c in range(3):
            total = jnp.zeros((SUBLANES, LANES), F32)
            for h in range(depth):
                k = c * depth + h
                seen = jnp.where(mask, seen_ref[k * across : (k + 1) * across, column], 0.0)
                total += near[h] * jnp.sum(seen.reshape(across // SUBLANES, SUBLANES, LANES), axis=0)
            met = jnp.sum(total, axis=0, keepdims=True)
            drag = drag_coef * blob_ref[bodies + 8 * b + 6 : bodies + 8 * b + 7, :] * (
                met - blob_ref[bodies + 8 * b + 3 + c : bodies + 8 * b + 4 + c, :]
            )
            force_ref[c, b : b + 1, :] += drag
            for h in range(depth):
                weights[c * depth + h : c * depth + h + 1, column] = (-source_gain) * near[h] * drag
        ones = lane_one_hot(halves, jnp.where(over >= half, over - half, over))
        for n, part in enumerate(split_parts(weights[:, column])):
            for k in range(3 * depth):
                coupled[k * half : (k + 1) * half, n * wide + b * LANES : n * wide + (b + 1) * LANES] = place_lines(
                    ones, part[k : k + 1], half
                )
    for c in range(3):
        face = slice(c * depth * half, (c + 1) * depth * half)
        source_ref[face, :] = lax.dot_general(
            coupled[face, :], spots[...], (((1,), (1,)), ((), ())), preferred_element_type=F32
        )

    for i in range(listed):
        for c, h in share_out[blocks + i]:
            stencil(c, h)
        a, c = pair_ref[0, i], pair_ref[1, i]
        left = blob_ref[pl.ds(pl.multiple_of(bodies + 8 * a, 8), 8), :]
        ahead, behind = pair_sum(left, spread, c * LANES, react.at[i])
        for side, forces in enumerate((ahead, behind)):
            for d in range(3):
                found[2 * i + side, d : d + 1, :] = forces[d]
    coupling = rim_kernel_part(blocks, pairs, half, fold, sent, height_ins, next_ref, rim_refs)
    for b in range(blocks):
        for d in range(3):
            total = force_ref[d, b : b + 1, :]
            for i in range(listed):
                for side in range(2):
                    total += jnp.where(pair_ref[side, i] == b, found[2 * i + side, d : d + 1, :], 0.0)
            force_ref[d, b : b + 1, :] = total + coupling[d][b]


def finish_kernel(counts, sizes, force_ref, partial_ref, source_ref, *refs):
    n_in = sum(counts[1:])
    across_ins, along_ins = by_axis(refs[:n_in], counts[1:])
    force_hbm, next_hbm, next_ref, sems = refs[n_in:]
    copies = [pltpu.make_async_copy(force_ref, force_hbm, sems.at[0])]
    copies[0].start()
    depth, across, along = partial_ref.shape[1:]
    ends = sorted({(depth + 1) // 2, depth})
    fold = source_ref.shape[1] // along
    half = across // fold
    even = parities()

    def second_of(arrived, axis):
        second = arrived[1][...]
        if sizes[axis] % 2:
            return second
        place = lax.axis_index(AXES[axis])
        inside = jnp.logical_and(place > 0, place < sizes[axis] - 1)
        return jnp.where(inside, second, 0.0)

    def ordered(arrived, axis):
        first = arrived[0][...]
        if len(arrived) == 1:
            return jnp.where(even[axis], 0.0, first), jnp.where(even[axis], first, 0.0)
        second = second_of(arrived, axis)
        return jnp.where(even[axis], second, first), jnp.where(even[axis], first, second)

    across_low, across_high = ordered(across_ins, 1)
    across_low = diffuse * across_low
    across_high = diffuse * across_high
    edges = along_ins[0][...]
    if len(along_ins) > 1:
        edges = edges + second_of(along_ins, 2)
    edges = diffuse * edges
    lanes = lax.broadcasted_iota(jnp.int32, (across, along), 1)
    subs = lax.broadcasted_iota(jnp.int32, (SUBLANES, along), 0)
    tail = across - SUBLANES
    rim = jnp.logical_or(lanes == 0, lanes == along - 1)
    for c in range(3):
        for h in range(depth):
            k = c * depth + h
            given = [
                source_ref[k * half : (k + 1) * half, f * along : (f + 1) * along] for f in range(fold)
            ]
            value = partial_ref[c, h] + jnp.concatenate(given, axis=0)
            value += jnp.where(rim, pltpu.roll(edges, (along - 2 * k) % along, 1) if k else edges, 0.0)
            next_ref[c, h] = value
            next_ref[c, h, :SUBLANES, :] += jnp.where(subs == 0, across_low[k : k + 1, :], 0.0)
            next_ref[c, h, tail:, :] += jnp.where(subs == SUBLANES - 1, across_high[k : k + 1, :], 0.0)
            if h + 1 in ends:
                n = ends.index(h + 1)
                done = pl.ds(ends[n - 1] if n else 0, ends[n] - (ends[n - 1] if n else 0))
                copies.append(
                    pltpu.make_async_copy(next_ref.at[c, done], next_hbm.at[c, done], sems.at[1 + 2 * c + n])
                )
                copies[-1].start()
    for copy in copies:
        copy.wait()


def by_axis(refs, counts):
    groups, at = [], 0
    for n in counts:
        groups.append(refs[at : at + n])
        at += n
    return groups


def exchange(payloads, axis, closed):
    count = lax.axis_size(axis)
    results = []
    for n, payload in enumerate(payloads):
        route = []
        for i in range(n, count - 1, 2):
            route += [(i, i + 1), (i + 1, i)]
        if closed and n == 1 and count % 2 == 0:
            route += [(0, count - 1), (count - 1, 0)]
        results.append(lax.ppermute(payload, axis, route))
    return results


def body(particles, local_pairs, cross_pairs, drag_cell, drag_share, fluid):
    blocks = particles.shape[0]
    pairs = cross_pairs.shape[0]
    listed = local_pairs.shape[0]
    _, depth, across, along = fluid.shape
    counts = [min(2, lax.axis_size(axis) - 1) for axis in AXES]
    fold = 2 if across % 32 == 0 else 1
    half = across // fold
    wide = PARTS * blocks * LANES
    rows = blob_layout(across, blocks, pairs)[-1]
    shapes = [(rows, along), (3 * depth, along), (across, along)]
    vmem = pl.BlockSpec(memory_space=pltpu.VMEM)
    hbm = pl.BlockSpec(memory_space=pltpu.HBM)
    smem = pl.BlockSpec(memory_space=pltpu.SMEM)

    def kept(value):
        return pltpu.with_memory_space_constraint(value, pltpu.VMEM)

    listing, fluid_kept, *packed = pl.pallas_call(
        functools.partial(pack_kernel, counts),
        out_shape=[
            pltpu.SMEM((2, listed), jnp.int32),
            pltpu.VMEM(fluid.shape, F32),
        ]
        + [pltpu.VMEM(shape, F32) for shape, n in zip(shapes, counts) for _ in range(n)],
        in_specs=[hbm] * 6,
        out_specs=[smem] + [vmem] * (1 + sum(counts)),
        scratch_shapes=[
            pltpu.SMEM(cross_pairs.shape, jnp.int32),
            pltpu.VMEM(particles.shape, F32),
            pltpu.VMEM(drag_cell.shape, jnp.int32),
            pltpu.VMEM(drag_share.shape, F32),
            pltpu.SemaphoreType.DMA((8,)),
        ],
        compiler_params=pltpu.CompilerParams(vmem_limit_bytes=GRANT),
        name="pack",
    )(
        *[
            pltpu.with_memory_space_constraint(value, pltpu.HBM)
            for value in (local_pairs.T, cross_pairs, particles, drag_cell, drag_share, fluid)
        ]
    )
    received = []
    for axis, payloads in zip(AXES, by_axis(packed, counts)):
        received += exchange(payloads, axis, axis != AXES[0])

    height_count = counts[0]
    force, partial, source = pl.pallas_call(
        functools.partial(local_kernel, blocks, pairs),
        out_shape=[
            pltpu.VMEM((3, blocks, LANES), F32),
            pltpu.VMEM(fluid.shape, F32),
            pltpu.VMEM((3 * depth * half, fold * along), F32),
        ],
        in_specs=[smem] + [vmem] * (1 + 2 * height_count),
        out_specs=[vmem] * 3,
        scratch_shapes=[
            pltpu.VMEM((blocks * LANES, 9 * LANES), F32),
            pltpu.VMEM((3 * depth * across, PARTS * along), BF16),
            pltpu.VMEM((PARTS * along, blocks * LANES + along), BF16),
            pltpu.VMEM((fold * along, wide), BF16),
            pltpu.VMEM((listed, LANES, LANES), F32),
            pltpu.VMEM((3 * depth * across, blocks * LANES + along), F32),
            pltpu.VMEM((2 * listed, SUBLANES, LANES), F32),
            pltpu.VMEM((3 * depth, blocks * LANES), F32),
            pltpu.VMEM((3 * depth * half, wide), BF16),
            pltpu.VMEM((height_count * pairs * LANES, 9 * LANES), F32),
            pltpu.VMEM((6 * across, PARTS * along), BF16),
            pltpu.VMEM((PARTS * along, blocks * LANES), BF16),
            pltpu.VMEM((6 * across, blocks * LANES), F32),
            pltpu.VMEM((3 * half, wide), BF16),
            pltpu.VMEM((fold * along, wide), BF16),
        ],
        compiler_params=pltpu.CompilerParams(vmem_limit_bytes=GRANT),
        name="local",
    )(
        pltpu.with_memory_space_constraint(listing, pltpu.SMEM),
        *[kept(value) for value in (fluid_kept, *packed[:height_count], *received[:height_count])],
    )

    rest = received[height_count:]
    out_force, out_next = pl.pallas_call(
        functools.partial(finish_kernel, counts, [lax.axis_size(axis) for axis in AXES]),
        out_shape=[
            jax.ShapeDtypeStruct((3, blocks, LANES), F32),
            jax.ShapeDtypeStruct(fluid.shape, F32),
        ],
        in_specs=[vmem] * (3 + len(rest)),
        out_specs=[hbm, hbm],
        scratch_shapes=[pltpu.VMEM(fluid.shape, F32), pltpu.SemaphoreType.DMA((7,))],
        compiler_params=pltpu.CompilerParams(vmem_limit_bytes=GRANT),
        name="finish",
    )(*[kept(value) for value in [force, partial, source, *rest]])
    return jnp.transpose(out_force, (1, 0, 2)), out_next


def solution(mesh):
    in_specs = (
        P(("gx", "gy", "gz"), None, None),
        P(("gx", "gy", "gz"), None),
        P(("gx", "gy", "gz"), None),
        P(("gx", "gy", "gz"), None),
        P(("gx", "gy", "gz"), None),
        P(None, "gx", "gy", "gz"),
    )
    out_specs = (P(("gx", "gy", "gz"), None, None), P(None, "gx", "gy", "gz"))
    return jax.shard_map(body, mesh=mesh, in_specs=in_specs, out_specs=out_specs, check_vma=False)
```
